32 devices in a mesh: dp: 32 (over z, y, x, core).
Axes of the slice: x: 2, y: 2, z: 4, core: 2. Of those that a mesh axis runs over, the one named last changes fastest.
Arguments:
- images: bfloat16 [256, 50, 768], P('dp'), may hold values from -6 to 6
- captions: bfloat16 [128, 77, 512], P('dp'), may hold values from -6 to 6
- caption_ends: int32 [128, 2], P('dp'), may hold values from 4 to 76, as said below
- image_norm_gain: bfloat16 [768], P('dp'), may hold values from 0.5 to 1.5
- image_norm_bias: bfloat16 [768], P('dp'), may hold values from -1.75 to 1.75
- image_attend_weight: bfloat16 [768, 2304], P('dp'), may hold values from -0.21875 to 0.21875
- image_attend_bias: bfloat16 [1536], P('dp'), may hold values from -1.75 to 1.75
- image_output_weight: bfloat16 [768, 768], P('dp'), may hold values from -1.25 to 1.25
- image_output_bias: bfloat16 [768], P('dp'), may hold values from -1.75 to 1.75
- image_second_gain: bfloat16 [768], P('dp'), may hold values from 0.5 to 1.5
- image_second_bias: bfloat16 [768], P('dp'), may hold values from -1.75 to 1.75
- image_expand_weight: bfloat16 [768, 3072], P('dp'), may hold values from -0.21875 to 0.21875
- image_expand_bias: bfloat16 [3072], P('dp'), may hold values from -1.75 to 1.75
- image_reduce_weight: bfloat16 [3072, 768], P('dp'), may hold values from -0.15625 to 0.15625
- image_reduce_bias: bfloat16 [768], P('dp'), may hold values from -1.75 to 1.75
- image_final_gain: bfloat16 [768], P('dp'), may hold values from 0.5 to 1.5
- image_final_bias: bfloat16 [768], P('dp'), may hold values from -1.75 to 1.75
- image_projection: bfloat16 [768, 512], P('dp'), may hold values from -0.21875 to 0.21875
- caption_norm_gain: bfloat16 [512], P('dp'), may hold values from 0.5 to 1.5
- caption_norm_bias: bfloat16 [512], P('dp'), may hold values from -1.75 to 1.75
- caption_attend_weight: bfloat16 [512, 1536], P('dp'), may hold values from -0.25 to 0.25
- caption_attend_bias: bfloat16 [1024], P('dp'), may hold values from -1.75 to 1.75
- caption_output_weight: bfloat16 [512, 512], P('dp'), may hold values from -0.75 to 0.75
- caption_output_bias: bfloat16 [512], P('dp'), may hold values from -1.75 to 1.75
- caption_second_gain: bfloat16 [512], P('dp'), may hold values from 0.5 to 1.5
- caption_second_bias: bfloat16 [512], P('dp'), may hold values from -1.75 to 1.75
- caption_expand_weight: bfloat16 [512, 2048], P('dp'), may hold values from -0.25 to 0.25
- caption_expand_bias: bfloat16 [2048], P('dp'), may hold values from -1.75 to 1.75
- caption_reduce_weight: bfloat16 [2048, 512], P('dp'), may hold values from -0.1875 to 0.1875
- caption_reduce_bias: bfloat16 [512], P('dp'), may hold values from -1.75 to 1.75
- caption_final_gain: bfloat16 [512], P('dp'), may hold values from 0.5 to 1.5
- caption_final_bias: bfloat16 [512], P('dp'), may hold values from -1.75 to 1.75
- caption_projection: bfloat16 [512, 512], P('dp'), may hold values from -0.25 to 0.25
- logit_scale: float32 [1], replicated, may hold values from 3.4 to 3.9
Outputs:
- contrastive_loss: float32 [1], replicated
- branch_rms: float32 [6], replicated
- images_gradient: bfloat16 [256, 50, 768], P('dp')
- captions_gradient: bfloat16 [128, 77, 512], P('dp')
- image_norm_gain_gradient: float32 [768], P('dp')
- image_norm_bias_gradient: float32 [768], P('dp')
- image_attend_weight_gradient: float32 [768, 2304], P('dp')
- image_attend_bias_gradient: float32 [1536], P('dp')
- image_output_weight_gradient: float32 [768, 768], P('dp')
- image_output_bias_gradient: float32 [768], P('dp')
- image_second_gain_gradient: float32 [768], P('dp')
- image_second_bias_gradient: float32 [768], P('dp')
- image_expand_weight_gradient: float32 [768, 3072], P('dp')
- image_expand_bias_gradient: float32 [3072], P('dp')
- image_reduce_weight_gradient: float32 [3072, 768], P('dp')
- image_reduce_bias_gradient: float32 [768], P('dp')
- image_final_gain_gradient: float32 [768], P('dp')
- image_final_bias_gradient: float32 [768], P('dp')
- image_projection_gradient: float32 [768, 512], P('dp')
- caption_norm_gain_gradient: float32 [512], P('dp')
- caption_norm_bias_gradient: float32 [512], P('dp')
- caption_attend_weight_gradient: float32 [512, 1536], P('dp')
- caption_attend_bias_gradient: float32 [1024], P('dp')
- caption_output_weight_gradient: float32 [512, 512], P('dp')
- caption_output_bias_gradient: float32 [512], P('dp')
- caption_second_gain_gradient: float32 [512], P('dp')
- caption_second_bias_gradient: float32 [512], P('dp')
- caption_expand_weight_gradient: float32 [512, 2048], P('dp')
- caption_expand_bias_gradient: float32 [2048], P('dp')
- caption_reduce_weight_gradient: float32 [2048, 512], P('dp')
- caption_reduce_bias_gradient: float32 [512], P('dp')
- caption_final_gain_gradient: float32 [512], P('dp')
- caption_final_bias_gradient: float32 [512], P('dp')
- caption_projection_gradient: float32 [512, 512], P('dp')
- logit_scale_gradient: float32 [1], replicated
The draws below stay inside these ranges and needn't reach their ends.
Inputs may be any that keep to these rules, and one draw needn't show every extreme that they name: `caption_ends`: in each row the first caption spans tokens 0 to the first end, the second from the first end to the second end; each caption has 4 to 38 tokens; tokens from the second end on are padding.
All inputs are finite; a program needn't handle non-finite values.
Results may differ from the reference program's by a relative error of at most 0.025.
The reference program's roundings to bfloat16 on the way count: a program that leaves them out, or rounds other values in their place, can miss the bound.
Values may be sent and summed in bfloat16 or wider, within the bound.
A program may use at most 256 MiB of HBM per device.

```python
import math
import jax
import jax.numpy as jnp
from jax import lax

DI = 768
HD = 64
FI = 3072
DT = 512
FT = 2048
EMB = 512
PATCH = 50
TL = 77
IMAGES = 256
ROWS = 128


def draw_caption_ends(key, part):
    first = jax.random.randint(jax.random.fold_in(key, 11), (ROWS,), 4, TL // 2 + 1)
    second = jax.random.randint(jax.random.fold_in(key, 12), (ROWS,), 4, TL // 2 + 1)
    places = jnp.arange(ROWS)
    first = jnp.where(places == 0, TL // 2, jnp.where(places == 1, 4, first))
    second = jnp.where(places == 0, TL // 2, second)
    return jnp.stack([first, first + second], 1).astype(jnp.int32)


def strengthened(values, stream_key, source, target, parts, factor):
    owner, partner = [(jnp.arange(values.shape[position]) // (values.shape[position] // parts)).reshape([-1 if axis == position else 1 for axis in range(values.ndim)]) for position in (source, target)]
    chosen = jax.random.permutation(stream_key, parts)[partner]
    strong = (owner == chosen) | (owner == (partner + parts // 2) % parts)
    return jnp.where(strong, factor * values, values)


def steps_of(rng, dims, shards, low, largest):
    level = 1.0
    for position, blocks in shards:
        heights = jax.random.uniform(jax.random.fold_in(jax.random.fold_in(rng, 6), position), (blocks,), jnp.float32, low / len(shards), largest / len(shards))
        level = level * jnp.repeat(jnp.exp(heights), dims[position] // blocks).reshape((-1,) + (1,) * (len(dims) - 1 - position))
    return level


def bell_draw(own_key, dims, scale, most, split=(), held_as=jnp.bfloat16):
    values = jax.random.normal(own_key, dims, jnp.float32) * scale
    if len(split) > 0:
        values = steps_of(own_key, dims, split, -0.22, 0.18) * values
    return jnp.clip(values, min=-most, max=most).astype(held_as)


def bell_draw_with(stream_key, shape, deviation, reach, split, heavy, kind=jnp.bfloat16):
    entries = deviation * jax.random.normal(stream_key, shape, jnp.float32)
    if split:
        entries = entries * steps_of(stream_key, shape, split, -0.22, 0.18)
    return jnp.clip(strengthened(entries, jax.random.fold_in(stream_key, 3), *heavy), -reach, reach).astype(kind)


def setup_inputs(seed: int = 0) -> dict:
    seeds = jax.random.split(jax.random.key(seed), 35)
    images = bell_draw_with(seeds[0], (IMAGES, PATCH, DI), 1.0, 6.0, ((0, 32),), (0, 2, 32, 2.75))
    captions = bell_draw_with(seeds[1], (ROWS, TL, DT), 1.0, 6.0, ((0, 32),), (0, 2, 32, 2.75))
    caption_ends = draw_caption_ends(jax.random.fold_in(seeds[34], 71), 0)
    image_norm_gain = jnp.clip(1.0 + 0.1 * jax.random.normal(seeds[3], (DI,), jnp.float32), 0.5, 1.5).astype(jnp.bfloat16)
    image_norm_bias = bell_draw(seeds[4], (DI,), 0.3, 1.75, ((0, 32),))
    image_attend_weight = bell_draw(seeds[5], (DI, 3 * DI), DI ** -0.5, 0.21875, ((0, 32),))
    image_attend_bias = bell_draw(seeds[6], (2 * DI,), 0.3, 1.75, ((0, 32),))
    image_output_weight = bell_draw(seeds[7], (DI, DI), (DI // 32) ** -0.5, 1.25, ((0, 32),))
    image_output_bias = bell_draw(seeds[8], (DI,), 0.3, 1.75, ((0, 32),))
    image_second_gain = jnp.clip(1.0 + 0.1 * jax.random.normal(seeds[9], (DI,), jnp.float32), 0.5, 1.5).astype(jnp.bfloat16)
    image_second_bias = bell_draw(seeds[10], (DI,), 0.3, 1.75, ((0, 32),))
    image_expand_weight = bell_draw(seeds[11], (DI, FI), DI ** -0.5, 0.21875, ((0, 32),))
    image_expand_bias = bell_draw(seeds[12], (FI,), 0.3, 1.75, ((0, 32),))
    image_reduce_weight = bell_draw(seeds[13], (FI, DI), (FI // 2) ** -0.5, 0.15625, ((0, 32),))
    image_reduce_bias = bell_draw(seeds[14], (DI,), 0.3, 1.75, ((0, 32),))
    image_final_gain = jnp.clip(1.0 + 0.1 * jax.random.normal(seeds[15], (DI,), jnp.float32), 0.5, 1.5).astype(jnp.bfloat16)
    image_final_bias = bell_draw(seeds[16], (DI,), 0.3, 1.75, ((0, 32),))
    image_projection = bell_draw(seeds[17], (DI, EMB), DI ** -0.5, 0.21875, ((0, 32),))
    caption_norm_gain = jnp.clip(1.0 + 0.1 * jax.random.normal(seeds[18], (DT,), jnp.float32), 0.5, 1.5).astype(jnp.bfloat16)
    caption_norm_bias = bell_draw(seeds[19], (DT,), 0.3, 1.75, ((0, 32),))
    caption_attend_weight = bell_draw(seeds[20], (DT, 3 * DT), DT ** -0.5, 0.25, ((0, 32),))
    caption_attend_bias = bell_draw(seeds[21], (2 * DT,), 0.3, 1.75, ((0, 32),))
    caption_output_weight = bell_draw(seeds[22], (DT, DT), (DT // 8) ** -0.5, 0.75, ((0, 32),))
    caption_output_bias = bell_draw(seeds[23], (DT,), 0.3, 1.75, ((0, 32),))
    caption_second_gain = jnp.clip(1.0 + 0.1 * jax.random.normal(seeds[24], (DT,), jnp.float32), 0.5, 1.5).astype(jnp.bfloat16)
    caption_second_bias = bell_draw(seeds[25], (DT,), 0.3, 1.75, ((0, 32),))
    caption_expand_weight = bell_draw(seeds[26], (DT, FT), DT ** -0.5, 0.25, ((0, 32),))
    caption_expand_bias = bell_draw(seeds[27], (FT,), 0.3, 1.75, ((0, 32),))
    caption_reduce_weight = bell_draw(seeds[28], (FT, DT), (FT // 2) ** -0.5, 0.1875, ((0, 32),))
    caption_reduce_bias = bell_draw(seeds[29], (DT,), 0.3, 1.75, ((0, 32),))
    caption_final_gain = jnp.clip(1.0 + 0.1 * jax.random.normal(seeds[30], (DT,), jnp.float32), 0.5, 1.5).astype(jnp.bfloat16)
    caption_final_bias = bell_draw(seeds[31], (DT,), 0.3, 1.75, ((0, 32),))
    caption_projection = bell_draw(seeds[32], (DT, EMB), DT ** -0.5, 0.25, ((0, 32),))
    logit_scale = jnp.clip(jax.random.uniform(seeds[33], (1,), jnp.float32, 3.4, 3.9), 3.4, 3.9)
    return dict(images=images, captions=captions, caption_ends=caption_ends, image_norm_gain=image_norm_gain, image_norm_bias=image_norm_bias, image_attend_weight=image_attend_weight, image_attend_bias=image_attend_bias, image_output_weight=image_output_weight, image_output_bias=image_output_bias, image_second_gain=image_second_gain, image_second_bias=image_second_bias, image_expand_weight=image_expand_weight, image_expand_bias=image_expand_bias, image_reduce_weight=image_reduce_weight, image_reduce_bias=image_reduce_bias, image_final_gain=image_final_gain, image_final_bias=image_final_bias, image_projection=image_projection, caption_norm_gain=caption_norm_gain, caption_norm_bias=caption_norm_bias, caption_attend_weight=caption_attend_weight, caption_attend_bias=caption_attend_bias, caption_output_weight=caption_output_weight, caption_output_bias=caption_output_bias, caption_second_gain=caption_second_gain, caption_second_bias=caption_second_bias, caption_expand_weight=caption_expand_weight, caption_expand_bias=caption_expand_bias, caption_reduce_weight=caption_reduce_weight, caption_reduce_bias=caption_reduce_bias, caption_final_gain=caption_final_gain, caption_final_bias=caption_final_bias, caption_projection=caption_projection, logit_scale=logit_scale)


@jax.custom_vjp
def low(v):
    return lax.optimization_barrier(v.astype(jnp.bfloat16)).astype(jnp.float32)

@jax.custom_vjp
def low_back(v):
    return v

def low_keep(v):
    return (low(v), None)

def low_pass(kept, grad):
    return (grad,)

def back_keep(v):
    return (v, None)

def back_low(kept, grad):
    return (low(grad),)
low.defvjp(low_keep, low_pass)
low_back.defvjp(back_keep, back_low)
HIGHEST = lax.Precision.HIGHEST

def matmul(left, right):
    return jnp.dot(left, right, precision=HIGHEST)

def layer_norm(rows, gain, bias):
    centred = rows - lax.optimization_barrier(jnp.mean(rows, -1, keepdims=True))
    return centred * lax.rsqrt(lax.optimization_barrier(jnp.mean(centred * centred, -1, keepdims=True)) + 1e-05) * gain + bias

def caption_allowed(end_rows, length):
    places = jnp.arange(length, dtype=jnp.int32)
    pieces = (places[None, :] >= end_rows[:, 0:1]).astype(jnp.int32) + (places[None, :] >= end_rows[:, 1:2]).astype(jnp.int32)
    living = places[None, :] < end_rows[:, 1:2]
    same_piece = pieces[:, :, None] == pieces[:, None, :]
    causal = places[:, None] >= places[None, :]
    diagonal = places[:, None] == places[None, :]
    return same_piece & causal[None] & living[:, None, :] | diagonal[None]

def tower(inputs, allowed, weights):
    norm_gain, norm_bias, attend_weight, attend_bias, output_weight, output_bias, second_gain, second_bias, expand_weight, expand_bias, reduce_weight, reduce_bias = weights
    sequences, length, features = inputs.shape
    head_count = features // HD
    stream = inputs.reshape(sequences * length, features)
    normed = low(layer_norm(stream, norm_gain, norm_bias))
    bias_full = jnp.concatenate([attend_bias[:features], jnp.zeros_like(attend_bias[:features]), attend_bias[features:]])
    mixed = low(low_back(matmul(normed, attend_weight) + bias_full)).reshape(sequences, length, 3, head_count, HD)
    queries = mixed[:, :, 0]
    key_rows = mixed[:, :, 1]
    value_rows = mixed[:, :, 2]
    scores = low_back(jnp.einsum('sqhd,skhd->shqk', queries, key_rows, precision=HIGHEST) / 8.0)
    scores = jnp.where(allowed[:, None], scores, -1e+30)
    softened = jax.nn.softmax(scores, axis=-1)
    attended = jnp.einsum('shqk,skhd->sqhd', low(softened), value_rows, precision=HIGHEST)
    attended = low(low_back(attended)).reshape(sequences * length, features)
    branch = low_back(matmul(attended, output_weight) + output_bias)
    middle = stream + branch
    normed_two = low(layer_norm(middle, second_gain, second_bias))
    hidden = low_back(matmul(normed_two, expand_weight) + expand_bias)
    active = low(hidden * jax.nn.sigmoid(1.702 * hidden))
    second = low_back(matmul(active, reduce_weight) + reduce_bias)
    result = middle + second
    squares = jnp.stack([jnp.sum(branch * branch), jnp.sum(second * second), jnp.sum(result * result)])
    return (result.reshape(sequences, length, features), squares)

def embed(rows, gain, bias, projection):
    normed = low(layer_norm(rows, gain, bias))
    raw_embed = low_back(matmul(normed, projection))
    return low(raw_embed * lax.rsqrt(lax.optimization_barrier(jnp.sum(raw_embed * raw_embed, -1, keepdims=True)) + 1e-06))

def objective(image_input, caption_input, caption_ends, vision_params, caption_params, scale_param):
    image_group = math.gcd(IMAGES, 64)
    image_blocks = image_input.reshape(IMAGES // image_group, image_group, PATCH, DI)
    full_allowed = jnp.ones((image_group, PATCH, PATCH), dtype=bool)

    def image_step(carry, block):
        output, squares = tower(block, full_allowed, vision_params[:12])
        return (carry + squares, output[:, 0, :])
    image_squares, image_rows = lax.scan(jax.checkpoint(image_step), jnp.zeros((3,), image_input.dtype), image_blocks)
    row_group = math.gcd(ROWS, 32)
    caption_blocks = caption_input.reshape(ROWS // row_group, row_group, TL, DT)
    end_blocks = caption_ends.reshape(ROWS // row_group, row_group, 2)

    def caption_step(carry, pair):
        block, end_rows = pair
        output, squares = tower(block, caption_allowed(end_rows, TL), caption_params[:12])
        picked = jnp.take_along_axis(output, (end_rows - 1)[:, :, None], axis=1)
        return (carry + squares, picked.reshape(row_group * 2, DT))
    caption_squares, caption_rows = lax.scan(jax.checkpoint(caption_step), jnp.zeros((3,), caption_input.dtype), (caption_blocks, end_blocks))
    image_vectors = embed(image_rows.reshape(IMAGES, DI), vision_params[12], vision_params[13], vision_params[14])
    caption_vectors = embed(caption_rows.reshape(IMAGES, DT), caption_params[12], caption_params[13], caption_params[14])
    scale = jnp.exp(scale_param[0])
    row_logits = scale * low_back(matmul(image_vectors, caption_vectors.T))
    col_logits = scale * low_back(matmul(caption_vectors, image_vectors.T))
    total = jnp.sum(jax.nn.logsumexp(row_logits, axis=-1) - jnp.diagonal(row_logits))
    total = total + jnp.sum(jax.nn.logsumexp(col_logits, axis=-1) - jnp.diagonal(col_logits))
    loss_value = total / (2 * IMAGES)
    return (loss_value.reshape(1), jnp.concatenate([image_squares, caption_squares]))

def reference(images, captions, caption_ends, image_norm_gain, image_norm_bias, image_attend_weight, image_attend_bias, image_output_weight, image_output_bias, image_second_gain, image_second_bias, image_expand_weight, image_expand_bias, image_reduce_weight, image_reduce_bias, image_final_gain, image_final_bias, image_projection, caption_norm_gain, caption_norm_bias, caption_attend_weight, caption_attend_bias, caption_output_weight, caption_output_bias, caption_second_gain, caption_second_bias, caption_expand_weight, caption_expand_bias, caption_reduce_weight, caption_reduce_bias, caption_final_gain, caption_final_bias, caption_projection, logit_scale):
    vision_params = tuple((weight.astype(jnp.float32) for weight in (image_norm_gain, image_norm_bias, image_attend_weight, image_attend_bias, image_output_weight, image_output_bias, image_second_gain, image_second_bias, image_expand_weight, image_expand_bias, image_reduce_weight, image_reduce_bias, image_final_gain, image_final_bias, image_projection)))
    caption_params = tuple((weight.astype(jnp.float32) for weight in (caption_norm_gain, caption_norm_bias, caption_attend_weight, caption_attend_bias, caption_output_weight, caption_output_bias, caption_second_gain, caption_second_bias, caption_expand_weight, caption_expand_bias, caption_reduce_weight, caption_reduce_bias, caption_final_gain, caption_final_bias, caption_projection)))

    def wrapped(image_input, caption_input, vision_tuple, caption_tuple, scale_param):
        return objective(image_input, caption_input, caption_ends, vision_tuple, caption_tuple, scale_param)
    loss_value, backward, squares = jax.vjp(wrapped, images.astype(jnp.float32), captions.astype(jnp.float32), vision_params, caption_params, logit_scale.astype(jnp.float32), has_aux=True)
    image_grad, caption_grad, vision_grads, caption_grads, scale_grad = backward(jnp.ones_like(loss_value))
    image_count = IMAGES * PATCH * DI
    caption_count = ROWS * TL * DT
    counts = jnp.array([image_count, image_count, image_count, caption_count, caption_count, caption_count], dtype=squares.dtype)
    branch_rms = jnp.sqrt(squares / counts)
    return (loss_value, branch_rms, image_grad.astype(jnp.bfloat16), caption_grad.astype(jnp.bfloat16), vision_grads[0], vision_grads[1], vision_grads[2], vision_grads[3], vision_grads[4], vision_grads[5], vision_grads[6], vision_grads[7], vision_grads[8], vision_grads[9], vision_grads[10], vision_grads[11], vision_grads[12], vision_grads[13], vision_grads[14], caption_grads[0], caption_grads[1], caption_grads[2], caption_grads[3], caption_grads[4], caption_grads[5], caption_grads[6], caption_grads[7], caption_grads[8], caption_grads[9], caption_grads[10], caption_grads[11], caption_grads[12], caption_grads[13], caption_grads[14], scale_grad)
```

```python
import jax
import jax.numpy as jnp
from jax import lax
from jax.sharding import PartitionSpec as P

HD = 64
F32 = jnp.float32
BF16 = jnp.bfloat16


def product(left, right):
    return jnp.dot(left, right, preferred_element_type=F32)


def left_product(left, right):
    return lax.dot_general(left, right, (((0,), (0,)), ((), ())), preferred_element_type=F32)


def right_product(left, right):
    return lax.dot_general(left, right, (((1,), (1,)), ((), ())), preferred_element_type=F32)


def unit_norm(rows):
    centred = rows - jnp.mean(rows, -1, keepdims=True)
    inverse = lax.rsqrt(jnp.mean(centred * centred, -1, keepdims=True) + 1e-05)
    return centred * inverse, inverse


def norm_inward(upstream, unit_rows, inverse, gain):
    scaled = upstream * gain
    return inverse * (
        scaled
        - jnp.mean(scaled, -1, keepdims=True)
        - unit_rows * jnp.mean(scaled * unit_rows, -1, keepdims=True)
    )


def caption_allowed(end_rows, length):
    places = jnp.arange(length, dtype=jnp.int32)
    pieces = (places[None, :] >= end_rows[:, 0:1]).astype(jnp.int32) + (
        places[None, :] >= end_rows[:, 1:2]
    ).astype(jnp.int32)
    living = places[None, :] < end_rows[:, 1:2]
    same_piece = pieces[:, :, None] == pieces[:, None, :]
    causal = places[:, None] >= places[None, :]
    diagonal = places[:, None] == places[None, :]
    return same_piece & causal[None] & living[:, None, :] | diagonal[None]


def spread_heads(rows):
    count, width = rows.shape
    heads = width // HD
    head = jnp.arange(heads)[:, None, None]
    lane_head = jnp.arange(width)[None, None, :] // HD
    return jnp.where(head == lane_head, rows[None], jnp.zeros((), rows.dtype)).reshape(
        heads * count, width
    )


def fold_heads(rows, count):
    total, width = rows.shape
    heads = width // HD
    head = jnp.arange(heads)[:, None, None]
    lane_head = jnp.arange(width)[None, None, :] // HD
    return jnp.sum(jnp.where(head == lane_head, rows.reshape(heads, count, width), 0.0), 0)


def local_forward(inputs, allowed, mine, pick_rows, weights):
    sequences, length, width = inputs.shape
    heads = width // HD
    stream = inputs.reshape(sequences * length, width).astype(F32)
    unit_one, inverse_one = unit_norm(stream)
    normed = (unit_one * weights["norm_gain"] + weights["norm_bias"]).astype(BF16)
    bias = weights["attend_bias"]
    bias_full = jnp.concatenate([bias[:width], jnp.zeros((width,), F32), bias[width:]])
    mixed = (product(normed, weights["attend"]) + bias_full).astype(BF16)
    queries, keys, values = mixed[:, :width], mixed[:, width : 2 * width], mixed[:, 2 * width :]
    split = lambda rows: rows.reshape(sequences, length, heads, HD)
    scores = jnp.einsum("sqhd,skhd->shqk", split(queries), split(keys), preferred_element_type=F32)
    scores = scores / 8.0
    if allowed is not None:
        scores = jnp.where(allowed[:, None], scores, -1e30)
    softened = jax.nn.softmax(scores, axis=-1).astype(BF16)
    attended = jnp.einsum("shqk,skhd->sqhd", softened, split(values), preferred_element_type=F32)
    attended = attended.astype(BF16).reshape(sequences * length, width)
    branch = product(attended, weights["output"]) + weights["output_bias"]
    middle = stream + branch
    unit_two, _ = unit_norm(middle)
    normed_two = (unit_two * weights["second_gain"] + weights["second_bias"]).astype(BF16)
    hidden = product(normed_two, weights["expand"]) + weights["expand_bias"]
    active = (hidden * jax.nn.sigmoid(1.702 * hidden)).astype(BF16)
    second = product(active, weights["reduce"]) + weights["reduce_bias"]
    result = middle + second
    squares = jnp.stack([jnp.sum(branch * branch), jnp.sum(second * second), jnp.sum(result * result)])
    picked_queries = queries[pick_rows]
    picked_scores = right_product(keys, spread_heads(picked_queries)) / 8.0
    seen = jnp.tile(mine, (1, heads))
    picked_scores = jnp.where(seen, picked_scores, -1e30)
    soft = jax.nn.softmax(picked_scores, axis=0)
    return dict(
        squares=squares,
        unit_one=unit_one,
        inverse_one=inverse_one,
        normed=normed,
        keys=keys,
        values=values,
        soft=soft,
        value_factor=left_product(normed, soft.astype(BF16)).astype(BF16),
        middle_rows=middle[pick_rows],
        attended_rows=attended[pick_rows],
        normed_rows=normed[pick_rows],
        query_rows=picked_queries,
    )


def head_forward(middle, weights):
    unit_two, inverse_two = unit_norm(middle)
    normed_two = (unit_two * weights["second_gain"] + weights["second_bias"]).astype(BF16)
    hidden = product(normed_two, weights["expand"]) + weights["expand_bias"]
    active = (hidden * jax.nn.sigmoid(1.702 * hidden)).astype(BF16)
    result = middle + (product(active, weights["reduce"]) + weights["reduce_bias"])
    unit_final, inverse_final = unit_norm(result)
    head_normed = (unit_final * weights["final_gain"] + weights["final_bias"]).astype(BF16)
    raw_embed = product(head_normed, weights["projection"])
    scaling = lax.rsqrt(jnp.sum(raw_embed * raw_embed, -1, keepdims=True) + 1e-06)
    direction = raw_embed * scaling
    kept = (unit_two, inverse_two, normed_two, hidden, active, unit_final, inverse_final, head_normed)
    return direction.astype(BF16), direction, scaling, kept


def head_backward(upstream, direction, scaling, kept, weights):
    unit_two, inverse_two, normed_two, hidden, active, unit_final, inverse_final, head_normed = kept
    raw_low = (
        scaling * (upstream - direction * jnp.sum(upstream * direction, -1, keepdims=True))
    ).astype(BF16)
    head_grad = right_product(raw_low, weights["projection"])
    result_grad = norm_inward(head_grad, unit_final, inverse_final, weights["final_gain"])
    second_low = result_grad.astype(BF16)
    gate = jax.nn.sigmoid(1.702 * hidden)
    hidden_low = (
        right_product(second_low, weights["reduce"]) * (gate + 1.702 * hidden * gate * (1.0 - gate))
    ).astype(BF16)
    two_grad = right_product(hidden_low, weights["expand"])
    middle_grad = result_grad + norm_inward(two_grad, unit_two, inverse_two, weights["second_gain"])
    branch_low = middle_grad.astype(BF16)
    attended_grad = right_product(branch_low, weights["output"]).astype(BF16)
    sums = dict(
        final_gain=jnp.sum(head_grad * unit_final, 0),
        final_bias=jnp.sum(head_grad, 0),
        reduce_bias=jnp.sum(second_low.astype(F32), 0),
        expand_bias=jnp.sum(hidden_low.astype(F32), 0),
        second_gain=jnp.sum(two_grad * unit_two, 0),
        second_bias=jnp.sum(two_grad, 0),
        output_bias=jnp.sum(branch_low.astype(F32), 0),
    )
    factors = dict(
        projection=(head_normed, raw_low),
        reduce=(active, second_low),
        expand=(normed_two, hidden_low),
    )
    return middle_grad, branch_low, attended_grad, sums, factors


def local_backward(kept, mine, pick_rows, middle_grad_rows, attended_grad_rows, weights):
    width = weights["output"].shape[0]
    count = pick_rows.shape[0]
    heads = width // HD
    wide_grad = spread_heads(attended_grad_rows)
    soft = kept["soft"]
    soft_grad = right_product(kept["values"], wide_grad)
    score_low = (soft * (soft_grad - jnp.sum(soft_grad * soft, 0, keepdims=True))).astype(BF16)
    query_grad = (fold_heads(left_product(score_low, kept["keys"]), count) / 8.0).astype(BF16)
    key_factor = left_product(kept["normed"], score_low).astype(BF16)
    attend = weights["attend"]
    key_side = right_product(spread_heads(kept["query_rows"]), attend[:, width : 2 * width]) / 8.0
    value_side = right_product(wide_grad, attend[:, 2 * width :])
    query_side = right_product(query_grad, attend[:, :width])
    normed_grad = product(score_low, key_side.astype(BF16)) + product(
        soft.astype(BF16), value_side.astype(BF16)
    )
    normed_grad = normed_grad.at[pick_rows].add(query_side)
    inward = norm_inward(normed_grad, kept["unit_one"], kept["inverse_one"], weights["norm_gain"])
    input_grad = inward.at[pick_rows].add(middle_grad_rows)
    gain_grad = jnp.sum(normed_grad * kept["unit_one"], 0)
    bias_grad = jnp.sum(normed_grad, 0)
    return input_grad, query_grad, key_factor, gain_grad, bias_grad


def my_columns(rows, size, index):
    return lax.dynamic_slice_in_dim(rows, index * size, size, rows.ndim - 1)


NAMES = (
    "norm_gain",
    "norm_bias",
    "attend",
    "attend_bias",
    "output",
    "output_bias",
    "second_gain",
    "second_bias",
    "expand",
    "expand_bias",
    "reduce",
    "reduce_bias",
    "final_gain",
    "final_bias",
    "projection",
)
VECTORS = tuple(name for name in NAMES if name.endswith("bias") or name.endswith("gain"))


def gather(rows):
    return lax.all_gather(rows, "dp", axis=0, tiled=True)


def exchange(rows, devices):
    width, terms = rows.shape
    blocks = rows.reshape(devices, width // devices, terms)
    return lax.all_to_all(blocks, "dp", 0, 0)


def gather_weights(shards):
    devices = lax.axis_size("dp")
    whole = {}
    wide = ("attend", "output", "expand", "projection")
    block = gather(jnp.concatenate([shards[name] for name in wide], 1))
    start = 0
    for name in wide:
        size = shards[name].shape[1]
        whole[name] = block[:, start : start + size]
        start += size
    whole["reduce"] = gather(shards["reduce"])
    flat = jnp.concatenate([shards[name] for name in VECTORS])
    flat = gather(flat[None].astype(F32))
    start = 0
    for name in VECTORS:
        size = shards[name].shape[0]
        whole[name] = flat[:, start : start + size].reshape(devices * size)
        start += size
    return whole


def per_device(images, captions, caption_ends, *rest):
    image_shards = dict(zip(NAMES, rest[:15]))
    caption_shards = dict(zip(NAMES, rest[15:30]))
    logit_scale = rest[30]
    devices = lax.axis_size("dp")
    index = lax.axis_index("dp")
    image_weights = gather_weights(image_shards)
    caption_weights = gather_weights(caption_shards)
    image_count, patches, image_width = images.shape
    row_count, row_length, caption_width = captions.shape
    batch = devices * image_count

    image_tokens = jnp.arange(image_count * patches, dtype=jnp.int32)
    image_picks = jnp.arange(image_count, dtype=jnp.int32) * patches
    image_mine = image_tokens[:, None] // patches == jnp.arange(image_count)[None, :]
    image_kept = local_forward(images, None, image_mine, image_picks, image_weights)

    caption_tokens = jnp.arange(row_count * row_length, dtype=jnp.int32)[:, None]
    row_start = jnp.arange(row_count, dtype=jnp.int32)[:, None] * row_length
    caption_picks = (row_start + caption_ends - 1).reshape(row_count * 2)
    starts = row_start + jnp.concatenate([jnp.zeros((row_count, 1), jnp.int32), caption_ends[:, :1]], 1)
    caption_mine = (caption_tokens >= starts.reshape(1, -1)) & (caption_tokens <= caption_picks[None, :])
    allowed = caption_allowed(caption_ends, row_length)
    caption_kept = local_forward(captions, allowed, caption_mine, caption_picks, caption_weights)

    towers = (
        (image_kept, image_weights, image_mine, image_picks, image_count),
        (caption_kept, caption_weights, caption_mine, caption_picks, row_count * 2),
    )
    middle_all = gather(jnp.concatenate([image_kept["middle_rows"], caption_kept["middle_rows"]], 1))
    low_names = ("attended_rows", "normed_rows", "query_rows")
    low_all = gather(
        jnp.concatenate([kept[name] for kept in (image_kept, caption_kept) for name in low_names], 1)
    )
    widths = (image_width, caption_width)
    middles = (middle_all[:, :image_width], middle_all[:, image_width:])
    lows = []
    start = 0
    for width in widths:
        lows.append(tuple(low_all[:, start + j * width : start + (j + 1) * width] for j in range(3)))
        start += 3 * width

    image_vectors, image_direction, image_scaling, image_head = head_forward(middles[0], image_weights)
    caption_vectors, caption_direction, caption_scaling, caption_head = head_forward(
        middles[1], caption_weights
    )
    scale = jnp.exp(logit_scale[0])
    logits = scale * right_product(image_vectors, caption_vectors)
    places = jnp.arange(batch, dtype=jnp.int32)
    one_hot = (places[:, None] == places[None, :]).astype(F32)
    row_top = jnp.max(logits, 1, keepdims=True)
    row_lse = row_top + jnp.log(jnp.sum(jnp.exp(logits - row_top), 1, keepdims=True))
    col_top = jnp.max(logits, 0, keepdims=True)
    col_lse = col_top + jnp.log(jnp.sum(jnp.exp(logits - col_top), 0, keepdims=True))
    diagonal = jnp.sum(logits * one_hot)
    factor = 1.0 / (2.0 * batch)
    loss = (jnp.sum(row_lse) + jnp.sum(col_lse) - 2.0 * diagonal) * factor
    row_grad = (jnp.exp(logits - row_lse) - one_hot) * factor
    col_grad = (jnp.exp(logits - col_lse) - one_hot) * factor
    scale_grad = jnp.sum(row_grad * logits) + jnp.sum(col_grad * logits)
    row_low = (scale * row_grad).astype(BF16)
    col_low = (scale * col_grad).astype(BF16)
    image_vec_grad = product(row_low, caption_vectors) + product(col_low, caption_vectors)
    caption_vec_grad = left_product(col_low, image_vectors) + left_product(row_low, image_vectors)

    backs = (
        head_backward(image_vec_grad, image_direction, image_scaling, image_head, image_weights),
        head_backward(caption_vec_grad, caption_direction, caption_scaling, caption_head, caption_weights),
    )
    input_grads, query_grads, key_factors, norm_sums = [], [], [], []
    for (kept, weights, mine, picks, count), back in zip(towers, backs):
        mine_of = lambda rows: lax.dynamic_slice_in_dim(rows, index * count, count, 0)
        input_grad, query_grad, key_factor, gain_grad, bias_grad = local_backward(
            kept, mine, picks, mine_of(back[0]), mine_of(back[2]), weights
        )
        input_grads.append(input_grad)
        query_grads.append(query_grad)
        key_factors.append(key_factor)
        norm_sums.extend((gain_grad, bias_grad))

    query_all = gather(jnp.concatenate(query_grads, 1))
    query_all = (query_all[:, :image_width], query_all[:, image_width:])
    sums = jnp.concatenate([image_kept["squares"], caption_kept["squares"]] + norm_sums)
    sums = lax.psum(sums, "dp")
    square_sums = sums[:6]
    norm_totals = []
    start = 6
    for width in (image_width, image_width, caption_width, caption_width):
        norm_totals.append(sums[start : start + width])
        start += width

    shards = []
    for tower in range(2):
        kept, weights, _, _, count = towers[tower]
        _, branch_low, attended_grad, head_sums, factors = backs[tower]
        width = widths[tower]
        size = width // devices
        heads = width // HD
        attended_all, normed_all, queries_all = lows[tower]
        columns = lambda rows: my_columns(rows, rows.shape[-1] // devices, index)
        query_block = left_product(columns(normed_all), query_all[tower])
        blocks = [query_block]
        for factor_rows, side in ((key_factors[tower], queries_all), (kept["value_factor"], attended_grad)):
            met = exchange(factor_rows, devices).reshape(devices, size, heads, count)
            side = side.reshape(devices, count, heads, HD)
            blocks.append(
                jnp.einsum("sfhi,sihd->fhd", met, side, preferred_element_type=F32).reshape(size, width)
            )
        blocks[1] = blocks[1] / 8.0
        bias_wide = jnp.concatenate(
            [
                jnp.sum(query_all[tower].astype(F32), 0),
                jnp.sum(attended_grad.astype(F32), 0),
            ]
        )
        shards.extend(
            (
                columns(norm_totals[2 * tower]),
                columns(norm_totals[2 * tower + 1]),
                jnp.concatenate(blocks, 1),
                columns(bias_wide),
                left_product(columns(attended_all), branch_low),
                columns(head_sums["output_bias"]),
                columns(head_sums["second_gain"]),
                columns(head_sums["second_bias"]),
                left_product(columns(factors["expand"][0]), factors["expand"][1]),
                columns(head_sums["expand_bias"]),
                left_product(columns(factors["reduce"][0]), factors["reduce"][1]),
                columns(head_sums["reduce_bias"]),
                columns(head_sums["final_gain"]),
                columns(head_sums["final_bias"]),
                left_product(columns(factors["projection"][0]), factors["projection"][1]),
            )
        )
    image_cells = float(batch * patches * image_width)
    caption_cells = float(devices * row_count * row_length * caption_width)
    cells = jnp.array([image_cells] * 3 + [caption_cells] * 3, F32)
    return (
        loss.reshape(1),
        jnp.sqrt(square_sums / cells),
        input_grads[0].reshape(images.shape).astype(BF16),
        input_grads[1].reshape(captions.shape).astype(BF16),
        *shards,
        scale_grad.reshape(1),
    )


def solution(mesh):
    rows, matrix, cube = P("dp"), P("dp", None), P("dp", None, None)
    weights = tuple(rows if name in VECTORS else matrix for name in NAMES)
    return jax.shard_map(
        per_device,
        mesh=mesh,
        in_specs=(cube, cube, matrix) + weights + weights + (P(),),
        out_specs=(P(), P(), cube, cube) + weights + weights + (P(),),
        check_vma=False,
    )
```

```python
from types import SimpleNamespace

import jax
import jax.numpy as jnp
from jax import lax
from jax.experimental import pallas as pl
from jax.experimental.pallas import tpu as pltpu
from jax.sharding import PartitionSpec as P

HD = 64
F32 = jnp.float32
BF16 = jnp.bfloat16


def product(left, right):
    return jnp.dot(left, right, preferred_element_type=F32)


def left_product(left, right):
    return lax.dot_general(left, right, (((0,), (0,)), ((), ())), preferred_element_type=F32)


def right_product(left, right):
    return lax.dot_general(left, right, (((1,), (1,)), ((), ())), preferred_element_type=F32)


def unit_norm(rows):
    centred = rows - jnp.mean(rows, -1, keepdims=True)
    inverse = lax.rsqrt(jnp.mean(centred * centred, -1, keepdims=True) + 1e-05)
    return centred * inverse, inverse


def norm_inward(upstream, unit_rows, inverse, gain):
    scaled = upstream * gain
    return inverse * (
        scaled
        - jnp.mean(scaled, -1, keepdims=True)
        - unit_rows * jnp.mean(scaled * unit_rows, -1, keepdims=True)
    )


def caption_allowed(end_rows, length):
    places = jnp.arange(length, dtype=jnp.int32)
    pieces = (places[None, :] >= end_rows[:, 0:1]).astype(jnp.int32) + (
        places[None, :] >= end_rows[:, 1:2]
    ).astype(jnp.int32)
    living = places[None, :] < end_rows[:, 1:2]
    same_piece = pieces[:, :, None] == pieces[:, None, :]
    causal = places[:, None] >= places[None, :]
    diagonal = places[:, None] == places[None, :]
    return same_piece & causal[None] & living[:, None, :] | diagonal[None]


def spread_heads(rows):
    count, width = rows.shape
    heads = width // HD
    head = jnp.arange(heads)[:, None, None]
    lane_head = jnp.arange(width)[None, None, :] // HD
    return jnp.where(head == lane_head, rows[None], jnp.zeros((), rows.dtype)).reshape(
        heads * count, width
    )


def fold_heads(rows, count):
    total, width = rows.shape
    heads = width // HD
    head = jnp.arange(heads)[:, None, None]
    lane_head = jnp.arange(width)[None, None, :] // HD
    return jnp.sum(jnp.where(head == lane_head, rows.reshape(heads, count, width), 0.0), 0)


def local_forward(inputs, allowed, mine, pick_rows, weights):
    sequences, length, width = inputs.shape
    heads = width // HD
    stream = inputs.reshape(sequences * length, width).astype(F32)
    unit_one, inverse_one = unit_norm(stream)
    normed = (unit_one * weights.norm_gain + weights.norm_bias).astype(BF16)
    bias = weights.attend_bias
    bias_full = jnp.concatenate([bias[:width], jnp.zeros((width,), F32), bias[width:]])
    mixed = (product(normed, weights.attend) + bias_full).astype(BF16)
    queries, keys, values = mixed[:, :width], mixed[:, width : 2 * width], mixed[:, 2 * width :]
    split = lambda rows: rows.reshape(sequences, length, heads, HD)
    scores = jnp.einsum("sqhd,skhd->shqk", split(queries), split(keys), preferred_element_type=F32)
    scores = scores / 8.0
    if allowed is not None:
        scores = jnp.where(allowed[:, None], scores, -1e30)
    softened = jax.nn.softmax(scores, axis=-1).astype(BF16)
    attended = jnp.einsum("shqk,skhd->sqhd", softened, split(values), preferred_element_type=F32)
    attended = attended.astype(BF16).reshape(sequences * length, width)
    branch = product(attended, weights.output) + weights.output_bias
    middle = stream + branch
    unit_two, _ = unit_norm(middle)
    normed_two = (unit_two * weights.second_gain + weights.second_bias).astype(BF16)
    hidden = product(normed_two, weights.expand) + weights.expand_bias
    active = (hidden * jax.nn.sigmoid(1.702 * hidden)).astype(BF16)
    second = product(active, weights.reduce) + weights.reduce_bias
    result = middle + second
    squares = jnp.stack([jnp.sum(branch * branch), jnp.sum(second * second), jnp.sum(result * result)])
    picked_queries = queries[pick_rows]
    picked_scores = right_product(keys, spread_heads(picked_queries)) / 8.0
    seen = jnp.tile(mine, (1, heads))
    picked_scores = jnp.where(seen, picked_scores, -1e30)
    soft = jax.nn.softmax(picked_scores, axis=0)
    return SimpleNamespace(
        squares=squares,
        unit_one=unit_one,
        inverse_one=inverse_one,
        normed=normed,
        keys=keys,
        values=values,
        soft=soft,
        value_factor=left_product(normed, soft.astype(BF16)).astype(BF16),
        middle_rows=middle[pick_rows],
        attended_rows=attended[pick_rows],
        normed_rows=normed[pick_rows],
        query_rows=picked_queries,
    )


def head_forward(middle, weights):
    unit_two, inverse_two = unit_norm(middle)
    normed_two = (unit_two * weights.second_gain + weights.second_bias).astype(BF16)
    hidden = product(normed_two, weights.expand) + weights.expand_bias
    active = (hidden * jax.nn.sigmoid(1.702 * hidden)).astype(BF16)
    result = middle + (product(active, weights.reduce) + weights.reduce_bias)
    unit_final, inverse_final = unit_norm(result)
    head_normed = (unit_final * weights.final_gain + weights.final_bias).astype(BF16)
    raw_embed = product(head_normed, weights.projection)
    scaling = lax.rsqrt(jnp.sum(raw_embed * raw_embed, -1, keepdims=True) + 1e-06)
    direction = raw_embed * scaling
    kept = (unit_two, inverse_two, normed_two, hidden, active, unit_final, inverse_final, head_normed)
    return direction.astype(BF16), direction, scaling, kept


def head_backward(upstream, direction, scaling, kept, weights):
    unit_two, inverse_two, normed_two, hidden, active, unit_final, inverse_final, head_normed = kept
    raw_low = (
        scaling * (upstream - direction * jnp.sum(upstream * direction, -1, keepdims=True))
    ).astype(BF16)
    head_grad = right_product(raw_low, weights.projection)
    result_grad = norm_inward(head_grad, unit_final, inverse_final, weights.final_gain)
    second_low = result_grad.astype(BF16)
    gate = jax.nn.sigmoid(1.702 * hidden)
    hidden_low = (
        right_product(second_low, weights.reduce) * (gate + 1.702 * hidden * gate * (1.0 - gate))
    ).astype(BF16)
    two_grad = right_product(hidden_low, weights.expand)
    middle_grad = result_grad + norm_inward(two_grad, unit_two, inverse_two, weights.second_gain)
    branch_low = middle_grad.astype(BF16)
    attended_grad = right_product(branch_low, weights.output).astype(BF16)
    sums = SimpleNamespace(
        final_gain=jnp.sum(head_grad * unit_final, 0),
        final_bias=jnp.sum(head_grad, 0),
        reduce_bias=jnp.sum(second_low.astype(F32), 0),
        expand_bias=jnp.sum(hidden_low.astype(F32), 0),
        second_gain=jnp.sum(two_grad * unit_two, 0),
        second_bias=jnp.sum(two_grad, 0),
        output_bias=jnp.sum(branch_low.astype(F32), 0),
    )
    factors = SimpleNamespace(
        projection=(head_normed, raw_low),
        reduce=(active, second_low),
        expand=(normed_two, hidden_low),
    )
    return middle_grad, branch_low, attended_grad, sums, factors


def local_backward(kept, mine, pick_rows, middle_grad_rows, attended_grad_rows, weights):
    width = weights.output.shape[0]
    count = pick_rows.shape[0]
    heads = width // HD
    wide_grad = spread_heads(attended_grad_rows)
    soft = kept.soft
    soft_grad = right_product(kept.values, wide_grad)
    score_low = (soft * (soft_grad - jnp.sum(soft_grad * soft, 0, keepdims=True))).astype(BF16)
    query_grad = (fold_heads(left_product(score_low, kept.keys), count) / 8.0).astype(BF16)
    key_factor = left_product(kept.normed, score_low).astype(BF16)
    attend = weights.attend
    key_side = right_product(spread_heads(kept.query_rows), attend[:, width : 2 * width]) / 8.0
    value_side = right_product(wide_grad, attend[:, 2 * width :])
    query_side = right_product(query_grad, attend[:, :width])
    normed_grad = product(score_low, key_side.astype(BF16)) + product(
        soft.astype(BF16), value_side.astype(BF16)
    )
    normed_grad = normed_grad.at[pick_rows].add(query_side)
    inward = norm_inward(normed_grad, kept.unit_one, kept.inverse_one, weights.norm_gain)
    input_grad = inward.at[pick_rows].add(middle_grad_rows)
    gain_grad = jnp.sum(normed_grad * kept.unit_one, 0)
    bias_grad = jnp.sum(normed_grad, 0)
    return input_grad, query_grad, key_factor, gain_grad, bias_grad


def my_columns(rows, size, index):
    return lax.dynamic_slice_in_dim(rows, index * size, size, rows.ndim - 1)


NAMES = (
    "norm_gain",
    "norm_bias",
    "attend",
    "attend_bias",
    "output",
    "output_bias",
    "second_gain",
    "second_bias",
    "expand",
    "expand_bias",
    "reduce",
    "reduce_bias",
    "final_gain",
    "final_bias",
    "projection",
)
VECTORS = tuple(name for name in NAMES if name[-4:] in ("bias", "gain"))


MATRICES = (NAMES[2], NAMES[4], NAMES[8], NAMES[10], NAMES[14])
PAIRED = (NAMES[2], NAMES[4], NAMES[8], NAMES[14])
VMEM_LIMIT = 65000 << 10


def gather(rows):
    return lax.all_gather(rows, "dp", axis=0, tiled=True)


def exchange(rows, devices):
    width, terms = rows.shape
    blocks = rows.reshape(devices, width // devices, terms)
    return lax.all_to_all(blocks, "dp", 0, 0)


def gather_weights(shards):
    devices = lax.axis_size("dp")
    whole = {}
    wide = PAIRED
    block = gather(jnp.concatenate([shards[name] for name in wide], 1))
    start = 0
    for name in wide:
        size = shards[name].shape[1]
        whole[name] = block[:, start : start + size]
        start += size
    whole[MATRICES[3]] = gather(shards[MATRICES[3]])
    flat = jnp.concatenate([shards[name] for name in VECTORS])
    flat = gather(flat[None].astype(F32))
    start = 0
    for name in VECTORS:
        size = shards[name].shape[0]
        whole[name] = flat[:, start : start + size].reshape(devices * size)
        start += size
    return SimpleNamespace(**whole)


def per_device(images, captions, caption_ends, *rest):
    image_shards = dict(zip(NAMES, rest[:15]))
    caption_shards = dict(zip(NAMES, rest[15:30]))
    logit_scale = rest[30]
    devices = lax.axis_size("dp")
    if (devices, images.shape, captions.shape) == (BOX, (8, 50, 768), (4, 77, 512)):
        return step_on_box(
            images, captions, caption_ends, image_shards, caption_shards, logit_scale
        )
    index = lax.axis_index("dp")
    image_weights = gather_weights(image_shards)
    caption_weights = gather_weights(caption_shards)
    image_count, patches, image_width = images.shape
    row_count, row_length, caption_width = captions.shape
    batch = devices * image_count

    image_tokens = jnp.arange(image_count * patches, dtype=jnp.int32)
    image_picks = jnp.arange(image_count, dtype=jnp.int32) * patches
    image_mine = image_tokens[:, None] // patches == jnp.arange(image_count)[None, :]
    image_kept = local_forward(images, None, image_mine, image_picks, image_weights)

    caption_tokens = jnp.arange(row_count * row_length, dtype=jnp.int32)[:, None]
    row_start = jnp.arange(row_count, dtype=jnp.int32)[:, None] * row_length
    caption_picks = (row_start + caption_ends - 1).reshape(row_count * 2)
    starts = row_start + jnp.concatenate([jnp.zeros((row_count, 1), jnp.int32), caption_ends[:, :1]], 1)
    caption_mine = (caption_tokens >= starts.reshape(1, -1)) & (caption_tokens <= caption_picks[None, :])
    allowed = caption_allowed(caption_ends, row_length)
    caption_kept = local_forward(captions, allowed, caption_mine, caption_picks, caption_weights)

    towers = (
        (image_kept, image_weights, image_mine, image_picks, image_count),
        (caption_kept, caption_weights, caption_mine, caption_picks, row_count * 2),
    )
    middle_all = gather(jnp.concatenate([image_kept.middle_rows, caption_kept.middle_rows], 1))
    low_rows = []
    for kept in (image_kept, caption_kept):
        low_rows += [kept.attended_rows, kept.normed_rows, kept.query_rows]
    low_all = gather(jnp.concatenate(low_rows, 1))
    widths = (image_width, caption_width)
    middles = (middle_all[:, :image_width], middle_all[:, image_width:])
    lows = []
    start = 0
    for width in widths:
        lows.append(tuple(low_all[:, start + j * width : start + (j + 1) * width] for j in range(3)))
        start += 3 * width

    image_vectors, image_direction, image_scaling, image_head = head_forward(middles[0], image_weights)
    caption_vectors, caption_direction, caption_scaling, caption_head = head_forward(
        middles[1], caption_weights
    )
    scale = jnp.exp(logit_scale[0])
    logits = scale * right_product(image_vectors, caption_vectors)
    places = jnp.arange(batch, dtype=jnp.int32)
    one_hot = (places[:, None] == places[None, :]).astype(F32)
    row_top = jnp.max(logits, 1, keepdims=True)
    row_lse = row_top + jnp.log(jnp.sum(jnp.exp(logits - row_top), 1, keepdims=True))
    col_top = jnp.max(logits, 0, keepdims=True)
    col_lse = col_top + jnp.log(jnp.sum(jnp.exp(logits - col_top), 0, keepdims=True))
    diagonal = jnp.sum(logits * one_hot)
    factor = 1.0 / (2.0 * batch)
    loss = (jnp.sum(row_lse) + jnp.sum(col_lse) - 2.0 * diagonal) * factor
    row_grad = (jnp.exp(logits - row_lse) - one_hot) * factor
    col_grad = (jnp.exp(logits - col_lse) - one_hot) * factor
    scale_grad = jnp.sum(row_grad * logits) + jnp.sum(col_grad * logits)
    row_low = (scale * row_grad).astype(BF16)
    col_low = (scale * col_grad).astype(BF16)
    image_vec_grad = product(row_low, caption_vectors) + product(col_low, caption_vectors)
    caption_vec_grad = left_product(col_low, image_vectors) + left_product(row_low, image_vectors)

    backs = (
        head_backward(image_vec_grad, image_direction, image_scaling, image_head, image_weights),
        head_backward(caption_vec_grad, caption_direction, caption_scaling, caption_head, caption_weights),
    )
    input_grads, query_grads, key_factors, norm_sums = [], [], [], []
    for (kept, weights, mine, picks, count), back in zip(towers, backs):
        mine_of = lambda rows: lax.dynamic_slice_in_dim(rows, index * count, count, 0)
        input_grad, query_grad, key_factor, gain_grad, bias_grad = local_backward(
            kept, mine, picks, mine_of(back[0]), mine_of(back[2]), weights
        )
        input_grads.append(input_grad)
        query_grads.append(query_grad)
        key_factors.append(key_factor)
        norm_sums.extend((gain_grad, bias_grad))

    query_all = gather(jnp.concatenate(query_grads, 1))
    query_all = (query_all[:, :image_width], query_all[:, image_width:])
    sums = jnp.concatenate([image_kept.squares, caption_kept.squares] + norm_sums)
    sums = lax.psum(sums, "dp")
    square_sums = sums[:6]
    norm_totals = []
    start = 6
    for width in (image_width, image_width, caption_width, caption_width):
        norm_totals.append(sums[start : start + width])
        start += width

    shards = []
    for tower in range(2):
        kept, weights, _, _, count = towers[tower]
        _, branch_low, attended_grad, head_sums, factors = backs[tower]
        width = widths[tower]
        size = width // devices
        heads = width // HD
        attended_all, normed_all, queries_all = lows[tower]
        columns = lambda rows: my_columns(rows, rows.shape[-1] // devices, index)
        query_block = left_product(columns(normed_all), query_all[tower])
        blocks = [query_block]
        for factor_rows, side in ((key_factors[tower], queries_all), (kept.value_factor, attended_grad)):
            met = exchange(factor_rows, devices).reshape(devices, size, heads, count)
            side = side.reshape(devices, count, heads, HD)
            blocks.append(
                jnp.einsum("sfhi,sihd->fhd", met, side, preferred_element_type=F32).reshape(size, width)
            )
        blocks[1] = blocks[1] / 8.0
        bias_wide = jnp.concatenate(
            [
                jnp.sum(query_all[tower].astype(F32), 0),
                jnp.sum(attended_grad.astype(F32), 0),
            ]
        )
        shards.extend(
            (
                columns(norm_totals[2 * tower]),
                columns(norm_totals[2 * tower + 1]),
                jnp.concatenate(blocks, 1),
                columns(bias_wide),
                left_product(columns(attended_all), branch_low),
                columns(head_sums.output_bias),
                columns(head_sums.second_gain),
                columns(head_sums.second_bias),
                left_product(columns(factors.expand[0]), factors.expand[1]),
                columns(head_sums.expand_bias),
                left_product(columns(factors.reduce[0]), factors.reduce[1]),
                columns(head_sums.reduce_bias),
                columns(head_sums.final_gain),
                columns(head_sums.final_bias),
                left_product(columns(factors.projection[0]), factors.projection[1]),
            )
        )
    image_cells = float(batch * patches * image_width)
    caption_cells = float(devices * row_count * row_length * caption_width)
    cells = jnp.array([image_cells] * 3 + [caption_cells] * 3, F32)
    return (
        loss.reshape(1),
        jnp.sqrt(square_sums / cells),
        input_grads[0].reshape(images.shape).astype(BF16),
        input_grads[1].reshape(captions.shape).astype(BF16),
        *shards,
        scale_grad.reshape(1),
    )


MESH = pl.DeviceIdType.MESH
BOX = 32


class Tower:
    def __init__(self, is_image, sequences, length, width, hidden, picks):
        self.is_image, self.sequences, self.length = is_image, sequences, length
        self.width, self.hidden = width, hidden
        self.heads = width // HD
        self.picks = picks
        self.tokens = sequences * length
        self.rows = -(-self.tokens // 80) * 80
        self.terms = self.heads * picks
        self.batch = BOX * picks
        self.mine = width // BOX
        self.vector_rows = (0, 8, 9) if is_image else (16, 10, 11)
        if is_image:
            self.window = 112
            self.windows = [(96 * j, 100 * j, 100 * j + 100) for j in range(sequences // 2)]
        else:
            self.window = 96
            self.windows = [
                (length * j // 16 * 16, length * j, length * (j + 1)) for j in range(sequences)
            ]


def iota(shape, axis):
    return lax.broadcasted_iota(jnp.int32, shape, axis)


def dot(left, right, over=((1,), (0,)), precision=None):
    return lax.dot_general(
        left, right, (over, ((), ())), preferred_element_type=F32, precision=precision
    )


ROWS_BY_COLUMNS = ((1,), (1,))
COLUMNS_BY_COLUMNS = ((0,), (0,))
HIGHEST = lax.Precision.HIGHEST


def loop(count, body):
    lax.fori_loop(0, count, lambda step, carry: (body(step), carry)[1], 0)


def rows_at(step, size):
    return pl.ds(pl.multiple_of(step * size, size), size)


def centred_unit(rows):
    width = rows.shape[-1]
    centred = rows - jnp.sum(rows, -1, keepdims=True) * (1.0 / width)
    inverse = lax.rsqrt(jnp.sum(centred * centred, -1, keepdims=True) * (1.0 / width) + 1e-05)
    return centred * inverse, inverse


def inward_of(upstream, unit_rows, inverse, gain):
    width = upstream.shape[-1]
    scaled = upstream * gain
    mean = jnp.sum(scaled, -1, keepdims=True) * (1.0 / width)
    slope = jnp.sum(scaled * unit_rows, -1, keepdims=True) * (1.0 / width)
    return inverse * (scaled - mean - unit_rows * slope)


def gate_of(hidden):
    return 0.5 * jnp.tanh(0.851 * hidden) + 0.5


def column_sum(rows):
    return jnp.sum(rows, 0, keepdims=True)


def spread_rows(rows, heads):
    lane_head = jnp.right_shift(iota(rows.shape, 1), 6)
    return jnp.concatenate([jnp.where(lane_head == h, rows, 0.0) for h in range(heads)], 0).astype(BF16)


def fold_rows(rows, heads, picks):
    lane_head = jnp.right_shift(iota((picks, rows.shape[1]), 1), 6)
    total = jnp.zeros((picks, rows.shape[1]), F32)
    for h in range(heads):
        total = total + jnp.where(lane_head == h, rows[h * picks : (h + 1) * picks], 0.0)
    return total


WIDTH_VECTORS = tuple(name for name in VECTORS if name not in (NAMES[3], NAMES[9]))


class Row:
    norm_gain, norm_bias, output_bias, second_gain, second_bias, reduce_bias, final_gain, final_bias = range(8)


class Places:
    def __init__(self):
        self.me = lax.axis_index("dp")
        self.core = lax.rem(self.me, 2)
        self.x = lax.rem(self.me // 2, 2)
        self.y = lax.rem(self.me // 4, 2)
        self.z = self.me // 8

    def device(self, ahead, across_y, across_x, other):
        z = lax.rem(self.z + ahead, 4)
        y = self.y + across_y - 2 * self.y * across_y
        x = self.x + across_x - 2 * self.x * across_x
        core = self.core + other - 2 * self.core * other
        return ((z * 2 + y) * 2 + x) * 2 + core


class Item:
    def __init__(self, target, size, mode, paired=False):
        self.target, self.size, self.mode, self.paired = target, size, mode, paired
        self.sent = 0


class Spread:
    def __init__(self, places, items, near_sem, core_sem, send_sem):
        self.places, self.items = places, items
        self.near_sem, self.core_sem, self.send_sem = near_sem, core_sem, send_sem
        self.x_next = places.device(0, 0, 1, 0)
        self.y_next = places.device(0, 1, 0, 0)
        self.sibling = places.device(0, 0, 0, 1)
        self.z_next = [None] + [places.device(step, 0, 0, 0) for step in (1, 2, 3)]

    def block(self, number, key):
        item = self.items[number]
        ahead, across_y, across_x = key
        owner = self.places.device((4 - ahead) % 4, across_y, across_x, 0)
        if item.paired:
            half = item.target.shape[1] // 2
            rows = pl.ds(pl.multiple_of((owner // 2) * (2 * item.size), 2 * item.size), 2 * item.size)
            return item.target.at[rows, pl.ds(pl.multiple_of(self.places.core * half, 128), half)]
        return item.target.at[pl.ds(pl.multiple_of(owner * item.size, item.size), item.size)]

    def send(self, number, key, device, sem):
        block = self.block(number, key)
        pltpu.make_async_remote_copy(
            src_ref=block,
            dst_ref=block,
            send_sem=self.send_sem.at[number],
            recv_sem=sem,
            device_id=(device,),
            device_id_type=MESH,
        ).start()
        self.items[number].sent += 1

    def near(self, number, key):
        ahead, across_y, across_x = key
        return self.near_sem.at[number, ahead * 4 + across_y * 2 + across_x]

    def forward(self, number, key):
        ahead, across_y, across_x = key
        item = self.items[number]
        if (across_y, across_x) == (0, 0):
            if ahead == 0:
                for step in (1, 2, 3):
                    self.send(number, key, self.z_next[step], self.near(number, (step, 0, 0)))
            self.send(number, key, self.x_next, self.near(number, (ahead, 0, 1)))
            self.send(number, key, self.y_next, self.near(number, (ahead, 1, 0)))
        elif (across_y, across_x) == (0, 1) and item.mode == "Y":
            self.send(number, key, self.y_next, self.near(number, (ahead, 1, 1)))
        elif (across_y, across_x) == (1, 0) and item.mode == "X":
            self.send(number, key, self.x_next, self.near(number, (ahead, 1, 1)))
        if not (item.paired and key == (0, 0, 0)):
            self.send(number, key, self.sibling, self.core_sem.at[number])

    def whole(self, ref, number, sem):
        return pltpu.make_async_remote_copy(
            src_ref=ref,
            dst_ref=ref,
            send_sem=self.send_sem.at[number],
            recv_sem=sem,
            device_id=(self.sibling,),
            device_id_type=MESH,
        )

    def start(self, number):
        self.forward(number, (0, 0, 0))

    def pass_on(self, number, stage):
        keys = (
            [(step, 0, 0) for step in (1, 2, 3)],
            [(step, *side) for step in range(4) for side in ((0, 1), (1, 0))],
            [(step, 1, 1) for step in range(4)],
        )[stage]
        for key in keys:
            self.whole(self.block(number, key), number, self.near(number, key)).wait_recv()
            self.forward(number, key)

    def wait(self, number):
        item = self.items[number]
        if item.paired:
            ref = item.target.at[pl.ds(0, 30 * item.size), pl.ds(0, item.target.shape[1] // 2)]
        else:
            ref = item.target.at[pl.ds(0, 16 * item.size)]
        self.whole(ref, number, self.core_sem.at[number]).wait_recv()

    def finish(self):
        for number, item in enumerate(self.items):
            rows = item.sent * item.size
            ref = item.target.at[pl.ds(0, rows)]
            self.whole(ref, number, self.core_sem.at[number]).wait_send()


def fraction_floor(numbers, divisor):
    return jnp.floor((numbers.astype(F32) + 0.5) * (1.0 / divisor))


def columns_at(step, size):
    return pl.ds(pl.multiple_of(step * size, size), size)


class Step:
    def __init__(self, towers, r, places):
        self.towers, self.r, self.places = towers, r, places
        self.me = places.me

    def vector(self, tower, row):
        return tower.refs.vectors[row : row + 1, :]


    def pack_vectors(self):
        r = self.r
        pack = r.vpack
        pack[...] = jnp.zeros_like(pack)
        for tower in self.towers:
            first, attend_row, expand_row = tower.vector_rows
            shards = tower.shards
            rows = [(first + k, getattr(shards, name)) for k, name in enumerate(WIDTH_VECTORS)]
            for row, source in rows + [(attend_row, shards.attend_bias), (expand_row, shards.expand_bias)]:
                pack[row : row + 1, 0 : source.shape[0]] = source[...].astype(F32)[None, :]
        r.vall[pl.ds(pl.multiple_of(self.me * 24, 8), 24)] = pack[...]

    def place_own(self, shard, whole):
        size = shard.shape[0]
        whole[pl.ds(pl.multiple_of(self.me * size, size), size)] = shard[...]

    def join_pair(self, shard, other, whole):
        size = shard.shape[0]
        rows = pl.ds(pl.multiple_of((self.me // 2) * (2 * size), 2 * size), 2 * size)
        first = self.places.core == 0

        def body(step):
            columns = columns_at(step, 256)
            own, met = shard[:, columns].astype(F32), other[:, columns].astype(F32)
            both = jnp.concatenate([jnp.where(first, own, met), jnp.where(first, met, own)], 0)
            whole[rows, columns] = both.astype(BF16)

        loop(shard.shape[1] // 256, body)

    def unpack_vectors(self, tower):
        r = self.r
        first, attend_row, expand_row = tower.vector_rows
        width, hidden = tower.width, tower.hidden
        for row, size, target in (
            (first, width // BOX, tower.refs.vectors),
            (attend_row, 2 * width // BOX, tower.refs.attend_vector),
            (expand_row, hidden // BOX, tower.refs.expand_vector),
        ):
            group = row // 8 * 8
            blocks = r.vall[...].reshape(BOX, 24, 128)[:, group : group + 8, :]
            blocks = blocks.reshape(BOX * 8, 128).astype(BF16)
            chunk = 256

            def body(step, row=row, size=size, blocks=blocks, target=target):
                lane = iota((1, chunk), 1) + step * chunk
                owner = fraction_floor(lane, size)
                within = lane.astype(F32) - owner * size
                spread = (iota((128, chunk), 0).astype(F32) == within).astype(F32).astype(BF16)
                met = dot(blocks, spread).reshape(BOX, 8, chunk)
                device = iota((BOX, 8, chunk), 0).astype(F32)
                total = jnp.sum(jnp.where(device == owner.reshape(1, 1, chunk), met, 0.0), 0)
                if target is tower.refs.vectors:
                    target[:, columns_at(step, chunk)] = total
                else:
                    target[0:1, columns_at(step, chunk)] = total[row % 8 : row % 8 + 1]

            loop(target.shape[1] // chunk, body)
        bias = tower.refs.mixed_bias
        bias[0:1, 0:width] = tower.refs.attend_vector[0:1, 0:width]
        bias[0:1, width : 2 * width] = jnp.zeros((1, width), F32)
        bias[0:1, 2 * width :] = tower.refs.attend_vector[0:1, width:]

    def load_tokens(self, tower):
        source, rows = tower.refs.tokens, tower.refs.x
        if tower.rows > tower.tokens:
            low = tower.tokens // 8 * 8
            rows[low:, :] = jnp.zeros((tower.rows - low, tower.width), F32)
        for number in range(tower.sequences):
            start = number * tower.length
            rows[start : start + tower.length, :] = source[number].astype(F32)

    def norm_tokens(self, tower, source, target, gain, bias):
        gain, bias = self.vector(tower, gain), self.vector(tower, bias)

        def body(step):
            rows = rows_at(step, 80)
            unit, _ = centred_unit(source[rows, :])
            target[rows, :] = (unit * gain + bias).astype(BF16)

        loop(tower.rows // 80, body)


    def mix(self, tower):
        normed, mixed = tower.refs.normed, tower.refs.mixed
        weight, bias = tower.weights.attend, tower.refs.mixed_bias

        def body(step):
            columns = columns_at(step, 256)
            mixed[:, columns] = (dot(normed[...], weight[:, columns]) + bias[0:1, columns]).astype(BF16)

        loop(3 * tower.width // 256, body)

    def masks(self, tower):
        bias = tower.refs.mask
        side = tower.window
        query, key = iota((side, side), 0), iota((side, side), 1)
        for number, (row, _, _) in enumerate(tower.windows):
            if tower.is_image:
                allowed = fraction_floor(query + row, tower.length) == fraction_floor(
                    key + row, tower.length
                )
            else:
                first, second = self.r.ends[number, 0], self.r.ends[number, 1]
                query_place, key_place = [
                    place + (row - number * tower.length) for place in (query, key)
                ]

                def piece(place):
                    return jnp.where(place >= first, 1, 0) + jnp.where(place >= second, 1, 0)

                allowed = (
                    (piece(query_place) == piece(key_place))
                    & (query_place >= key_place)
                    & (key_place < second)
                    & (key_place >= 0)
                    & (query_place < tower.length)
                ) | (query == key)
            bias[number] = jnp.where(allowed, 0.0, -1e30)

    def attend(self, tower):
        width, side = tower.width, tower.window
        mixed, total, bias = tower.refs.mixed, tower.refs.att, tower.refs.mask
        total[...] = jnp.zeros_like(total)

        def body(step):
            lane = iota((1, 128), 1)
            left = jnp.where(lane < HD, 1.0, 0.0)
            sides = (left.astype(BF16), (1.0 - left).astype(BF16))
            for number, (row, first, last) in enumerate(tower.windows):
                rows = slice(row, row + side)
                query, key, value = [
                    mixed[rows, columns_at(step + part * (width // 128), 128)] for part in range(3)
                ]
                out = []
                for half in sides:
                    scores = dot(query * half, key, ROWS_BY_COLUMNS) * 0.125 + bias[number]
                    weights = jnp.exp(scores - jnp.max(scores, -1, keepdims=True))
                    weights = weights * (1.0 / jnp.sum(weights, -1, keepdims=True))
                    out.append(dot(weights.astype(BF16), value))
                both = jnp.where(lane < HD, out[0], out[1])
                place = iota((side, 1), 0) + row
                kept = jnp.where((place >= first) & (place < last), 1.0, 0.0)
                columns = columns_at(step, 128)
                total[rows, columns] = total[rows, columns] + both * kept

        loop(width // 128, body)
        low = tower.refs.attlow

        def narrow(step):
            low[rows_at(step, 80), :] = total[rows_at(step, 80), :].astype(BF16)

        loop(tower.rows // 80, narrow)

    def add_square(self, slot, rows, tower):
        if tower.rows > tower.tokens:
            rows = jnp.where(iota((rows.shape[0], 1), 0) < tower.tokens, rows, 0.0)
        squares = column_sum(rows * rows)
        width = squares.shape[1]
        folded = sum(squares[:, k * 128 : (k + 1) * 128] for k in range(width // 128))
        self.r.squares[slot : slot + 1, :] = self.r.squares[slot : slot + 1, :] + folded

    def project(self, tower):
        stream, middle, low = tower.refs.x, tower.refs.middle, tower.refs.attlow
        weight = tower.weights.output
        slot = 0 if tower.is_image else 3
        bias_row = Row.output_bias

        def body(step):
            columns = columns_at(step, 256)
            bias = tower.refs.vectors[bias_row : bias_row + 1, columns]
            branch = dot(low[...], weight[:, columns]) + bias
            middle[:, columns] = stream[:, columns] + branch
            self.add_square(slot, branch, tower)

        loop(tower.width // 256, body)

    def own_active(self, tower):
        rows = slice(0, tower.rows)
        normed, active = tower.refs.normed_two, self.r.active
        weight, bias = tower.weights.expand, tower.refs.expand_vector

        def body(step):
            columns = columns_at(step, 256)
            hidden = dot(normed[...], weight[:, columns]) + bias[0:1, columns]
            active[rows, columns] = (hidden * gate_of(hidden)).astype(BF16)

        loop(tower.hidden // 256, body)

    def own_second(self, tower):
        rows = slice(0, tower.rows)
        active, middle, weight = self.r.active, tower.refs.middle, tower.weights.reduce
        slot = 1 if tower.is_image else 4
        bias_row = Row.reduce_bias

        def body(step):
            columns = columns_at(step, 256)
            bias = tower.refs.vectors[bias_row : bias_row + 1, columns]
            second = dot(active[rows, 0 : tower.hidden], weight[:, columns]) + bias
            self.add_square(slot, second, tower)
            self.add_square(slot + 1, second + middle[:, columns], tower)

        loop(tower.width // 256, body)


    def pick_places(self, tower):
        if tower.is_image:
            return [(i * tower.length, i * tower.length) for i in range(tower.picks)]
        places = []
        for i in range(tower.picks):
            start, ends = (i // 2) * tower.length, self.r.ends
            first = start + (ends[i // 2, 0] if i % 2 else 0)
            places.append((first, start + ends[i // 2, i % 2] - 1))
        return places

    def selection(self, tower):
        row = iota((tower.picks, 1), 0)
        token = jnp.zeros((tower.picks, 1), jnp.int32)
        for i, (_, pick) in enumerate(self.pick_places(tower)):
            token = jnp.where(row == i, pick, token)
        return jnp.where(iota((tower.picks, tower.rows), 1) == token, 1.0, 0.0)

    def placement(self, tower):
        lane = iota((1, tower.picks), 1)
        token = jnp.zeros((1, tower.picks), jnp.int32)
        for i, (_, pick) in enumerate(self.pick_places(tower)):
            token = jnp.where(lane == i, pick, token)
        return jnp.where(iota((tower.rows, tower.picks), 0) == token, 1.0, 0.0)

    def picked_forward(self, tower):
        width, heads, terms, picks = tower.width, tower.heads, tower.terms, tower.picks
        select = self.selection(tower)
        low_select = select.astype(BF16)
        mixed, normed = tower.refs.mixed, tower.refs.normed
        queries = dot(low_select, mixed[:, 0:width])
        middle_rows = dot(select, tower.refs.middle[...], precision=HIGHEST)
        normed_rows = dot(low_select, normed[...])
        attended_rows = dot(low_select, tower.refs.attlow[...])
        wide = spread_rows(queries, heads)
        tower.refs.qe[...] = wide
        scores = dot(mixed[:, width : 2 * width], wide, ROWS_BY_COLUMNS) * 0.125
        lane = jnp.bitwise_and(iota((1, terms), 1), picks - 1)
        first = jnp.zeros((1, terms), jnp.int32)
        last = jnp.zeros((1, terms), jnp.int32)
        for i, (begin, pick) in enumerate(self.pick_places(tower)):
            first = jnp.where(lane == i, begin, first)
            last = jnp.where(lane == i, pick, last)
        if tower.is_image:
            last = first + (tower.length - 1)
        place = iota((tower.rows, terms), 0)
        scores = jnp.where((place >= first) & (place <= last), scores, -1e30)
        soft = jnp.exp(scores - jnp.max(scores, 0, keepdims=True))
        soft = soft * (1.0 / column_sum(soft))
        tower.refs.soft[...] = soft
        factor = dot(soft.astype(BF16), normed[...], COLUMNS_BY_COLUMNS)
        pad = jnp.zeros((128 - terms - 2 * picks, width), F32)
        rows = jnp.concatenate([factor, normed_rows, attended_rows, pad], 0)
        self.store_factor(tower, tower.refs.t_met, rows)
        return middle_rows, queries

    def store_factor(self, tower, met, rows):
        blocks = rows.T.reshape(BOX, tower.mine, 128).astype(BF16)
        tower.refs.factor_out[...] = blocks
        met[self.me] = tower.refs.factor_out[self.me]


    def head_middle(self, tower, rows):
        start = 0 if tower.is_image else self.towers[0].width
        return self.r.middles[rows, start : start + tower.width]

    def head_hidden(self, tower):
        normed = tower.refs.h_normed
        gain, bias = self.vector(tower, Row.second_gain), self.vector(tower, Row.second_bias)

        def norm(step):
            rows = rows_at(step, 64)
            unit, _ = centred_unit(self.head_middle(tower, rows))
            normed[rows, :] = (unit * gain + bias).astype(BF16)

        loop(tower.batch // 64, norm)
        weight, expand_bias = tower.weights.expand, tower.refs.expand_vector
        hidden_ref, active = tower.refs.h_hidden, tower.refs.h_active

        def body(step):
            columns = columns_at(step, 256)
            hidden = dot(normed[...], weight[:, columns]) + expand_bias[0:1, columns]
            hidden_ref[:, columns] = hidden
            active[:, columns] = (hidden * gate_of(hidden)).astype(BF16)

        loop(tower.hidden // 256, body)

    def head_vectors(self, tower):
        result, active = tower.refs.h_unit, tower.refs.h_active
        weight = tower.weights.reduce
        bias_row = Row.reduce_bias
        start = 0 if tower.is_image else self.towers[0].width

        def body(step):
            columns = columns_at(step, 256)
            bias = tower.refs.vectors[bias_row : bias_row + 1, columns]
            middle = self.r.middles[:, pl.ds(pl.multiple_of(start + step * 256, 256), 256)]
            result[:, columns] = middle + (dot(active[...], weight[:, columns]) + bias)

        loop(tower.width // 256, body)
        gain, bias = self.vector(tower, Row.final_gain), self.vector(tower, Row.final_bias)
        inverse_ref, normed = tower.refs.h_inverse, tower.refs.h_final

        def norm(step):
            rows = rows_at(step, 64)
            unit, inverse = centred_unit(result[rows, :])
            result[rows, :] = unit
            inverse_ref[rows, :] = inverse
            normed[rows, :] = (unit * gain + bias).astype(BF16)

        loop(tower.batch // 64, norm)

        def embed(step):
            rows = rows_at(step, 64)
            raw = dot(normed[rows, :], tower.weights.projection[...])
            scaling = lax.rsqrt(jnp.sum(raw * raw, -1, keepdims=True) + 1e-06)
            direction = raw * scaling
            tower.refs.h_scaling[rows, :] = scaling
            tower.refs.h_direction[rows, :] = direction
            tower.refs.h_vectors[rows, :] = direction.astype(BF16)

        loop(tower.batch // 64, embed)

    def contrast(self):
        image, caption = self.towers
        batch = image.batch
        vectors, others = image.refs.h_vectors[...], caption.refs.h_vectors[...]
        scale = jnp.exp(jnp.full((1, 1), self.r.logit_scale[0], F32))
        logits = scale * dot(vectors, others, ROWS_BY_COLUMNS)
        same = jnp.where(iota((batch, batch), 0) == iota((batch, batch), 1), 1.0, 0.0)
        row_top = jnp.max(logits, 1, keepdims=True)
        row_lse = row_top + jnp.log(jnp.sum(jnp.exp(logits - row_top), 1, keepdims=True))
        column_top = jnp.max(logits, 0, keepdims=True)
        column_lse = column_top + jnp.log(column_sum(jnp.exp(logits - column_top)))

        def whole_sum(rows):
            return jnp.sum(column_sum(rows), 1, keepdims=True)

        factor = 1.0 / (2.0 * batch)
        loss = (
            whole_sum(row_lse) + whole_sum(column_lse) - 2.0 * whole_sum(logits * same)
        ) * factor
        row_grad = (jnp.exp(logits - row_lse) - same) * factor
        column_grad = (jnp.exp(logits - column_lse) - same) * factor
        scale_grad = whole_sum(row_grad * logits) + whole_sum(column_grad * logits)
        self.r.out_loss[...] = loss[0, :]
        self.r.out_scale[...] = scale_grad[0, :]
        row_low, column_low = self.r.row_low, self.r.column_low
        row_low[...] = (scale * row_grad).astype(BF16)
        column_low[...] = (scale * column_grad).astype(BF16)

        def image_side(step):
            rows = rows_at(step, 64)
            others = caption.refs.h_vectors[...]
            self.raw_grad(image, rows, dot(row_low[rows, :], others) + dot(column_low[rows, :], others))

        def caption_side(step):
            rows = rows_at(step, 128)
            others = image.refs.h_vectors[...]
            upstream = dot(column_low[:, rows], others, COLUMNS_BY_COLUMNS)
            upstream = upstream + dot(row_low[:, rows], others, COLUMNS_BY_COLUMNS)
            self.raw_grad(caption, rows, upstream)

        loop(batch // 64, image_side)
        loop(batch // 128, caption_side)

    def raw_grad(self, tower, rows, upstream):
        direction = tower.refs.h_direction[rows, :]
        along = jnp.sum(upstream * direction, -1, keepdims=True)
        raw = tower.refs.h_scaling[rows, :] * (upstream - direction * along)
        tower.refs.h_raw[rows, :] = raw.astype(BF16)

    def add_sum(self, tower, slot, row):
        sums = tower.refs.sums
        sums[slot : slot + 1, :] = sums[slot : slot + 1, :] + row

    def against(self, tower, source, weight, target):
        def body(step):
            target[:, columns_at(step, 256)] = dot(
                source[...], weight[rows_at(step, 256), :], ROWS_BY_COLUMNS
            )

        loop(tower.width // 256, body)

    def head_backward(self, tower):
        grad, result_grad = tower.refs.h_grad, tower.refs.h_middle_grad
        unit_ref, inverse_ref = tower.refs.h_unit, tower.refs.h_inverse
        second_low = tower.refs.h_second_low
        tower.refs.sums[...] = jnp.zeros_like(tower.refs.sums)
        self.against(tower, tower.refs.h_raw, tower.weights.projection, grad)
        gain = self.vector(tower, Row.final_gain)

        def final_norm(step):
            rows = rows_at(step, 64)
            upstream, unit = grad[rows, :], unit_ref[rows, :]
            inward = inward_of(upstream, unit, inverse_ref[rows, :], gain)
            low = inward.astype(BF16)
            result_grad[rows, :] = inward
            second_low[rows, :] = low
            self.add_sum(tower, Row.final_gain, column_sum(upstream * unit))
            self.add_sum(tower, Row.final_bias, column_sum(upstream))
            self.add_sum(tower, Row.reduce_bias, column_sum(low.astype(F32)))

        loop(tower.batch // 64, final_norm)
        weight, hidden_ref = tower.weights.reduce, tower.refs.h_hidden
        hidden_low, expand_sums = tower.refs.h_hidden_low, tower.refs.expand_sums

        def body(step):
            columns = columns_at(step, 256)
            active_grad = dot(second_low[...], weight[rows_at(step, 256), :], ROWS_BY_COLUMNS)
            hidden = hidden_ref[:, columns]
            gate = gate_of(hidden)
            low = (active_grad * (gate + 1.702 * hidden * gate * (1.0 - gate))).astype(BF16)
            hidden_low[:, columns] = low
            expand_sums[0:1, columns] = column_sum(low.astype(F32))

        loop(tower.hidden // 256, body)
        self.against(tower, hidden_low, tower.weights.expand, grad)
        second_gain, branch_low = self.vector(tower, Row.second_gain), tower.refs.h_branch_low

        def second_norm(step):
            rows = rows_at(step, 64)
            upstream = grad[rows, :]
            unit, inverse = centred_unit(self.head_middle(tower, rows))
            inward = result_grad[rows, :] + inward_of(upstream, unit, inverse, second_gain)
            low = inward.astype(BF16)
            result_grad[rows, :] = inward
            branch_low[rows, :] = low
            self.add_sum(tower, Row.second_gain, column_sum(upstream * unit))
            self.add_sum(tower, Row.second_bias, column_sum(upstream))
            self.add_sum(tower, Row.output_bias, column_sum(low.astype(F32)))

        loop(tower.batch // 64, second_norm)
        self.against(tower, branch_low, tower.weights.output, grad)

        def narrow(step):
            rows = rows_at(step, 64)
            low = grad[rows, :].astype(BF16).astype(F32)
            grad[rows, :] = low
            tower.refs.value_sums[0:1, :] = tower.refs.value_sums[0:1, :] + column_sum(low)

        tower.refs.value_sums[...] = jnp.zeros_like(tower.refs.value_sums)
        loop(tower.batch // 64, narrow)


    def local_backward(self, tower):
        width, heads, picks, terms = tower.width, tower.heads, tower.picks, tower.terms
        mine = pl.ds(pl.multiple_of(self.me * picks, picks), picks)
        wide_grad = spread_rows(tower.refs.h_grad[mine, :], heads)
        mixed, normed = tower.refs.mixed, tower.refs.normed
        soft = tower.refs.soft[...]
        soft_grad = dot(mixed[:, 2 * width :], wide_grad, ROWS_BY_COLUMNS)
        score_low = (soft * (soft_grad - column_sum(soft_grad * soft))).astype(BF16)
        query_grad = fold_rows(
            dot(score_low, mixed[:, width : 2 * width], COLUMNS_BY_COLUMNS), heads, picks
        )
        query_low = (query_grad * 0.125).astype(BF16)
        attend = tower.weights.attend
        scores_ref, soft_low, wide_ref = self.r.score_low, self.r.soft_low, self.r.wide_grad
        scores_ref[0 : tower.rows, 0:terms] = score_low
        soft_low[0 : tower.rows, 0:terms] = soft.astype(BF16)
        wide_ref[0:terms, 0:width] = wide_grad
        placement = self.r.placement
        placement[0 : tower.rows, :] = self.placement(tower)
        queries = tower.refs.qe

        def sides(step):
            rows = rows_at(step, 256)
            key_side = dot(queries[...], attend[rows, width : 2 * width], ROWS_BY_COLUMNS) * 0.125
            value_side = dot(wide_ref[0:terms, 0:width], attend[rows, 2 * width :], ROWS_BY_COLUMNS)
            query_side = dot(query_low, attend[rows, 0:width], ROWS_BY_COLUMNS)
            tower.refs.att[:, rows] = (
                dot(scores_ref[0 : tower.rows, 0:terms], key_side.astype(BF16))
                + dot(soft_low[0 : tower.rows, 0:terms], value_side.astype(BF16))
                + dot(placement[0 : tower.rows, :], query_side, precision=HIGHEST)
            )

        loop(width // 256, sides)
        key_factor = dot(score_low, normed[...], COLUMNS_BY_COLUMNS)
        gain = self.vector(tower, Row.norm_gain)
        source, grad = tower.refs.tokens, tower.refs.att
        sums = tower.refs.norm_sums
        sums[...] = jnp.zeros_like(sums)
        for number in range(tower.sequences):
            rows = slice(number * tower.length, (number + 1) * tower.length)
            upstream = grad[rows, :]
            unit, inverse = centred_unit(source[number].astype(F32))
            grad[rows, :] = inward_of(upstream, unit, inverse, gain)
            sums[0:1, :] = sums[0:1, :] + column_sum(upstream * unit)
            sums[1:2, :] = sums[1:2, :] + column_sum(upstream)
        pad = jnp.zeros((128 - terms - 8, width), F32)
        self.store_factor(tower, tower.refs.s_met, jnp.concatenate([key_factor, sums[...], pad], 0))
        return query_low.astype(F32)

    def input_gradient(self, tower):
        mine = pl.ds(pl.multiple_of(self.me * tower.picks, tower.picks), tower.picks)
        grad, out = tower.refs.att, tower.refs.out_tokens
        placement = self.r.placement
        placement[0 : tower.rows, :] = self.placement(tower)

        def add(step):
            columns = columns_at(step, 256)
            middle_grad = tower.refs.h_middle_grad[mine, columns]
            placed = dot(placement[0 : tower.rows, :], middle_grad, precision=HIGHEST)
            grad[:, columns] = grad[:, columns] + placed

        loop(tower.width // 256, add)
        for number in range(tower.sequences):
            start = number * tower.length
            out[number] = grad[start : start + tower.length, :].astype(BF16)


    def my_columns(self, total, size):
        return jnp.where(iota((size, total), 1) == iota((size, total), 0) + self.me * size, 1.0, 0.0)

    def turned_columns(self, source, size):
        pick = self.my_columns(source.shape[1], size).astype(BF16)
        return dot(pick, source[...], ROWS_BY_COLUMNS).astype(BF16)

    def gradient_blocks(self, left, right, out):
        step_size = 256

        def body(step):
            columns = columns_at(step, step_size)
            out[:, columns] = dot(left, right[:, columns])

        loop(right.shape[1] // step_size, body)

    def head_gradients(self, tower):
        size = tower.mine
        self.gradient_blocks(
            self.turned_columns(tower.refs.h_final, size),
            tower.refs.h_raw,
            tower.outs.projection,
        )
        self.gradient_blocks(
            self.turned_columns(tower.refs.h_active, tower.hidden // BOX),
            tower.refs.h_second_low,
            tower.outs.reduce,
        )
        self.gradient_blocks(
            self.turned_columns(tower.refs.h_normed, size),
            tower.refs.h_hidden_low,
            tower.outs.expand,
        )
        pick = self.my_columns(tower.width, size)
        sums = dot(tower.refs.sums[...], pick, ROWS_BY_COLUMNS, HIGHEST)
        for k, name in enumerate(WIDTH_VECTORS[2:], 2):
            getattr(tower.outs, name)[...] = sums[k, :]
        pick = self.my_columns(tower.hidden, tower.hidden // BOX)
        tower.outs.expand_bias[...] = dot(
            tower.refs.expand_sums[...], pick, ROWS_BY_COLUMNS, HIGHEST
        )[0, :]

    def gathered_terms(self, tower, lane):
        met = tower.refs.t_met
        picks = tower.picks
        tiles = []
        spot = jnp.right_shift(iota((1, 128), 1), 3)
        for tile in range(tower.batch // 128):
            total = jnp.zeros((tower.mine, 128), F32)
            for k in range(128 // picks):
                block = met[tile * (128 // picks) + k].astype(F32)
                turned = pltpu.roll(block, (picks * k - lane) % 128, 1)
                total = total + jnp.where(spot == k, turned, 0.0)
            tiles.append(total)
        return jnp.concatenate(tiles, 1).astype(BF16)

    def output_gradient(self, tower):
        self.gradient_blocks(
            self.gathered_terms(tower, tower.terms + tower.picks),
            tower.refs.h_branch_low,
            tower.outs.output,
        )

    def factor_gradient(self, tower, met, side_of, part, scale):
        width, terms = tower.width, tower.terms
        out = tower.outs.attend
        columns = slice(part * width, (part + 1) * width)
        group = 2
        term, lane = iota((128, width), 0), iota((128, width), 1)
        mask = jnp.where((jnp.right_shift(term, 3) == jnp.right_shift(lane, 6)) & (term < terms), scale, 0.0)
        tower.refs.headmask[...] = mask
        out[:, columns] = jnp.zeros((tower.mine, width), F32)

        def body(step):
            left, right = [], []
            for k in range(group):
                device = step * group + k
                left.append(met[device])
                tall = jnp.concatenate([side_of(device)] * (128 // tower.picks), 0)
                right.append((tall * tower.refs.headmask[...]).astype(BF16))
            out[:, columns] = out[:, columns] + dot(
                jnp.concatenate(left, 1), jnp.concatenate(right, 0)
            )

        loop(BOX // group, body)

    def rows_of_pair(self, tower, ref, device):
        block = ref[pl.ds(pl.multiple_of(device * 16, 16), 16), :].astype(F32)
        rows = jnp.concatenate([block[0:8], block[8:16]], 1)
        start = 0 if tower.is_image else self.towers[0].width
        return rows[:, start : start + tower.width]

    def value_gradient(self, tower):
        grad, picks = tower.refs.h_grad, tower.picks

        def side(device):
            return grad[pl.ds(pl.multiple_of(device * picks, picks), picks), :]

        self.factor_gradient(tower, tower.refs.t_met, side, 2, 1.0)

    def key_gradient(self, tower):
        self.factor_gradient(
            tower,
            tower.refs.s_met,
            lambda device: self.rows_of_pair(tower, self.r.queries, device),
            1,
            0.125,
        )

    def query_gradient(self, tower):
        r, size, width = self.r, tower.mine, tower.width
        rows = tower.refs.h_query_low
        for device in range(0, BOX, 2):
            pair = [self.rows_of_pair(tower, r.query_grads, device + k) for k in range(2)]
            rows[device * 8 : device * 8 + 16, :] = jnp.concatenate(pair, 0).astype(BF16)
        left = self.gathered_terms(tower, tower.terms)
        tower.outs.attend[:, 0:width] = dot(left, rows[...])
        bias = tower.refs.bias_sums
        bias[0:1, 0:width] = column_sum(rows[...].astype(F32))
        bias[0:1, width:] = tower.refs.value_sums[0:1, :]
        pick = self.my_columns(2 * width, 2 * size)
        tower.outs.attend_bias[...] = dot(bias[...], pick, ROWS_BY_COLUMNS, HIGHEST)[0, :]
        total = jnp.zeros((size, 128), F32)
        met = tower.refs.s_met
        for device in range(BOX):
            total = total + met[device].astype(F32)
        lane = iota((8, 128), 1)
        row = iota((8, 128), 0)
        pick = jnp.where(lane == row + tower.terms, 1.0, 0.0)
        sums = dot(pick, total, ROWS_BY_COLUMNS, HIGHEST)
        tower.outs.norm_gain[...] = sums[0, :]
        tower.outs.norm_bias[...] = sums[1, :]


class Route:
    (
        vectors,
        caption_attend,
        caption_output,
        image_attend,
        image_output,
        caption_expand,
        caption_reduce,
        middles,
        queries,
        caption_projection,
        image_projection,
        image_expand,
        image_reduce,
        query_grads,
    ) = range(14)


def swap_out(me, count, source_of, target, send_sem, recv_sem):
    def body(step):
        device = lax.rem(me + 1 + step, count)
        pltpu.make_async_remote_copy(
            src_ref=source_of(device),
            dst_ref=target.at[me],
            send_sem=send_sem,
            recv_sem=recv_sem,
            device_id=(device,),
            device_id_type=MESH,
        ).start()

    loop(count - 1, body)


def swap_descriptor(me, count, target, send_sem, recv_sem):
    most = target.at[pl.ds(0, count - 1)]
    return pltpu.make_async_remote_copy(
        src_ref=most,
        dst_ref=most,
        send_sem=send_sem,
        recv_sem=recv_sem,
        device_id=(lax.rem(me + 1, count),),
        device_id_type=MESH,
    )


def step_kernel(image, caption, r):
    for tower in (image, caption):
        refs, batch = tower.refs, tower.batch
        refs.middle = refs.x
        refs.normed_two = refs.mixed.at[:, 0 : tower.width]
        refs.h_branch_low = refs.attlow.at[0:batch]
        refs.h_second_low = refs.mixed.at[0:batch, 0 : tower.width]
        refs.h_query_low = refs.h_normed
        refs.headmask = r.headmask.at[:, 0 : tower.width]
    places = Places()
    me = places.me
    step = Step((image, caption), r, places)
    routes = (
        (None, r.vall, 24, "X"),
        (caption.shards.attend, caption.weights.attend, 0, "X"),
        (caption.shards.output, caption.weights.output, 0, "Y"),
        (image.shards.attend, image.weights.attend, r.sib_attend, "Y"),
        (image.shards.output, image.weights.output, r.sib_output, "X"),
        (caption.shards.expand, caption.weights.expand, 0, "Y"),
        (caption.shards.reduce, caption.weights.reduce, 0, "X"),
        (None, r.middles, 8, "Y"),
        (None, r.queries, 16, "X"),
        (caption.shards.projection, caption.weights.projection, 0, "Y"),
        (image.shards.projection, image.weights.projection, r.sib_projection, "X"),
        (image.shards.expand, image.weights.expand, r.sib_expand, "X"),
        (image.shards.reduce, image.weights.reduce, 0, "Y"),
        (None, r.query_grads, 16, "X"),
    )
    items, pairs = [], {}
    for number, (shard, whole, other, mode) in enumerate(routes):
        if shard is None:
            items.append(Item(whole, other, mode))
            continue
        paired = not isinstance(other, int)
        if paired:
            pairs[number] = other
        items.append(Item(whole, shard.shape[0], mode, paired))
    spread = Spread(places, items, r.near_sem, r.core_sem, r.send_sem)

    barrier = pltpu.get_barrier_semaphore()
    loop(
        BOX - 1,
        lambda k: pl.semaphore_signal(
            barrier, inc=1, device_id=(lax.rem(me + 1 + k, BOX),), device_id_type=MESH
        ),
    )
    step.pack_vectors()
    pl.semaphore_wait(barrier, BOX - 1)

    pair_copies = {}
    for k, (number, other) in enumerate(pairs.items()):
        pair_copies[number] = pltpu.make_async_remote_copy(
            src_ref=routes[number][0],
            dst_ref=other,
            send_sem=r.pair_sem.at[0, k],
            recv_sem=r.pair_sem.at[1, k],
            device_id=(spread.sibling,),
            device_id_type=MESH,
        )
        pair_copies[number].start()
    for number, (shard, whole, other, _) in enumerate(routes):
        if number in pairs:
            pair_copies[number].wait()
            step.join_pair(shard, other, whole)
        elif shard is not None:
            step.place_own(shard, whole)
        if number == Route.vectors or shard is not None:
            spread.start(number)

    def service(t):
        for stage in range(3):
            if 0 <= t - stage < Route.query_grads:
                spread.pass_on(t - stage, stage)

    service(0)
    service(1)
    step.load_tokens(caption)
    step.load_tokens(image)
    step.masks(image)
    step.masks(caption)
    r.squares[...] = jnp.zeros_like(r.squares)
    service(2)
    spread.wait(Route.vectors)
    for tower in (caption, image):
        step.unpack_vectors(tower)
        step.norm_tokens(tower, tower.refs.x, tower.refs.normed, Row.norm_gain, Row.norm_bias)
    service(3)
    spread.wait(Route.caption_attend)
    step.mix(caption)
    step.attend(caption)
    service(4)
    spread.wait(Route.caption_output)
    step.project(caption)
    service(5)
    spread.wait(Route.image_attend)
    step.mix(image)
    service(6)
    step.attend(image)
    spread.wait(Route.image_output)
    step.project(image)
    picked = [step.picked_forward(tower) for tower in (image, caption)]
    mine = pl.ds(pl.multiple_of(me * 8, 8), 8)
    r.middles[mine, :] = jnp.concatenate([rows for rows, _ in picked], 1)
    queries = jnp.concatenate([rows for _, rows in picked], 1)
    half = queries.shape[1] // 2
    wide_mine = pl.ds(pl.multiple_of(me * 16, 16), 16)
    r.queries[wide_mine, :] = jnp.concatenate([queries[:, :half], queries[:, half:]], 0).astype(BF16)
    spread.start(Route.middles)
    spread.start(Route.queries)
    swap_sem = r.swap_sem
    for k, tower in enumerate((image, caption)):
        out, met = tower.refs.factor_out, tower.refs.t_met
        swap_out(me, BOX, lambda d, out=out: out.at[d], met, swap_sem.at[0, k], swap_sem.at[1, k])
    service(7)
    for tower in (caption, image):
        step.norm_tokens(
            tower, tower.refs.middle, tower.refs.normed_two, Row.second_gain, Row.second_bias
        )
    service(8)
    spread.wait(Route.caption_expand)
    step.own_active(caption)
    spread.wait(Route.caption_reduce)
    step.own_second(caption)
    service(9)
    spread.wait(Route.middles)
    step.head_hidden(caption)
    service(10)
    service(11)
    spread.wait(Route.caption_projection)
    step.head_vectors(caption)
    service(12)
    service(13)
    spread.wait(Route.image_expand)
    step.head_hidden(image)
    step.own_active(image)
    service(14)
    spread.wait(Route.image_reduce)
    spread.wait(Route.image_projection)
    spread.wait(Route.queries)
    step.head_vectors(image)
    step.contrast()
    step.head_backward(image)
    step.head_backward(caption)
    for k, tower in enumerate((image, caption)):
        swap_descriptor(me, BOX, tower.refs.t_met, swap_sem.at[0, k], swap_sem.at[1, k]).wait()
    grads = jnp.concatenate([step.local_backward(tower) for tower in (image, caption)], 1)
    r.query_grads[wide_mine, :] = jnp.concatenate([grads[:, :half], grads[:, half:]], 0).astype(BF16)
    spread.start(Route.query_grads)
    for k, tower in enumerate((image, caption), 2):
        out, met = tower.refs.factor_out, tower.refs.s_met
        swap_out(me, BOX, lambda d, out=out: out.at[d], met, swap_sem.at[0, k], swap_sem.at[1, k])
    step.own_second(image)
    spread.pass_on(Route.query_grads, 0)
    squares = r.squares
    r.squares_met[me] = squares[...]
    swap_out(me, BOX, lambda d: squares, r.squares_met, swap_sem.at[0, 4], swap_sem.at[1, 4])
    step.head_gradients(caption)
    spread.pass_on(Route.query_grads, 1)
    step.head_gradients(image)
    spread.pass_on(Route.query_grads, 2)
    for tower in (image, caption):
        step.input_gradient(tower)
        step.output_gradient(tower)
        step.value_gradient(tower)
    for k, tower in enumerate((image, caption), 2):
        swap_descriptor(me, BOX, tower.refs.s_met, swap_sem.at[0, k], swap_sem.at[1, k]).wait()
    for tower in (image, caption):
        step.key_gradient(tower)
    spread.wait(Route.query_grads)
    for tower in (image, caption):
        step.query_gradient(tower)
    swap_descriptor(me, BOX, r.squares_met, swap_sem.at[0, 4], swap_sem.at[1, 4]).wait()
    totals = jnp.sum(r.squares_met[...], 0)
    slot = iota((8, 128), 0)
    cells = jnp.where(
        slot < 3,
        1.0 / (BOX * image.tokens * image.width),
        1.0 / (BOX * caption.tokens * caption.width),
    )
    means = jnp.sqrt(jnp.sum(totals, 1, keepdims=True) * cells)
    diagonal = jnp.where(slot == iota((8, 128), 1), means, 0.0)
    r.out_rms[...] = column_sum(diagonal)[0, :6]
    spread.finish()


def tower_scratch(tower, embed):
    width, hidden, rows, batch = tower.width, tower.hidden, tower.rows, tower.batch
    return dict(
        vectors=((8, width), F32),
        attend_vector=((8, 2 * width), F32),
        expand_vector=((8, hidden), F32),
        mixed_bias=((8, 3 * width), F32),
        sums=((8, width), F32),
        value_sums=((8, width), F32),
        norm_sums=((8, width), F32),
        bias_sums=((8, 2 * width), F32),
        expand_sums=((8, hidden), F32),
        x=((rows, width), F32),
        normed=((rows, width), BF16),
        mixed=((rows, 3 * width), BF16),
        att=((rows, width), F32),
        attlow=((rows, width), BF16),
        mask=((len(tower.windows), tower.window, tower.window), F32),
        soft=((rows, tower.terms), F32),
        qe=((tower.terms, width), BF16),
        factor_out=((BOX, tower.mine, 128), BF16),
        t_met=((BOX, tower.mine, 128), BF16),
        s_met=((BOX, tower.mine, 128), BF16),
        h_normed=((batch, width), BF16),
        h_hidden=((batch, hidden), F32),
        h_active=((batch, hidden), BF16),
        h_hidden_low=((batch, hidden), BF16),
        h_unit=((batch, width), F32),
        h_inverse=((batch, 1), F32),
        h_final=((batch, width), BF16),
        h_scaling=((batch, 1), F32),
        h_direction=((batch, embed), F32),
        h_vectors=((batch, embed), BF16),
        h_raw=((batch, embed), BF16),
        h_grad=((batch, width), F32),
        h_middle_grad=((batch, width), F32),
    )


def step_on_box(images, captions, caption_ends, image_shards, caption_shards, logit_scale):
    image_in, caption_in = SimpleNamespace(**image_shards), SimpleNamespace(**caption_shards)
    image = Tower(True, *images.shape, image_in.expand.shape[1], images.shape[0])
    caption = Tower(False, *captions.shape, caption_in.expand.shape[1], 2 * captions.shape[0])
    both = image.width + caption.width
    count = Route.query_grads + 1
    shared = dict(
        vpack=((24, 128), F32),
        vall=((BOX * 24, 128), F32),
        middles=((BOX * 8, both), F32),
        queries=((BOX * 16, both // 2), BF16),
        query_grads=((BOX * 16, both // 2), BF16),
        squares=((8, 128), F32),
        squares_met=((BOX, 8, 128), F32),
        active=((image.rows, image.hidden), BF16),
        headmask=((128, image.width), F32),
        row_low=((image.batch, image.batch), BF16),
        column_low=((image.batch, image.batch), BF16),
        score_low=((image.rows, image.terms), BF16),
        soft_low=((image.rows, image.terms), BF16),
        wide_grad=((image.terms, image.width), BF16),
        placement=((image.rows, image.picks), F32),
        sib_attend=(image_in.attend.shape, BF16),
        sib_output=(image_in.output.shape, BF16),
        sib_projection=(image_in.projection.shape, BF16),
        sib_expand=(image_in.expand.shape, BF16),
    )
    semaphores = dict(near_sem=(count, 16), core_sem=(count,), send_sem=(count,), pair_sem=(2, 4), swap_sem=(2, 5))
    towers, shards = (image, caption), (image_shards, caption_shards)
    local = [tower_scratch(tower, image_in.projection.shape[1]) for tower in towers]

    def kernel(*refs):
        refs = iter(refs)

        def take(names):
            return SimpleNamespace(**{name: next(refs) for name in names})

        tokens = [next(refs), next(refs)]
        for tower in towers:
            tower.shards = take(NAMES)
        ends, logit_ref, out_loss, out_rms = [next(refs) for _ in range(4)]
        out_tokens = [next(refs), next(refs)]
        for tower in towers:
            tower.outs = take(NAMES)
        out_scale = next(refs)
        r = take(shared)
        for k, tower in enumerate(towers):
            tower.weights = take(MATRICES)
            tower.refs = take(local[k])
            tower.refs.tokens, tower.refs.out_tokens = tokens[k], out_tokens[k]
        for name in semaphores:
            setattr(r, name, next(refs))
        r.ends, r.logit_scale = ends, logit_ref
        r.out_loss, r.out_rms, r.out_scale = out_loss, out_rms, out_scale
        step_kernel(image, caption, r)

    scratch = [pltpu.VMEM(*spec) for spec in shared.values()]
    for own, specs in zip(shards, local):
        scratch += [pltpu.VMEM((BOX * own[name].shape[0], own[name].shape[1]), BF16) for name in MATRICES]
        scratch += [pltpu.VMEM(*spec) for spec in specs.values()]
    scratch += [pltpu.SemaphoreType.DMA(shape) for shape in semaphores.values()]
    weights = [own[name] for own in shards for name in NAMES]
    outputs = [((1,), F32), ((6,), F32), (images.shape, BF16), (captions.shape, BF16)]
    outputs += [(array.shape, F32) for array in weights] + [((1,), F32)]
    vmem, smem = pl.BlockSpec(memory_space=pltpu.VMEM), pl.BlockSpec(memory_space=pltpu.SMEM)
    return pl.pallas_call(
        kernel,
        out_shape=[jax.ShapeDtypeStruct(*spec) for spec in outputs],
        in_specs=[vmem] * (2 + len(weights)) + [smem] * 2,
        out_specs=[vmem] * len(outputs),
        scratch_shapes=scratch,
        compiler_params=pltpu.CompilerParams(
            collective_id=0, has_side_effects=True, vmem_limit_bytes=VMEM_LIMIT
        ),
        name="contrastive_step",
    )(images, captions, *weights, caption_ends, logit_scale)


def solution(mesh):
    rows, matrix, cube = P("dp"), P("dp", None), P("dp", None, None)
    weights = tuple(rows if name in VECTORS else matrix for name in NAMES)
    return jax.shard_map(
        per_device,
        mesh=mesh,
        in_specs=(cube, cube, matrix) + weights + weights + (P(),),
        out_specs=(P(), P(), cube, cube) + weights + weights + (P(),),
        check_vma=False,
    )
```

```python
from types import SimpleNamespace

import jax
import jax.numpy as jnp
from jax import lax
from jax.experimental import pallas as pl
from jax.experimental.pallas import tpu as pltpu
from jax.sharding import PartitionSpec as P

HD = 64
F32 = jnp.float32
BF16 = jnp.bfloat16


def product(left, right):
    return jnp.dot(left, right, preferred_element_type=F32)


def left_product(left, right):
    return lax.dot_general(left, right, (((0,), (0,)), ((), ())), preferred_element_type=F32)


def right_product(left, right):
    return lax.dot_general(left, right, (((1,), (1,)), ((), ())), preferred_element_type=F32)


def unit_norm(rows):
    centred = rows - jnp.mean(rows, -1, keepdims=True)
    inverse = lax.rsqrt(jnp.mean(centred * centred, -1, keepdims=True) + 1e-05)
    return centred * inverse, inverse


def norm_inward(upstream, unit_rows, inverse, gain):
    scaled = upstream * gain
    return inverse * (
        scaled
        - jnp.mean(scaled, -1, keepdims=True)
        - unit_rows * jnp.mean(scaled * unit_rows, -1, keepdims=True)
    )


def caption_allowed(end_rows, length):
    places = jnp.arange(length, dtype=jnp.int32)
    pieces = (places[None, :] >= end_rows[:, 0:1]).astype(jnp.int32) + (
        places[None, :] >= end_rows[:, 1:2]
    ).astype(jnp.int32)
    living = places[None, :] < end_rows[:, 1:2]
    same_piece = pieces[:, :, None] == pieces[:, None, :]
    causal = places[:, None] >= places[None, :]
    diagonal = places[:, None] == places[None, :]
    return same_piece & causal[None] & living[:, None, :] | diagonal[None]


def spread_heads(rows):
    count, width = rows.shape
    heads = width // HD
    head = jnp.arange(heads)[:, None, None]
    lane_head = jnp.arange(width)[None, None, :] // HD
    return jnp.where(head == lane_head, rows[None], jnp.zeros((), rows.dtype)).reshape(
        heads * count, width
    )


def fold_heads(rows, count):
    total, width = rows.shape
    heads = width // HD
    head = jnp.arange(heads)[:, None, None]
    lane_head = jnp.arange(width)[None, None, :] // HD
    return jnp.sum(jnp.where(head == lane_head, rows.reshape(heads, count, width), 0.0), 0)


def local_forward(inputs, allowed, mine, pick_rows, weights):
    sequences, length, width = inputs.shape
    heads = width // HD
    stream = inputs.reshape(sequences * length, width).astype(F32)
    unit_one, inverse_one = unit_norm(stream)
    normed = (unit_one * weights.norm_gain + weights.norm_bias).astype(BF16)
    bias = weights.attend_bias
    bias_full = jnp.concatenate([bias[:width], jnp.zeros((width,), F32), bias[width:]])
    mixed = (product(normed, weights.attend) + bias_full).astype(BF16)
    queries, keys, values = mixed[:, :width], mixed[:, width : 2 * width], mixed[:, 2 * width :]
    split = lambda rows: rows.reshape(sequences, length, heads, HD)
    scores = jnp.einsum("sqhd,skhd->shqk", split(queries), split(keys), preferred_element_type=F32)
    scores = scores / 8.0
    if allowed is not None:
        scores = jnp.where(allowed[:, None], scores, -1e30)
    softened = jax.nn.softmax(scores, axis=-1).astype(BF16)
    attended = jnp.einsum("shqk,skhd->sqhd", softened, split(values), preferred_element_type=F32)
    attended = attended.astype(BF16).reshape(sequences * length, width)
    branch = product(attended, weights.output) + weights.output_bias
    middle = stream + branch
    unit_two, _ = unit_norm(middle)
    normed_two = (unit_two * weights.second_gain + weights.second_bias).astype(BF16)
    hidden = product(normed_two, weights.expand) + weights.expand_bias
    active = (hidden * jax.nn.sigmoid(1.702 * hidden)).astype(BF16)
    second = product(active, weights.reduce) + weights.reduce_bias
    result = middle + second
    squares = jnp.stack([jnp.sum(branch * branch), jnp.sum(second * second), jnp.sum(result * result)])
    picked_queries = queries[pick_rows]
    picked_scores = right_product(keys, spread_heads(picked_queries)) / 8.0
    seen = jnp.tile(mine, (1, heads))
    picked_scores = jnp.where(seen, picked_scores, -1e30)
    soft = jax.nn.softmax(picked_scores, axis=0)
    return SimpleNamespace(
        squares=squares,
        unit_one=unit_one,
        inverse_one=inverse_one,
        normed=normed,
        keys=keys,
        values=values,
        soft=soft,
        value_factor=left_product(normed, soft.astype(BF16)).astype(BF16),
        middle_rows=middle[pick_rows],
        attended_rows=attended[pick_rows],
        normed_rows=normed[pick_rows],
        query_rows=picked_queries,
    )


def head_forward(middle, weights):
    unit_two, inverse_two = unit_norm(middle)
    normed_two = (unit_two * weights.second_gain + weights.second_bias).astype(BF16)
    hidden = product(normed_two, weights.expand) + weights.expand_bias
    active = (hidden * jax.nn.sigmoid(1.702 * hidden)).astype(BF16)
    result = middle + (product(active, weights.reduce) + weights.reduce_bias)
    unit_final, inverse_final = unit_norm(result)
    head_normed = (unit_final * weights.final_gain + weights.final_bias).astype(BF16)
    raw_embed = product(head_normed, weights.projection)
    scaling = lax.rsqrt(jnp.sum(raw_embed * raw_embed, -1, keepdims=True) + 1e-06)
    direction = raw_embed * scaling
    kept = (unit_two, inverse_two, normed_two, hidden, active, unit_final, inverse_final, head_normed)
    return direction.astype(BF16), direction, scaling, kept


def head_backward(upstream, direction, scaling, kept, weights):
    unit_two, inverse_two, normed_two, hidden, active, unit_final, inverse_final, head_normed = kept
    raw_low = (
        scaling * (upstream - direction * jnp.sum(upstream * direction, -1, keepdims=True))
    ).astype(BF16)
    head_grad = right_product(raw_low, weights.projection)
    result_grad = norm_inward(head_grad, unit_final, inverse_final, weights.final_gain)
    second_low = result_grad.astype(BF16)
    gate = jax.nn.sigmoid(1.702 * hidden)
    hidden_low = (
        right_product(second_low, weights.reduce) * (gate + 1.702 * hidden * gate * (1.0 - gate))
    ).astype(BF16)
    two_grad = right_product(hidden_low, weights.expand)
    middle_grad = result_grad + norm_inward(two_grad, unit_two, inverse_two, weights.second_gain)
    branch_low = middle_grad.astype(BF16)
    attended_grad = right_product(branch_low, weights.output).astype(BF16)
    sums = SimpleNamespace(
        final_gain=jnp.sum(head_grad * unit_final, 0),
        final_bias=jnp.sum(head_grad, 0),
        reduce_bias=jnp.sum(second_low.astype(F32), 0),
        expand_bias=jnp.sum(hidden_low.astype(F32), 0),
        second_gain=jnp.sum(two_grad * unit_two, 0),
        second_bias=jnp.sum(two_grad, 0),
        output_bias=jnp.sum(branch_low.astype(F32), 0),
    )
    factors = SimpleNamespace(
        projection=(head_normed, raw_low),
        reduce=(active, second_low),
        expand=(normed_two, hidden_low),
    )
    return middle_grad, branch_low, attended_grad, sums, factors


def local_backward(kept, mine, pick_rows, middle_grad_rows, attended_grad_rows, weights):
    width = weights.output.shape[0]
    count = pick_rows.shape[0]
    heads = width // HD
    wide_grad = spread_heads(attended_grad_rows)
    soft = kept.soft
    soft_grad = right_product(kept.values, wide_grad)
    score_low = (soft * (soft_grad - jnp.sum(soft_grad * soft, 0, keepdims=True))).astype(BF16)
    query_grad = (fold_heads(left_product(score_low, kept.keys), count) / 8.0).astype(BF16)
    key_factor = left_product(kept.normed, score_low).astype(BF16)
    attend = weights.attend
    key_side = right_product(spread_heads(kept.query_rows), attend[:, width : 2 * width]) / 8.0
    value_side = right_product(wide_grad, attend[:, 2 * width :])
    query_side = right_product(query_grad, attend[:, :width])
    normed_grad = product(score_low, key_side.astype(BF16)) + product(
        soft.astype(BF16), value_side.astype(BF16)
    )
    normed_grad = normed_grad.at[pick_rows].add(query_side)
    inward = norm_inward(normed_grad, kept.unit_one, kept.inverse_one, weights.norm_gain)
    input_grad = inward.at[pick_rows].add(middle_grad_rows)
    gain_grad = jnp.sum(normed_grad * kept.unit_one, 0)
    bias_grad = jnp.sum(normed_grad, 0)
    return input_grad, query_grad, key_factor, gain_grad, bias_grad


def my_columns(rows, size, index):
    return lax.dynamic_slice_in_dim(rows, index * size, size, rows.ndim - 1)


NAMES = (
    "norm_gain",
    "norm_bias",
    "attend",
    "attend_bias",
    "output",
    "output_bias",
    "second_gain",
    "second_bias",
    "expand",
    "expand_bias",
    "reduce",
    "reduce_bias",
    "final_gain",
    "final_bias",
    "projection",
)
VECTORS = tuple(name for name in NAMES if name[-4:] in ("bias", "gain"))


MATRICES = (NAMES[2], NAMES[4], NAMES[8], NAMES[10], NAMES[14])
PAIRED = (NAMES[2], NAMES[4], NAMES[8], NAMES[14])
VMEM_LIMIT = 65000 << 10


def gather(rows):
    return lax.all_gather(rows, "dp", axis=0, tiled=True)


def exchange(rows, devices):
    width, terms = rows.shape
    blocks = rows.reshape(devices, width // devices, terms)
    return lax.all_to_all(blocks, "dp", 0, 0)


def gather_weights(shards):
    devices = lax.axis_size("dp")
    whole = {}
    wide = PAIRED
    block = gather(jnp.concatenate([shards[name] for name in wide], 1))
    start = 0
    for name in wide:
        size = shards[name].shape[1]
        whole[name] = block[:, start : start + size]
        start += size
    whole[MATRICES[3]] = gather(shards[MATRICES[3]])
    flat = jnp.concatenate([shards[name] for name in VECTORS])
    flat = gather(flat[None].astype(F32))
    start = 0
    for name in VECTORS:
        size = shards[name].shape[0]
        whole[name] = flat[:, start : start + size].reshape(devices * size)
        start += size
    return SimpleNamespace(**whole)


def per_device(images, captions, caption_ends, *rest):
    image_shards = dict(zip(NAMES, rest[:15]))
    caption_shards = dict(zip(NAMES, rest[15:30]))
    logit_scale = rest[30]
    devices = lax.axis_size("dp")
    if (devices, images.shape, captions.shape) == (BOX, (8, 50, 768), (4, 77, 512)):
        return step_on_box(
            images, captions, caption_ends, image_shards, caption_shards, logit_scale
        )
    index = lax.axis_index("dp")
    image_weights = gather_weights(image_shards)
    caption_weights = gather_weights(caption_shards)
    image_count, patches, image_width = images.shape
    row_count, row_length, caption_width = captions.shape
    batch = devices * image_count

    image_tokens = jnp.arange(image_count * patches, dtype=jnp.int32)
    image_picks = jnp.arange(image_count, dtype=jnp.int32) * patches
    image_mine = image_tokens[:, None] // patches == jnp.arange(image_count)[None, :]
    image_kept = local_forward(images, None, image_mine, image_picks, image_weights)

    caption_tokens = jnp.arange(row_count * row_length, dtype=jnp.int32)[:, None]
    row_start = jnp.arange(row_count, dtype=jnp.int32)[:, None] * row_length
    caption_picks = (row_start + caption_ends - 1).reshape(row_count * 2)
    starts = row_start + jnp.concatenate([jnp.zeros((row_count, 1), jnp.int32), caption_ends[:, :1]], 1)
    caption_mine = (caption_tokens >= starts.reshape(1, -1)) & (caption_tokens <= caption_picks[None, :])
    allowed = caption_allowed(caption_ends, row_length)
    caption_kept = local_forward(captions, allowed, caption_mine, caption_picks, caption_weights)

    towers = (
        (image_kept, image_weights, image_mine, image_picks, image_count),
        (caption_kept, caption_weights, caption_mine, caption_picks, row_count * 2),
    )
    middle_all = gather(jnp.concatenate([image_kept.middle_rows, caption_kept.middle_rows], 1))
    low_rows = []
    for kept in (image_kept, caption_kept):
        low_rows += [kept.attended_rows, kept.normed_rows, kept.query_rows]
    low_all = gather(jnp.concatenate(low_rows, 1))
    widths = (image_width, caption_width)
    middles = (middle_all[:, :image_width], middle_all[:, image_width:])
    lows = []
    start = 0
    for width in widths:
        lows.append(tuple(low_all[:, start + j * width : start + (j + 1) * width] for j in range(3)))
        start += 3 * width

    image_vectors, image_direction, image_scaling, image_head = head_forward(middles[0], image_weights)
    caption_vectors, caption_direction, caption_scaling, caption_head = head_forward(
        middles[1], caption_weights
    )
    scale = jnp.exp(logit_scale[0])
    logits = scale * right_product(image_vectors, caption_vectors)
    places = jnp.arange(batch, dtype=jnp.int32)
    one_hot = (places[:, None] == places[None, :]).astype(F32)
    row_top = jnp.max(logits, 1, keepdims=True)
    row_lse = row_top + jnp.log(jnp.sum(jnp.exp(logits - row_top), 1, keepdims=True))
    col_top = jnp.max(logits, 0, keepdims=True)
    col_lse = col_top + jnp.log(jnp.sum(jnp.exp(logits - col_top), 0, keepdims=True))
    diagonal = jnp.sum(logits * one_hot)
    factor = 1.0 / (2.0 * batch)
    loss = (jnp.sum(row_lse) + jnp.sum(col_lse) - 2.0 * diagonal) * factor
    row_grad = (jnp.exp(logits - row_lse) - one_hot) * factor
    col_grad = (jnp.exp(logits - col_lse) - one_hot) * factor
    scale_grad = jnp.sum(row_grad * logits) + jnp.sum(col_grad * logits)
    row_low = (scale * row_grad).astype(BF16)
    col_low = (scale * col_grad).astype(BF16)
    image_vec_grad = product(row_low, caption_vectors) + product(col_low, caption_vectors)
    caption_vec_grad = left_product(col_low, image_vectors) + left_product(row_low, image_vectors)

    backs = (
        head_backward(image_vec_grad, image_direction, image_scaling, image_head, image_weights),
        head_backward(caption_vec_grad, caption_direction, caption_scaling, caption_head, caption_weights),
    )
    input_grads, query_grads, key_factors, norm_sums = [], [], [], []
    for (kept, weights, mine, picks, count), back in zip(towers, backs):
        mine_of = lambda rows: lax.dynamic_slice_in_dim(rows, index * count, count, 0)
        input_grad, query_grad, key_factor, gain_grad, bias_grad = local_backward(
            kept, mine, picks, mine_of(back[0]), mine_of(back[2]), weights
        )
        input_grads.append(input_grad)
        query_grads.append(query_grad)
        key_factors.append(key_factor)
        norm_sums.extend((gain_grad, bias_grad))

    query_all = gather(jnp.concatenate(query_grads, 1))
    query_all = (query_all[:, :image_width], query_all[:, image_width:])
    sums = jnp.concatenate([image_kept.squares, caption_kept.squares] + norm_sums)
    sums = lax.psum(sums, "dp")
    square_sums = sums[:6]
    norm_totals = []
    start = 6
    for width in (image_width, image_width, caption_width, caption_width):
        norm_totals.append(sums[start : start + width])
        start += width

    shards = []
    for tower in range(2):
        kept, weights, _, _, count = towers[tower]
        _, branch_low, attended_grad, head_sums, factors = backs[tower]
        width = widths[tower]
        size = width // devices
        heads = width // HD
        attended_all, normed_all, queries_all = lows[tower]
        columns = lambda rows: my_columns(rows, rows.shape[-1] // devices, index)
        query_block = left_product(columns(normed_all), query_all[tower])
        blocks = [query_block]
        for factor_rows, side in ((key_factors[tower], queries_all), (kept.value_factor, attended_grad)):
            met = exchange(factor_rows, devices).reshape(devices, size, heads, count)
            side = side.reshape(devices, count, heads, HD)
            blocks.append(
                jnp.einsum("sfhi,sihd->fhd", met, side, preferred_element_type=F32).reshape(size, width)
            )
        blocks[1] = blocks[1] / 8.0
        bias_wide = jnp.concatenate(
            [
                jnp.sum(query_all[tower].astype(F32), 0),
                jnp.sum(attended_grad.astype(F32), 0),
            ]
        )
        shards.extend(
            (
                columns(norm_totals[2 * tower]),
                columns(norm_totals[2 * tower + 1]),
                jnp.concatenate(blocks, 1),
                columns(bias_wide),
                left_product(columns(attended_all), branch_low),
                columns(head_sums.output_bias),
                columns(head_sums.second_gain),
                columns(head_sums.second_bias),
                left_product(columns(factors.expand[0]), factors.expand[1]),
                columns(head_sums.expand_bias),
                left_product(columns(factors.reduce[0]), factors.reduce[1]),
                columns(head_sums.reduce_bias),
                columns(head_sums.final_gain),
                columns(head_sums.final_bias),
                left_product(columns(factors.projection[0]), factors.projection[1]),
            )
        )
    image_cells = float(batch * patches * image_width)
    caption_cells = float(devices * row_count * row_length * caption_width)
    cells = jnp.array([image_cells] * 3 + [caption_cells] * 3, F32)
    return (
        loss.reshape(1),
        jnp.sqrt(square_sums / cells),
        input_grads[0].reshape(images.shape).astype(BF16),
        input_grads[1].reshape(captions.shape).astype(BF16),
        *shards,
        scale_grad.reshape(1),
    )


MESH = pl.DeviceIdType.MESH
BOX = 32


class Tower:
    def __init__(self, is_image, sequences, length, width, hidden, picks):
        self.is_image, self.sequences, self.length = is_image, sequences, length
        self.width, self.hidden = width, hidden
        self.heads = width // HD
        self.picks = picks
        self.tokens = sequences * length
        self.rows = -(-self.tokens // 80) * 80
        self.terms = self.heads * picks
        self.batch = BOX * picks
        self.mine = width // BOX
        self.vector_rows = (0, 8, 9) if is_image else (16, 10, 11)
        if is_image:
            self.window = 112
            self.windows = [(96 * j, 100 * j, 100 * j + 100) for j in range(sequences // 2)]
        else:
            self.window = 96
            self.windows = [
                (length * j // 16 * 16, length * j, length * (j + 1)) for j in range(sequences)
            ]


def iota(shape, axis):
    return lax.broadcasted_iota(jnp.int32, shape, axis)


def dot(left, right, over=((1,), (0,)), precision=None):
    return lax.dot_general(
        left, right, (over, ((), ())), preferred_element_type=F32, precision=precision
    )


ROWS_BY_COLUMNS = ((1,), (1,))
COLUMNS_BY_COLUMNS = ((0,), (0,))
HIGHEST = lax.Precision.HIGHEST


UNROLL = 1
LATE_EVERY = 2
LATE_FROM = 6


def loop(count, body):
    lax.fori_loop(0, count, lambda step, carry: (body(step), carry)[1], 0, unroll=min(count, UNROLL))


def rows_at(step, size):
    return pl.ds(pl.multiple_of(step * size, size), size)


def centred_unit(rows):
    width = rows.shape[-1]
    centred = rows - jnp.sum(rows, -1, keepdims=True) * (1.0 / width)
    inverse = lax.rsqrt(jnp.sum(centred * centred, -1, keepdims=True) * (1.0 / width) + 1e-05)
    return centred * inverse, inverse


def inward_of(upstream, unit_rows, inverse, gain):
    width = upstream.shape[-1]
    scaled = upstream * gain
    mean = jnp.sum(scaled, -1, keepdims=True) * (1.0 / width)
    slope = jnp.sum(scaled * unit_rows, -1, keepdims=True) * (1.0 / width)
    return inverse * (scaled - mean - unit_rows * slope)


def gate_of(hidden):
    return 0.5 * jnp.tanh(0.851 * hidden) + 0.5


def column_sum(rows):
    return jnp.sum(rows, 0, keepdims=True)


def spread_rows(rows, heads):
    lane_head = jnp.right_shift(iota(rows.shape, 1), 6)
    return jnp.concatenate([jnp.where(lane_head == h, rows, 0.0) for h in range(heads)], 0).astype(BF16)


def fold_rows(rows, heads, picks):
    lane_head = jnp.right_shift(iota((picks, rows.shape[1]), 1), 6)
    total = jnp.zeros((picks, rows.shape[1]), F32)
    for h in range(heads):
        total = total + jnp.where(lane_head == h, rows[h * picks : (h + 1) * picks], 0.0)
    return total


WIDTH_VECTORS = tuple(name for name in VECTORS if name not in (NAMES[3], NAMES[9]))


class Row:
    norm_gain, norm_bias, output_bias, second_gain, second_bias, reduce_bias, final_gain, final_bias = range(8)


class Places:
    def __init__(self):
        self.me = lax.axis_index("dp")
        self.core = lax.rem(self.me, 2)
        self.x = lax.rem(self.me // 2, 2)
        self.y = lax.rem(self.me // 4, 2)
        self.z = self.me // 8

    def device(self, ahead, across_y, across_x, other):
        z = lax.rem(self.z + ahead, 4)
        y = self.y + across_y - 2 * self.y * across_y
        x = self.x + across_x - 2 * self.x * across_x
        core = self.core + other - 2 * self.core * other
        return ((z * 2 + y) * 2 + x) * 2 + core


class Item:
    def __init__(self, target, size, mode, paired=False):
        self.target, self.size, self.mode, self.paired = target, size, mode, paired
        self.sent = 0


class Spread:
    def __init__(self, places, items, near_sem, core_sem, send_sem):
        self.places, self.items = places, items
        self.near_sem, self.core_sem, self.send_sem = near_sem, core_sem, send_sem
        self.x_next = places.device(0, 0, 1, 0)
        self.y_next = places.device(0, 1, 0, 0)
        self.sibling = places.device(0, 0, 0, 1)
        self.z_next = [None] + [places.device(step, 0, 0, 0) for step in (1, 2, 3)]

    def block(self, number, key):
        item = self.items[number]
        ahead, across_y, across_x = key
        owner = self.places.device((4 - ahead) % 4, across_y, across_x, 0)
        if item.paired:
            half = item.target.shape[1] // 2
            rows = pl.ds(pl.multiple_of((owner // 2) * (2 * item.size), 2 * item.size), 2 * item.size)
            return item.target.at[rows, pl.ds(pl.multiple_of(self.places.core * half, 128), half)]
        return item.target.at[pl.ds(pl.multiple_of(owner * item.size, item.size), item.size)]

    def send(self, number, key, device, sem):
        block = self.block(number, key)
        pltpu.make_async_remote_copy(
            src_ref=block,
            dst_ref=block,
            send_sem=self.send_sem.at[number],
            recv_sem=sem,
            device_id=(device,),
            device_id_type=MESH,
        ).start()
        self.items[number].sent += 1

    def near(self, number, key):
        ahead, across_y, across_x = key
        return self.near_sem.at[number, ahead * 4 + across_y * 2 + across_x]

    def forward(self, number, key):
        ahead, across_y, across_x = key
        item = self.items[number]
        if (across_y, across_x) == (0, 0):
            if ahead == 0:
                for step in (1, 2, 3):
                    self.send(number, key, self.z_next[step], self.near(number, (step, 0, 0)))
            self.send(number, key, self.x_next, self.near(number, (ahead, 0, 1)))
            self.send(number, key, self.y_next, self.near(number, (ahead, 1, 0)))
        elif (across_y, across_x) == (0, 1) and item.mode == "Y":
            self.send(number, key, self.y_next, self.near(number, (ahead, 1, 1)))
        elif (across_y, across_x) == (1, 0) and item.mode == "X":
            self.send(number, key, self.x_next, self.near(number, (ahead, 1, 1)))
        if not (item.paired and key == (0, 0, 0)):
            self.send(number, key, self.sibling, self.core_sem.at[number])

    def whole(self, ref, number, sem):
        return pltpu.make_async_remote_copy(
            src_ref=ref,
            dst_ref=ref,
            send_sem=self.send_sem.at[number],
            recv_sem=sem,
            device_id=(self.sibling,),
            device_id_type=MESH,
        )

    def start(self, number):
        self.forward(number, (0, 0, 0))

    def keys(self, stage):
        return (
            [(step, 0, 0) for step in (1, 2, 3)],
            [(step, *side) for step in range(4) for side in ((0, 1), (1, 0))],
            [(step, 1, 1) for step in range(4)],
        )[stage]

    def pass_on(self, number, key):
        self.whole(self.block(number, key), number, self.near(number, key)).wait_recv()
        self.forward(number, key)

    def wait(self, number):
        item = self.items[number]
        if item.paired:
            ref = item.target.at[pl.ds(0, 30 * item.size), pl.ds(0, item.target.shape[1] // 2)]
        else:
            ref = item.target.at[pl.ds(0, 16 * item.size)]
        self.whole(ref, number, self.core_sem.at[number]).wait_recv()

    def finish(self, number):
        item = self.items[number]
        ref = item.target.at[pl.ds(0, item.sent * item.size)]
        self.whole(ref, number, self.core_sem.at[number]).wait_send()


def fraction_floor(numbers, divisor):
    return jnp.floor((numbers.astype(F32) + 0.5) * (1.0 / divisor))


def columns_at(step, size):
    if isinstance(step, int):
        return slice(step * size, step * size + size)
    return pl.ds(pl.multiple_of(step * size, size), size)


class Step:
    def __init__(self, towers, r, places):
        self.towers, self.r, self.places = towers, r, places
        self.me = places.me

    def vector(self, tower, row):
        return tower.refs.vectors[row : row + 1, :]

    def pause(self, count=2):
        pass

    def paced(self, count, body, group=3):
        for first in range(0, count, group):
            loop(min(group, count - first), lambda step, first=first: body(first + step))
            self.pause()


    def pack_vectors(self):
        r = self.r
        pack = r.vpack
        pack[...] = jnp.zeros_like(pack)
        for tower in self.towers:
            first, attend_row, expand_row = tower.vector_rows
            shards = tower.shards
            rows = [(first + k, getattr(shards, name)) for k, name in enumerate(WIDTH_VECTORS)]
            for row, source in rows + [(attend_row, shards.attend_bias), (expand_row, shards.expand_bias)]:
                pack[row : row + 1, 0 : source.shape[0]] = source[...].astype(F32)[None, :]
        r.vall[pl.ds(pl.multiple_of(self.me * 24, 8), 24)] = pack[...]

    def place_own(self, shard, whole):
        size = shard.shape[0]
        whole[pl.ds(pl.multiple_of(self.me * size, size), size)] = shard[...]

    def join_pair(self, shard, other, whole):
        size = shard.shape[0]
        rows = pl.ds(pl.multiple_of((self.me // 2) * (2 * size), 2 * size), 2 * size)
        first = self.places.core == 0

        def body(step):
            columns = columns_at(step, 256)
            own, met = shard[:, columns].astype(F32), other[:, columns].astype(F32)
            both = jnp.concatenate([jnp.where(first, own, met), jnp.where(first, met, own)], 0)
            whole[rows, columns] = both.astype(BF16)

        loop(shard.shape[1] // 256, body)

    def unpack_vectors(self, tower):
        r = self.r
        first, attend_row, expand_row = tower.vector_rows
        width, hidden = tower.width, tower.hidden
        for row, size, target in (
            (first, width // BOX, tower.refs.vectors),
            (attend_row, 2 * width // BOX, tower.refs.attend_vector),
            (expand_row, hidden // BOX, tower.refs.expand_vector),
        ):
            group = row // 8 * 8
            blocks = r.vall[...].reshape(BOX, 24, 128)[:, group : group + 8, :]
            blocks = blocks.reshape(BOX * 8, 128).astype(BF16)
            chunk = 256

            def body(step, row=row, size=size, blocks=blocks, target=target):
                lane = iota((1, chunk), 1) + step * chunk
                owner = fraction_floor(lane, size)
                within = lane.astype(F32) - owner * size
                spread = (iota((128, chunk), 0).astype(F32) == within).astype(F32).astype(BF16)
                met = dot(blocks, spread).reshape(BOX, 8, chunk)
                device = iota((BOX, 8, chunk), 0).astype(F32)
                total = jnp.sum(jnp.where(device == owner.reshape(1, 1, chunk), met, 0.0), 0)
                if target is tower.refs.vectors:
                    target[:, columns_at(step, chunk)] = total
                else:
                    target[0:1, columns_at(step, chunk)] = total[row % 8 : row % 8 + 1]

            loop(target.shape[1] // chunk, body)
            self.pause()
        bias = tower.refs.mixed_bias
        bias[0:1, 0:width] = tower.refs.attend_vector[0:1, 0:width]
        bias[0:1, width : 2 * width] = jnp.zeros((1, width), F32)
        bias[0:1, 2 * width :] = tower.refs.attend_vector[0:1, width:]

    def load_tokens(self, tower):
        source, rows = tower.refs.tokens, tower.refs.x
        if tower.rows > tower.tokens:
            low = tower.tokens // 8 * 8
            rows[low:, :] = jnp.zeros((tower.rows - low, tower.width), F32)
        for number in range(tower.sequences):
            start = number * tower.length
            rows[start : start + tower.length, :] = source[:, number, :].astype(F32)

    def norm_tokens(self, tower, source, target, gain, bias):
        gain, bias = self.vector(tower, gain), self.vector(tower, bias)

        def body(step):
            rows = rows_at(step, 80)
            unit, _ = centred_unit(source[rows, :])
            target[rows, :] = (unit * gain + bias).astype(BF16)

        loop(tower.rows // 80, body)
        self.pause()


    def mix(self, tower):
        normed, mixed = tower.refs.normed, tower.refs.mixed
        weight, bias = tower.weights.attend, tower.refs.mixed_bias

        def body(step):
            columns = columns_at(step, 256)
            mixed[:, columns] = (dot(normed[...], weight[:, columns]) + bias[0:1, columns]).astype(BF16)

        self.paced(3 * tower.width // 256, body)

    def masks(self, tower):
        bias = tower.refs.mask
        side = tower.window
        query, key = iota((side, side), 0), iota((side, side), 1)
        for number, (row, _, _) in enumerate(tower.windows):
            if tower.is_image:
                allowed = fraction_floor(query + row, tower.length) == fraction_floor(
                    key + row, tower.length
                )
            else:
                first, second = self.r.ends[0, number], self.r.ends[1, number]
                query_place, key_place = [
                    place + (row - number * tower.length) for place in (query, key)
                ]

                def piece(place):
                    return jnp.where(place >= first, 1, 0) + jnp.where(place >= second, 1, 0)

                allowed = (
                    (piece(query_place) == piece(key_place))
                    & (query_place >= key_place)
                    & (key_place < second)
                    & (key_place >= 0)
                    & (query_place < tower.length)
                ) | (query == key)
            bias[number] = jnp.where(allowed, 0.0, -1e30)

    def attend(self, tower):
        width, side = tower.width, tower.window
        mixed, total, bias = tower.refs.mixed, tower.refs.att, tower.refs.mask
        total[...] = jnp.zeros_like(total)

        def body(step, windows):
            lane = iota((1, 128), 1)
            left = jnp.where(lane < HD, 1.0, 0.0)
            sides = (left.astype(BF16), (1.0 - left).astype(BF16))
            for number in windows:
                row, first, last = tower.windows[number]
                rows = slice(row, row + side)
                query, key, value = [
                    mixed[rows, columns_at(step + part * (width // 128), 128)] for part in range(3)
                ]
                out = []
                for half in sides:
                    scores = dot(query * half, key, ROWS_BY_COLUMNS) * 0.125 + bias[number]
                    weights = jnp.exp(scores - jnp.max(scores, -1, keepdims=True))
                    weights = weights * (1.0 / jnp.sum(weights, -1, keepdims=True))
                    out.append(dot(weights.astype(BF16), value))
                both = jnp.where(lane < HD, out[0], out[1])
                place = iota((side, 1), 0) + row
                kept = jnp.where((place >= first) & (place < last), 1.0, 0.0)
                columns = columns_at(step, 128)
                total[rows, columns] = total[rows, columns] + both * kept

        for pair in range(width // 128):
            for first in range(0, len(tower.windows), 2):
                body(pair, (first, first + 1))
                self.pause(3)
        low = tower.refs.attlow

        def narrow(step):
            low[rows_at(step, 80), :] = total[rows_at(step, 80), :].astype(BF16)

        loop(tower.rows // 80, narrow)

    def add_square(self, slot, rows, tower):
        if tower.rows > tower.tokens:
            rows = jnp.where(iota((rows.shape[0], 1), 0) < tower.tokens, rows, 0.0)
        squares = column_sum(rows * rows)
        width = squares.shape[1]
        folded = sum(squares[:, k * 128 : (k + 1) * 128] for k in range(width // 128))
        self.r.squares[slot : slot + 1, :] = self.r.squares[slot : slot + 1, :] + folded

    def project(self, tower):
        stream, middle, low = tower.refs.x, tower.refs.middle, tower.refs.attlow
        weight = tower.weights.output
        slot = 0 if tower.is_image else 3
        bias_row = Row.output_bias

        def body(step):
            columns = columns_at(step, 256)
            bias = tower.refs.vectors[bias_row : bias_row + 1, columns]
            branch = dot(low[...], weight[:, columns]) + bias
            middle[:, columns] = stream[:, columns] + branch
            self.add_square(slot, branch, tower)

        loop(tower.width // 256, body)
        self.pause()

    def own_active(self, tower):
        rows = slice(0, tower.rows)
        normed, active = tower.refs.normed_two, self.r.active
        weight, bias = tower.weights.expand, tower.refs.expand_vector

        def body(step):
            columns = columns_at(step, 256)
            hidden = dot(normed[...], weight[:, columns]) + bias[0:1, columns]
            active[rows, columns] = (hidden * gate_of(hidden)).astype(BF16)

        self.paced(tower.hidden // 256, body, 2)

    def own_second(self, tower):
        rows = slice(0, tower.rows)
        active, middle, weight = self.r.active, tower.refs.middle, tower.weights.reduce
        slot = 1 if tower.is_image else 4
        bias_row = Row.reduce_bias

        def body(step):
            columns = columns_at(step, 256)
            bias = tower.refs.vectors[bias_row : bias_row + 1, columns]
            second = dot(active[rows, 0 : tower.hidden], weight[:, columns]) + bias
            self.add_square(slot, second, tower)
            self.add_square(slot + 1, second + middle[:, columns], tower)

        self.paced(tower.width // 256, body, 1)


    def pick_places(self, tower):
        if tower.is_image:
            return [(i * tower.length, i * tower.length) for i in range(tower.picks)]
        places = []
        for i in range(tower.picks):
            start, ends = (i // 2) * tower.length, self.r.ends
            first = start + (ends[0, i // 2] if i % 2 else 0)
            places.append((first, start + ends[i % 2, i // 2] - 1))
        return places

    def selection(self, tower):
        row = iota((tower.picks, 1), 0)
        token = jnp.zeros((tower.picks, 1), jnp.int32)
        for i, (_, pick) in enumerate(self.pick_places(tower)):
            token = jnp.where(row == i, pick, token)
        return jnp.where(iota((tower.picks, tower.rows), 1) == token, 1.0, 0.0)

    def placement(self, tower):
        lane = iota((1, tower.picks), 1)
        token = jnp.zeros((1, tower.picks), jnp.int32)
        for i, (_, pick) in enumerate(self.pick_places(tower)):
            token = jnp.where(lane == i, pick, token)
        return jnp.where(iota((tower.rows, tower.picks), 0) == token, 1.0, 0.0)

    def picked_forward(self, tower):
        width, heads, terms, picks = tower.width, tower.heads, tower.terms, tower.picks
        select = self.selection(tower)
        low_select = select.astype(BF16)
        mixed, normed = tower.refs.mixed, tower.refs.normed
        queries = dot(low_select, mixed[:, 0:width])
        middle_rows = dot(select, tower.refs.middle[...], precision=HIGHEST)
        normed_rows = dot(low_select, normed[...])
        attended_rows = dot(low_select, tower.refs.attlow[...])
        wide = spread_rows(queries, heads)
        tower.refs.qe[...] = wide
        scores = dot(mixed[:, width : 2 * width], wide, ROWS_BY_COLUMNS) * 0.125
        lane = jnp.bitwise_and(iota((1, terms), 1), picks - 1)
        first = jnp.zeros((1, terms), jnp.int32)
        last = jnp.zeros((1, terms), jnp.int32)
        for i, (begin, pick) in enumerate(self.pick_places(tower)):
            first = jnp.where(lane == i, begin, first)
            last = jnp.where(lane == i, pick, last)
        if tower.is_image:
            last = first + (tower.length - 1)
        place = iota((tower.rows, terms), 0)
        scores = jnp.where((place >= first) & (place <= last), scores, -1e30)
        soft = jnp.exp(scores - jnp.max(scores, 0, keepdims=True))
        soft = soft * (1.0 / column_sum(soft))
        tower.refs.soft[...] = soft
        factor = dot(soft.astype(BF16), normed[...], COLUMNS_BY_COLUMNS)
        pad = jnp.zeros((128 - terms - 2 * picks, width), F32)
        rows = jnp.concatenate([factor, normed_rows, attended_rows, pad], 0)
        self.store_factor(tower, tower.refs.t_met, rows)
        return middle_rows, queries

    def store_factor(self, tower, met, rows):
        blocks = rows.T.reshape(BOX, tower.mine, 128).astype(BF16)
        tower.refs.factor_out[...] = blocks
        met[self.me] = tower.refs.factor_out[self.me]


    def head_middle(self, tower, rows):
        start = 0 if tower.is_image else self.towers[0].width
        return self.r.middles[rows, start : start + tower.width]

    def head_hidden(self, tower):
        normed = tower.refs.h_normed
        gain, bias = self.vector(tower, Row.second_gain), self.vector(tower, Row.second_bias)

        def norm(step):
            rows = rows_at(step, 64)
            unit, _ = centred_unit(self.head_middle(tower, rows))
            normed[rows, :] = (unit * gain + bias).astype(BF16)

        loop(tower.batch // 64, norm)
        weight, expand_bias = tower.weights.expand, tower.refs.expand_vector
        hidden_ref, active = tower.refs.h_hidden, tower.refs.h_active

        def body(step):
            columns = columns_at(step, 256)
            hidden = dot(normed[...], weight[:, columns]) + expand_bias[0:1, columns]
            hidden_ref[:, columns] = hidden
            active[:, columns] = (hidden * gate_of(hidden)).astype(BF16)

        self.paced(tower.hidden // 256, body, 3)

    def head_vectors(self, tower):
        result, active = tower.refs.h_unit, tower.refs.h_active
        weight = tower.weights.reduce
        bias_row = Row.reduce_bias
        start = 0 if tower.is_image else self.towers[0].width

        def body(step):
            columns = columns_at(step, 256)
            bias = tower.refs.vectors[bias_row : bias_row + 1, columns]
            middle = self.r.middles[:, pl.ds(pl.multiple_of(start + step * 256, 256), 256)]
            result[:, columns] = middle + (dot(active[...], weight[:, columns]) + bias)

        self.paced(tower.width // 256, body, 1)
        gain, bias = self.vector(tower, Row.final_gain), self.vector(tower, Row.final_bias)
        inverse_ref, normed = tower.refs.h_inverse, tower.refs.h_final

        def norm(step):
            rows = rows_at(step, 64)
            unit, inverse = centred_unit(result[rows, :])
            result[rows, :] = unit
            inverse_ref[rows, :] = inverse
            normed[rows, :] = (unit * gain + bias).astype(BF16)

        loop(tower.batch // 64, norm)
        self.pause()

        def embed(step):
            rows = rows_at(step, 64)
            raw = dot(normed[rows, :], tower.weights.projection[...])
            scaling = lax.rsqrt(jnp.sum(raw * raw, -1, keepdims=True) + 1e-06)
            direction = raw * scaling
            tower.refs.h_scaling[rows, :] = scaling
            tower.refs.h_direction[rows, :] = direction
            tower.refs.h_vectors[rows, :] = direction.astype(BF16)

        loop(tower.batch // 64, embed)

    def contrast(self):
        image, caption = self.towers
        batch = image.batch
        vectors, others = image.refs.h_vectors[...], caption.refs.h_vectors[...]
        scale = jnp.exp(jnp.full((1, 1), self.r.logit_scale[0], F32))
        logits = scale * dot(vectors, others, ROWS_BY_COLUMNS)
        same = jnp.where(iota((batch, batch), 0) == iota((batch, batch), 1), 1.0, 0.0)
        row_top = jnp.max(logits, 1, keepdims=True)
        row_lse = row_top + jnp.log(jnp.sum(jnp.exp(logits - row_top), 1, keepdims=True))
        column_top = jnp.max(logits, 0, keepdims=True)
        column_lse = column_top + jnp.log(column_sum(jnp.exp(logits - column_top)))

        def whole_sum(rows):
            return jnp.sum(column_sum(rows), 1, keepdims=True)

        factor = 1.0 / (2.0 * batch)
        loss = (
            whole_sum(row_lse) + whole_sum(column_lse) - 2.0 * whole_sum(logits * same)
        ) * factor
        row_grad = (jnp.exp(logits - row_lse) - same) * factor
        column_grad = (jnp.exp(logits - column_lse) - same) * factor
        scale_grad = whole_sum(row_grad * logits) + whole_sum(column_grad * logits)
        self.r.out_loss[...] = loss[0, :]
        self.r.out_scale[...] = scale_grad[0, :]
        row_low, column_low = self.r.row_low, self.r.column_low
        row_low[...] = (scale * row_grad).astype(BF16)
        column_low[...] = (scale * column_grad).astype(BF16)

        def image_side(step):
            rows = rows_at(step, 64)
            others = caption.refs.h_vectors[...]
            self.raw_grad(image, rows, dot(row_low[rows, :], others) + dot(column_low[rows, :], others))

        def caption_side(step):
            rows = rows_at(step, 128)
            others = image.refs.h_vectors[...]
            upstream = dot(column_low[:, rows], others, COLUMNS_BY_COLUMNS)
            upstream = upstream + dot(row_low[:, rows], others, COLUMNS_BY_COLUMNS)
            self.raw_grad(caption, rows, upstream)

        loop(batch // 64, image_side)
        loop(batch // 128, caption_side)

    def raw_grad(self, tower, rows, upstream):
        direction = tower.refs.h_direction[rows, :]
        along = jnp.sum(upstream * direction, -1, keepdims=True)
        raw = tower.refs.h_scaling[rows, :] * (upstream - direction * along)
        tower.refs.h_raw[rows, :] = raw.astype(BF16)

    def add_sum(self, tower, slot, row):
        sums = tower.refs.sums
        sums[slot : slot + 1, :] = sums[slot : slot + 1, :] + row

    def against(self, tower, source, weight, target):
        def body(step):
            target[:, columns_at(step, 256)] = dot(
                source[...], weight[rows_at(step, 256), :], ROWS_BY_COLUMNS
            )

        loop(tower.width // 256, body)

    def head_backward(self, tower):
        grad, result_grad = tower.refs.h_grad, tower.refs.h_middle_grad
        unit_ref, inverse_ref = tower.refs.h_unit, tower.refs.h_inverse
        second_low = tower.refs.h_second_low
        tower.refs.sums[...] = jnp.zeros_like(tower.refs.sums)
        self.against(tower, tower.refs.h_raw, tower.weights.projection, grad)
        gain = self.vector(tower, Row.final_gain)

        def final_norm(step):
            rows = rows_at(step, 64)
            upstream, unit = grad[rows, :], unit_ref[rows, :]
            inward = inward_of(upstream, unit, inverse_ref[rows, :], gain)
            low = inward.astype(BF16)
            result_grad[rows, :] = inward
            second_low[rows, :] = low
            self.add_sum(tower, Row.final_gain, column_sum(upstream * unit))
            self.add_sum(tower, Row.final_bias, column_sum(upstream))
            self.add_sum(tower, Row.reduce_bias, column_sum(low.astype(F32)))

        loop(tower.batch // 64, final_norm)
        weight, hidden_ref = tower.weights.reduce, tower.refs.h_hidden
        hidden_low, expand_sums = tower.refs.h_hidden_low, tower.refs.expand_sums

        def body(step):
            columns = columns_at(step, 256)
            active_grad = dot(second_low[...], weight[rows_at(step, 256), :], ROWS_BY_COLUMNS)
            hidden = hidden_ref[:, columns]
            gate = gate_of(hidden)
            low = (active_grad * (gate + 1.702 * hidden * gate * (1.0 - gate))).astype(BF16)
            hidden_low[:, columns] = low
            expand_sums[0:1, columns] = column_sum(low.astype(F32))

        loop(tower.hidden // 256, body)
        self.against(tower, hidden_low, tower.weights.expand, grad)
        second_gain, branch_low = self.vector(tower, Row.second_gain), tower.refs.h_branch_low

        def second_norm(step):
            rows = rows_at(step, 64)
            upstream = grad[rows, :]
            unit, inverse = centred_unit(self.head_middle(tower, rows))
            inward = result_grad[rows, :] + inward_of(upstream, unit, inverse, second_gain)
            low = inward.astype(BF16)
            result_grad[rows, :] = inward
            branch_low[rows, :] = low
            self.add_sum(tower, Row.second_gain, column_sum(upstream * unit))
            self.add_sum(tower, Row.second_bias, column_sum(upstream))
            self.add_sum(tower, Row.output_bias, column_sum(low.astype(F32)))

        loop(tower.batch // 64, second_norm)
        self.against(tower, branch_low, tower.weights.output, grad)

        def narrow(step):
            rows = rows_at(step, 64)
            low = grad[rows, :].astype(BF16).astype(F32)
            grad[rows, :] = low
            tower.refs.value_sums[0:1, :] = tower.refs.value_sums[0:1, :] + column_sum(low)

        tower.refs.value_sums[...] = jnp.zeros_like(tower.refs.value_sums)
        loop(tower.batch // 64, narrow)


    def local_backward(self, tower):
        width, heads, picks, terms = tower.width, tower.heads, tower.picks, tower.terms
        mine = pl.ds(pl.multiple_of(self.me * picks, picks), picks)
        wide_grad = spread_rows(tower.refs.h_grad[mine, :], heads)
        mixed, normed = tower.refs.mixed, tower.refs.normed
        soft = tower.refs.soft[...]
        soft_grad = dot(mixed[:, 2 * width :], wide_grad, ROWS_BY_COLUMNS)
        score_low = (soft * (soft_grad - column_sum(soft_grad * soft))).astype(BF16)
        query_grad = fold_rows(
            dot(score_low, mixed[:, width : 2 * width], COLUMNS_BY_COLUMNS), heads, picks
        )
        query_low = (query_grad * 0.125).astype(BF16)
        attend = tower.weights.attend
        scores_ref, soft_low, wide_ref = self.r.score_low, self.r.soft_low, self.r.wide_grad
        scores_ref[0 : tower.rows, 0:terms] = score_low
        soft_low[0 : tower.rows, 0:terms] = soft.astype(BF16)
        wide_ref[0:terms, 0:width] = wide_grad
        placement = self.r.placement
        placement[0 : tower.rows, :] = self.placement(tower)
        queries = tower.refs.qe

        def sides(step):
            rows = rows_at(step, 256)
            key_side = dot(queries[...], attend[rows, width : 2 * width], ROWS_BY_COLUMNS) * 0.125
            value_side = dot(wide_ref[0:terms, 0:width], attend[rows, 2 * width :], ROWS_BY_COLUMNS)
            query_side = dot(query_low, attend[rows, 0:width], ROWS_BY_COLUMNS)
            tower.refs.att[:, rows] = (
                dot(scores_ref[0 : tower.rows, 0:terms], key_side.astype(BF16))
                + dot(soft_low[0 : tower.rows, 0:terms], value_side.astype(BF16))
                + dot(placement[0 : tower.rows, :], query_side, precision=HIGHEST)
            )

        loop(width // 256, sides)
        key_factor = dot(score_low, normed[...], COLUMNS_BY_COLUMNS)
        gain = self.vector(tower, Row.norm_gain)
        source, grad = tower.refs.tokens, tower.refs.att
        sums = tower.refs.norm_sums
        sums[...] = jnp.zeros_like(sums)
        for number in range(tower.sequences):
            rows = slice(number * tower.length, (number + 1) * tower.length)
            upstream = grad[rows, :]
            unit, inverse = centred_unit(source[:, number, :].astype(F32))
            grad[rows, :] = inward_of(upstream, unit, inverse, gain)
            sums[0:1, :] = sums[0:1, :] + column_sum(upstream * unit)
            sums[1:2, :] = sums[1:2, :] + column_sum(upstream)
        pad = jnp.zeros((128 - terms - 8, width), F32)
        self.store_factor(tower, tower.refs.s_met, jnp.concatenate([key_factor, sums[...], pad], 0))
        return query_low.astype(F32)

    def input_gradient(self, tower):
        mine = pl.ds(pl.multiple_of(self.me * tower.picks, tower.picks), tower.picks)
        grad, out = tower.refs.att, tower.refs.out_tokens
        placement = self.r.placement
        placement[0 : tower.rows, :] = self.placement(tower)

        def add(step):
            columns = columns_at(step, 256)
            middle_grad = tower.refs.h_middle_grad[mine, columns]
            placed = dot(placement[0 : tower.rows, :], middle_grad, precision=HIGHEST)
            grad[:, columns] = grad[:, columns] + placed

        loop(tower.width // 256, add)
        for number in range(tower.sequences):
            start = number * tower.length
            out[:, number, :] = grad[start : start + tower.length, :].astype(BF16)


    def my_columns(self, total, size):
        return jnp.where(iota((size, total), 1) == iota((size, total), 0) + self.me * size, 1.0, 0.0)

    def turned_columns(self, source, size):
        pick = self.my_columns(source.shape[1], size).astype(BF16)
        return dot(pick, source[...], ROWS_BY_COLUMNS).astype(BF16)

    def gradient_blocks(self, left, right, out):
        step_size = 256

        def body(step):
            columns = columns_at(step, step_size)
            out[:, columns] = dot(left, right[:, columns])

        loop(right.shape[1] // step_size, body)

    def turn_head(self, tower):
        refs, size = tower.refs, tower.mine
        refs.turned_normed[...] = self.turned_columns(refs.h_normed, size)
        refs.turned_active[...] = self.turned_columns(refs.h_active, tower.hidden // BOX)
        refs.turned_final[...] = self.turned_columns(refs.h_final, size)

    def head_gradients(self, tower):
        size = tower.mine
        self.gradient_blocks(
            tower.refs.turned_final[...],
            tower.refs.h_raw,
            tower.outs.projection,
        )
        self.gradient_blocks(
            tower.refs.turned_active[...],
            tower.refs.h_second_low,
            tower.outs.reduce,
        )
        self.gradient_blocks(
            tower.refs.turned_normed[...],
            tower.refs.h_hidden_low,
            tower.outs.expand,
        )
        pick = self.my_columns(tower.width, size)
        sums = dot(tower.refs.sums[...], pick, ROWS_BY_COLUMNS, HIGHEST)
        for k, name in enumerate(WIDTH_VECTORS[2:], 2):
            getattr(tower.outs, name)[...] = sums[k, :]
        pick = self.my_columns(tower.hidden, tower.hidden // BOX)
        tower.outs.expand_bias[...] = dot(
            tower.refs.expand_sums[...], pick, ROWS_BY_COLUMNS, HIGHEST
        )[0, :]

    def regroup(self, tower, met):
        grouped, size = self.r.grouped, tower.mine
        lane = jnp.right_shift(iota((size, 128), 1), 3)
        for tile in range(BOX // 16):
            blocks = [met[tile * 16 + k].astype(F32) for k in range(16)]
            for span in (1, 2, 4, 8):
                low = jnp.bitwise_and(lane, span) == 0
                for k in range(16):
                    if k & span:
                        continue
                    first, second = blocks[k], blocks[k + span]
                    blocks[k] = jnp.where(low, first, pltpu.roll(second, 8 * span, 1))
                    blocks[k + span] = jnp.where(low, pltpu.roll(first, 128 - 8 * span, 1), second)
            for group, block in enumerate(blocks):
                start = (tile * 16 + group) * size
                grouped[start : start + size, :] = block

    def group_terms(self, tower, group, count=1):
        size, tiles = tower.mine, []
        for tile in range(BOX // 16):
            start = (tile * 16 + group) * size
            tiles.append(self.r.grouped[start : start + count * size, :])
        return jnp.concatenate(tiles, 1).astype(BF16)

    def output_gradient(self, tower):
        self.gradient_blocks(
            self.group_terms(tower, tower.heads + 1), tower.refs.h_branch_low, tower.outs.output
        )

    def factor_gradient(self, tower, side, part):
        size, width = tower.mine, tower.width
        left = self.group_terms(tower, 0, tower.heads)

        def body(step):
            columns = columns_at(step, 128)
            met = dot(left, side[:, columns].astype(BF16))
            lane = jnp.right_shift(iota((size, 128), 1), 6)
            total = jnp.zeros((size, 128), F32)
            for head in range(tower.heads):
                mine = lane + 2 * step == head
                total = total + jnp.where(mine, met[head * size : (head + 1) * size], 0.0)
            out = pl.ds(pl.multiple_of(part * width + step * 128, 128), 128)
            tower.outs.attend[:, out] = total

        loop(width // 128, body)

    def rows_of_pair(self, tower, ref, device):
        block = ref[pl.ds(pl.multiple_of(device * 16, 16), 16), :].astype(F32)
        rows = jnp.concatenate([block[0:8], block[8:16]], 1)
        start = 0 if tower.is_image else self.towers[0].width
        return rows[:, start : start + tower.width]

    def unpack_rows(self, tower, source, target, scale):
        for device in range(0, BOX, 2):
            pair = [self.rows_of_pair(tower, source, device + k) for k in range(2)]
            target[device * 8 : device * 8 + 16, :] = (jnp.concatenate(pair, 0) * scale).astype(BF16)

    def query_gradient(self, tower):
        r, size, width = self.r, tower.mine, tower.width
        rows = tower.refs.h_query_low
        self.unpack_rows(tower, r.query_grads, rows, 1.0)
        tower.outs.attend[:, 0:width] = dot(tower.refs.normed_terms[...], rows[...])
        bias = tower.refs.bias_sums
        bias[0:1, 0:width] = column_sum(rows[...].astype(F32))
        bias[0:1, width:] = tower.refs.value_sums[0:1, :]
        pick = self.my_columns(2 * width, 2 * size)
        tower.outs.attend_bias[...] = dot(bias[...], pick, ROWS_BY_COLUMNS, HIGHEST)[0, :]
        total = jnp.zeros((size, 128), F32)
        met = tower.refs.s_met
        for device in range(BOX):
            total = total + met[device].astype(F32)
        lane = iota((8, 128), 1)
        row = iota((8, 128), 0)
        pick = jnp.where(lane == row + tower.terms, 1.0, 0.0)
        sums = dot(pick, total, ROWS_BY_COLUMNS, HIGHEST)
        tower.outs.norm_gain[...] = sums[0, :]
        tower.outs.norm_bias[...] = sums[1, :]


class Route:
    (
        vectors,
        caption_attend,
        caption_output,
        image_attend,
        image_output,
        image_expand,
        image_projection,
        middles,
        queries,
        image_reduce,
        caption_projection,
        caption_expand,
        caption_reduce,
        query_grads,
    ) = range(14)


def swap_out(me, count, source_of, target, send_sem, recv_sem):
    def body(step):
        device = lax.rem(me + 1 + step, count)
        pltpu.make_async_remote_copy(
            src_ref=source_of(device),
            dst_ref=target.at[me],
            send_sem=send_sem,
            recv_sem=recv_sem,
            device_id=(device,),
            device_id_type=MESH,
        ).start()

    loop(count - 1, body)


def swap_descriptor(me, count, target, send_sem, recv_sem):
    most = target.at[pl.ds(0, count - 1)]
    return pltpu.make_async_remote_copy(
        src_ref=most,
        dst_ref=most,
        send_sem=send_sem,
        recv_sem=recv_sem,
        device_id=(lax.rem(me + 1, count),),
        device_id_type=MESH,
    )


def step_kernel(image, caption, r):
    for tower in (image, caption):
        refs, batch = tower.refs, tower.batch
        refs.middle = refs.x
        refs.normed_two = refs.mixed.at[:, 0 : tower.width]
        refs.h_branch_low = refs.attlow.at[0:batch]
        refs.h_second_low = refs.mixed.at[0:batch, 0 : tower.width]
        refs.h_query_low = refs.h_normed
        refs.h_queries = refs.attlow.at[0:batch]
        refs.h_direction = refs.h_grad.at[:, 0 : tower.weights.projection.shape[1]]
        refs.h_unit = refs.att.at[0:batch]
    r.grouped = r.vall
    places = Places()
    me = places.me
    step = Step((image, caption), r, places)
    routes = (
        (None, r.vall, 24, "X"),
        (caption.shards.attend, caption.weights.attend, 0, "X"),
        (caption.shards.output, caption.weights.output, 0, "Y"),
        (image.shards.attend, image.weights.attend, r.sib_attend, "Y"),
        (image.shards.output, image.weights.output, r.sib_output, "X"),
        (image.shards.expand, image.weights.expand, r.sib_expand, "X"),
        (image.shards.projection, image.weights.projection, r.sib_projection, "X"),
        (None, r.middles, 8, "Y"),
        (None, r.queries, 16, "X"),
        (image.shards.reduce, image.weights.reduce, 0, "Y"),
        (caption.shards.projection, caption.weights.projection, 0, "Y"),
        (caption.shards.expand, caption.weights.expand, 0, "Y"),
        (caption.shards.reduce, caption.weights.reduce, 0, "X"),
        (None, r.query_grads, 16, "X"),
    )
    items, pairs = [], {}
    for number, (shard, whole, other, mode) in enumerate(routes):
        if shard is None:
            items.append(Item(whole, other, mode))
            continue
        paired = not isinstance(other, int)
        if paired:
            pairs[number] = other
        items.append(Item(whole, shard.shape[0], mode, paired))
    spread = Spread(places, items, r.near_sem, r.core_sem, r.send_sem)

    barrier = pltpu.get_barrier_semaphore()
    loop(
        BOX - 1,
        lambda k: pl.semaphore_signal(
            barrier, inc=1, device_id=(lax.rem(me + 1 + k, BOX),), device_id_type=MESH
        ),
    )
    step.pack_vectors()
    pl.semaphore_wait(barrier, BOX - 1)

    pair_copies = {}
    for k, (number, other) in enumerate(pairs.items()):
        pair_copies[number] = pltpu.make_async_remote_copy(
            src_ref=routes[number][0],
            dst_ref=other,
            send_sem=r.pair_sem.at[0, k],
            recv_sem=r.pair_sem.at[1, k],
            device_id=(spread.sibling,),
            device_id_type=MESH,
        )
        pair_copies[number].start()
    for number, (shard, whole, other, _) in enumerate(routes):
        if number in pairs:
            pair_copies[number].wait()
            step.join_pair(shard, other, whole)
        elif shard is not None:
            step.place_own(shard, whole)
        if number == Route.vectors or shard is not None:
            spread.start(number)

    queue = []
    for turn in range(Route.query_grads + 2):
        for stage in range(3):
            if 0 <= turn - stage < Route.query_grads:
                queue += [(turn - stage, key) for key in spread.keys(stage)]

    held = [Route.middles, Route.queries]

    def serve(count=2):
        for _ in range(count):
            ready = [entry for entry in queue if entry[0] not in held]
            if ready:
                queue.remove(ready[0])
                spread.pass_on(*ready[0])

    def need(number):
        while any(entry[0] == number for entry in queue):
            serve(1)
        spread.wait(number)

    step.pause = serve
    serve(3)
    for work in (
        lambda: step.load_tokens(caption),
        lambda: step.load_tokens(image),
        lambda: step.masks(image),
        lambda: step.masks(caption),
    ):
        work()
        serve(3)
    r.squares[...] = jnp.zeros_like(r.squares)
    need(Route.vectors)
    for tower in (caption, image):
        step.unpack_vectors(tower)
        step.norm_tokens(tower, tower.refs.x, tower.refs.normed, Row.norm_gain, Row.norm_bias)
    need(Route.caption_attend)
    step.mix(caption)
    step.attend(caption)
    need(Route.caption_output)
    step.project(caption)
    need(Route.image_attend)
    step.mix(image)
    step.attend(image)
    need(Route.image_output)
    step.project(image)
    picked = []
    for tower in (image, caption):
        picked.append(step.picked_forward(tower))
        serve(3)
    mine = pl.ds(pl.multiple_of(me * 8, 8), 8)
    r.middles[mine, :] = jnp.concatenate([rows for rows, _ in picked], 1)
    queries = jnp.concatenate([rows for _, rows in picked], 1)
    half = queries.shape[1] // 2
    wide_mine = pl.ds(pl.multiple_of(me * 16, 16), 16)
    r.queries[wide_mine, :] = jnp.concatenate([queries[:, :half], queries[:, half:]], 0).astype(BF16)
    spread.start(Route.middles)
    rest = [entry for entry in queue if entry[0] not in held]
    late = [(Route.middles, key) for stage in range(3) for key in spread.keys(stage)]
    queue.clear()
    for place, entry in enumerate(rest):
        queue.append(entry)
        if place % LATE_EVERY == 0 and place >= LATE_FROM and late:
            queue.append(late.pop(0))
    queue += late
    held.clear()
    for tower in (image, caption):
        step.norm_tokens(
            tower, tower.refs.middle, tower.refs.normed_two, Row.second_gain, Row.second_bias
        )
    need(Route.image_expand)
    step.own_active(image)
    need(Route.middles)
    step.head_hidden(image)
    need(Route.image_reduce)
    need(Route.image_projection)
    step.head_vectors(image)
    step.turn_head(image)
    serve()
    step.own_second(image)
    need(Route.caption_expand)
    step.head_hidden(caption)
    step.own_active(caption)
    need(Route.caption_reduce)
    need(Route.caption_projection)
    spread.start(Route.queries)
    swap_sem = r.swap_sem
    for k, tower in enumerate((image, caption)):
        out, met = tower.refs.factor_out, tower.refs.t_met
        swap_out(me, BOX, lambda d, out=out: out.at[d], met, swap_sem.at[0, k], swap_sem.at[1, k])
    step.head_vectors(caption)
    queue += [(Route.queries, key) for stage in range(3) for key in spread.keys(stage)]
    step.pause = lambda count=2: None
    step.contrast()
    serve(3)
    step.head_backward(image)
    serve(8)
    step.head_backward(caption)
    serve(4)
    for k, tower in enumerate((image, caption)):
        swap_descriptor(me, BOX, tower.refs.t_met, swap_sem.at[0, k], swap_sem.at[1, k]).wait()
    queue += [(Route.query_grads, key) for stage in range(3) for key in spread.keys(stage)]
    grads = jnp.concatenate([step.local_backward(tower) for tower in (image, caption)], 1)
    r.query_grads[wide_mine, :] = jnp.concatenate([grads[:, :half], grads[:, half:]], 0).astype(BF16)
    spread.start(Route.query_grads)
    for k, tower in enumerate((image, caption), 2):
        out, met = tower.refs.factor_out, tower.refs.s_met
        swap_out(me, BOX, lambda d, out=out: out.at[d], met, swap_sem.at[0, k], swap_sem.at[1, k])
    step.own_second(caption)
    serve(3)
    squares = r.squares
    r.squares_met[me] = squares[...]
    swap_out(me, BOX, lambda d: squares, r.squares_met, swap_sem.at[0, 4], swap_sem.at[1, 4])
    step.turn_head(caption)
    step.head_gradients(caption)
    serve(8)
    step.head_gradients(image)
    serve(4)
    spread.wait(Route.queries)
    spread.finish(Route.vectors)
    for tower in (image, caption):
        refs = tower.refs
        step.input_gradient(tower)
        step.regroup(tower, refs.t_met)
        step.output_gradient(tower)
        refs.normed_terms[...] = step.group_terms(tower, tower.heads)
        step.factor_gradient(tower, refs.h_grad, 2)
        step.unpack_rows(tower, r.queries, refs.h_queries, 0.125)
    for k, tower in enumerate((image, caption), 2):
        swap_descriptor(me, BOX, tower.refs.s_met, swap_sem.at[0, k], swap_sem.at[1, k]).wait()
    for tower in (image, caption):
        step.regroup(tower, tower.refs.s_met)
        step.factor_gradient(tower, tower.refs.h_queries, 1)
    spread.wait(Route.query_grads)
    for tower in (image, caption):
        step.query_gradient(tower)
    swap_descriptor(me, BOX, r.squares_met, swap_sem.at[0, 4], swap_sem.at[1, 4]).wait()
    totals = jnp.sum(r.squares_met[...], 0)
    slot = iota((8, 128), 0)
    cells = jnp.where(
        slot < 3,
        1.0 / (BOX * image.tokens * image.width),
        1.0 / (BOX * caption.tokens * caption.width),
    )
    means = jnp.sqrt(jnp.sum(totals, 1, keepdims=True) * cells)
    diagonal = jnp.where(slot == iota((8, 128), 1), means, 0.0)
    r.out_rms[...] = column_sum(diagonal)[0, :6]
    for number in range(1, len(items)):
        spread.finish(number)


def tower_scratch(tower, embed):
    width, hidden, rows, batch = tower.width, tower.hidden, tower.rows, tower.batch
    return dict(
        vectors=((8, width), F32),
        attend_vector=((8, 2 * width), F32),
        expand_vector=((8, hidden), F32),
        mixed_bias=((8, 3 * width), F32),
        sums=((8, width), F32),
        value_sums=((8, width), F32),
        norm_sums=((8, width), F32),
        bias_sums=((8, 2 * width), F32),
        expand_sums=((8, hidden), F32),
        x=((rows, width), F32),
        normed=((rows, width), BF16),
        mixed=((rows, 3 * width), BF16),
        att=((rows, width), F32),
        attlow=((rows, width), BF16),
        mask=((len(tower.windows), tower.window, tower.window), F32),
        soft=((rows, tower.terms), F32),
        qe=((tower.terms, width), BF16),
        factor_out=((BOX, tower.mine, 128), BF16),
        t_met=((BOX, tower.mine, 128), BF16),
        s_met=((BOX, tower.mine, 128), BF16),
        normed_terms=((tower.mine, batch), BF16),
        turned_final=((tower.mine, batch), BF16),
        turned_normed=((tower.mine, batch), BF16),
        turned_active=((hidden // BOX, batch), BF16),
        h_normed=((batch, width), BF16),
        h_hidden=((batch, hidden), F32),
        h_active=((batch, hidden), BF16),
        h_hidden_low=((batch, hidden), BF16),
        h_inverse=((batch, 1), F32),
        h_final=((batch, width), BF16),
        h_scaling=((batch, 1), F32),
        h_vectors=((batch, embed), BF16),
        h_raw=((batch, embed), BF16),
        h_grad=((batch, width), F32),
        h_middle_grad=((batch, width), F32),
    )


def step_on_box(images, captions, caption_ends, image_shards, caption_shards, logit_scale):
    image_in, caption_in = SimpleNamespace(**image_shards), SimpleNamespace(**caption_shards)
    image = Tower(True, *images.shape, image_in.expand.shape[1], images.shape[0])
    caption = Tower(False, *captions.shape, caption_in.expand.shape[1], 2 * captions.shape[0])
    both = image.width + caption.width
    count = Route.query_grads + 1
    shared = dict(
        vpack=((24, 128), F32),
        vall=((BOX * 24, 128), F32),
        middles=((BOX * 8, both), F32),
        queries=((BOX * 16, both // 2), BF16),
        query_grads=((BOX * 16, both // 2), BF16),
        squares=((8, 128), F32),
        squares_met=((BOX, 8, 128), F32),
        active=((image.rows, image.hidden), BF16),
        row_low=((image.batch, image.batch), BF16),
        column_low=((image.batch, image.batch), BF16),
        score_low=((image.rows, image.terms), BF16),
        soft_low=((image.rows, image.terms), BF16),
        wide_grad=((image.terms, image.width), BF16),
        placement=((image.rows, image.picks), F32),
        sib_attend=(image_in.attend.shape, BF16),
        sib_output=(image_in.output.shape, BF16),
        sib_projection=(image_in.projection.shape, BF16),
        sib_expand=(image_in.expand.shape, BF16),
    )
    semaphores = dict(near_sem=(count, 16), core_sem=(count,), send_sem=(count,), pair_sem=(2, 4), swap_sem=(2, 5))
    towers, shards = (image, caption), (image_shards, caption_shards)
    local = [tower_scratch(tower, image_in.projection.shape[1]) for tower in towers]

    def kernel(*refs):
        refs = iter(refs)

        def take(names):
            return SimpleNamespace(**{name: next(refs) for name in names})

        tokens = [next(refs), next(refs)]
        for tower in towers:
            tower.shards = take(NAMES)
        ends, logit_ref, out_loss, out_rms = [next(refs) for _ in range(4)]
        out_tokens = [next(refs), next(refs)]
        for tower in towers:
            tower.outs = take(NAMES)
        out_scale = next(refs)
        r = take(shared)
        for k, tower in enumerate(towers):
            tower.weights = take(MATRICES)
            tower.refs = take(local[k])
            tower.refs.tokens, tower.refs.out_tokens = tokens[k], out_tokens[k]
        for name in semaphores:
            setattr(r, name, next(refs))
        r.ends, r.logit_scale = ends, logit_ref
        r.out_loss, r.out_rms, r.out_scale = out_loss, out_rms, out_scale
        step_kernel(image, caption, r)

    scratch = [pltpu.VMEM(*spec) for spec in shared.values()]
    for own, specs in zip(shards, local):
        scratch += [pltpu.VMEM((BOX * own[name].shape[0], own[name].shape[1]), BF16) for name in MATRICES]
        scratch += [pltpu.VMEM(*spec) for spec in specs.values()]
    scratch += [pltpu.SemaphoreType.DMA(shape) for shape in semaphores.values()]
    weights = [own[name] for own in shards for name in NAMES]
    tokens = [jnp.swapaxes(images, 0, 1), jnp.swapaxes(captions, 0, 1)]
    outputs = [((1,), F32), ((6,), F32)] + [(array.shape, BF16) for array in tokens]
    outputs += [(array.shape, F32) for array in weights] + [((1,), F32)]
    vmem, smem = pl.BlockSpec(memory_space=pltpu.VMEM), pl.BlockSpec(memory_space=pltpu.SMEM)
    shapes = [jax.ShapeDtypeStruct(*spec) for spec in outputs]
    results = pl.pallas_call(
        kernel,
        out_shape=shapes,
        in_specs=[vmem] * (2 + len(weights)) + [smem] * 2,
        out_specs=[vmem] * len(outputs),
        scratch_shapes=scratch,
        compiler_params=pltpu.CompilerParams(
            collective_id=0, has_side_effects=True, vmem_limit_bytes=VMEM_LIMIT
        ),
        name="contrastive_step",
    )(*tokens, *weights, caption_ends.T, logit_scale)

    def hand_over(*refs):
        sems = refs[-1]
        pairs = zip(refs[: len(shapes)], refs[len(shapes) : -1])
        copies = [pltpu.make_async_copy(*pair, sems.at[k]) for k, pair in enumerate(pairs)]
        for copy in copies:
            copy.start()
        for copy in copies:
            copy.wait()

    anywhere = pl.BlockSpec(memory_space=pl.ANY)
    results = pl.pallas_call(
        hand_over,
        out_shape=shapes,
        in_specs=[anywhere] * len(shapes),
        out_specs=[vmem] * len(shapes),
        scratch_shapes=[pltpu.SemaphoreType.DMA((len(shapes),))],
        compiler_params=pltpu.CompilerParams(vmem_limit_bytes=VMEM_LIMIT),
        name="hand_over",
    )(*results)
    tokens = [jnp.swapaxes(rows, 0, 1) for rows in results[2:4]]
    return (*results[:2], *tokens, *results[4:])


def solution(mesh):
    rows, matrix, cube = P("dp"), P("dp", None), P("dp", None, None)
    weights = tuple(rows if name in VECTORS else matrix for name in NAMES)
    return jax.shard_map(
        per_device,
        mesh=mesh,
        in_specs=(cube, cube, matrix) + weights + weights + (P(),),
        out_specs=(P(), P(), cube, cube) + weights + weights + (P(),),
        check_vma=False,
    )
```

```python
from types import SimpleNamespace

import jax
import jax.numpy as jnp
from jax import lax
from jax.experimental import pallas as pl
from jax.experimental.pallas import tpu as pltpu
from jax.sharding import PartitionSpec as P

HD = 64
F32 = jnp.float32
BF16 = jnp.bfloat16


def product(left, right):
    return jnp.dot(left, right, preferred_element_type=F32)


def left_product(left, right):
    return lax.dot_general(left, right, (((0,), (0,)), ((), ())), preferred_element_type=F32)


def right_product(left, right):
    return lax.dot_general(left, right, (((1,), (1,)), ((), ())), preferred_element_type=F32)


def unit_norm(rows):
    centred = rows - jnp.mean(rows, -1, keepdims=True)
    inverse = lax.rsqrt(jnp.mean(centred * centred, -1, keepdims=True) + 1e-05)
    return centred * inverse, inverse


def norm_inward(upstream, unit_rows, inverse, gain):
    scaled = upstream * gain
    return inverse * (
        scaled
        - jnp.mean(scaled, -1, keepdims=True)
        - unit_rows * jnp.mean(scaled * unit_rows, -1, keepdims=True)
    )


def caption_allowed(end_rows, length):
    places = jnp.arange(length, dtype=jnp.int32)
    pieces = (places[None, :] >= end_rows[:, 0:1]).astype(jnp.int32) + (
        places[None, :] >= end_rows[:, 1:2]
    ).astype(jnp.int32)
    living = places[None, :] < end_rows[:, 1:2]
    same_piece = pieces[:, :, None] == pieces[:, None, :]
    causal = places[:, None] >= places[None, :]
    diagonal = places[:, None] == places[None, :]
    return same_piece & causal[None] & living[:, None, :] | diagonal[None]


def spread_heads(rows):
    count, width = rows.shape
    heads = width // HD
    head = jnp.arange(heads)[:, None, None]
    lane_head = jnp.arange(width)[None, None, :] // HD
    return jnp.where(head == lane_head, rows[None], jnp.zeros((), rows.dtype)).reshape(
        heads * count, width
    )


def fold_heads(rows, count):
    total, width = rows.shape
    heads = width // HD
    head = jnp.arange(heads)[:, None, None]
    lane_head = jnp.arange(width)[None, None, :] // HD
    return jnp.sum(jnp.where(head == lane_head, rows.reshape(heads, count, width), 0.0), 0)


def local_forward(inputs, allowed, mine, pick_rows, weights):
    sequences, length, width = inputs.shape
    heads = width // HD
    stream = inputs.reshape(sequences * length, width).astype(F32)
    unit_one, inverse_one = unit_norm(stream)
    normed = (unit_one * weights.norm_gain + weights.norm_bias).astype(BF16)
    bias = weights.attend_bias
    bias_full = jnp.concatenate([bias[:width], jnp.zeros((width,), F32), bias[width:]])
    mixed = (product(normed, weights.attend) + bias_full).astype(BF16)
    queries, keys, values = mixed[:, :width], mixed[:, width : 2 * width], mixed[:, 2 * width :]
    split = lambda rows: rows.reshape(sequences, length, heads, HD)
    scores = jnp.einsum("sqhd,skhd->shqk", split(queries), split(keys), preferred_element_type=F32)
    scores = scores / 8.0
    if allowed is not None:
        scores = jnp.where(allowed[:, None], scores, -1e30)
    softened = jax.nn.softmax(scores, axis=-1).astype(BF16)
    attended = jnp.einsum("shqk,skhd->sqhd", softened, split(values), preferred_element_type=F32)
    attended = attended.astype(BF16).reshape(sequences * length, width)
    branch = product(attended, weights.output) + weights.output_bias
    middle = stream + branch
    unit_two, _ = unit_norm(middle)
    normed_two = (unit_two * weights.second_gain + weights.second_bias).astype(BF16)
    hidden = product(normed_two, weights.expand) + weights.expand_bias
    active = (hidden * jax.nn.sigmoid(1.702 * hidden)).astype(BF16)
    second = product(active, weights.reduce) + weights.reduce_bias
    result = middle + second
    squares = jnp.stack([jnp.sum(branch * branch), jnp.sum(second * second), jnp.sum(result * result)])
    picked_queries = queries[pick_rows]
    picked_scores = right_product(keys, spread_heads(picked_queries)) / 8.0
    seen = jnp.tile(mine, (1, heads))
    picked_scores = jnp.where(seen, picked_scores, -1e30)
    soft = jax.nn.softmax(picked_scores, axis=0)
    return SimpleNamespace(
        squares=squares,
        unit_one=unit_one,
        inverse_one=inverse_one,
        normed=normed,
        keys=keys,
        values=values,
        soft=soft,
        value_factor=left_product(normed, soft.astype(BF16)).astype(BF16),
        middle_rows=middle[pick_rows],
        attended_rows=attended[pick_rows],
        normed_rows=normed[pick_rows],
        query_rows=picked_queries,
    )


def head_forward(middle, weights):
    unit_two, inverse_two = unit_norm(middle)
    normed_two = (unit_two * weights.second_gain + weights.second_bias).astype(BF16)
    hidden = product(normed_two, weights.expand) + weights.expand_bias
    active = (hidden * jax.nn.sigmoid(1.702 * hidden)).astype(BF16)
    result = middle + (product(active, weights.reduce) + weights.reduce_bias)
    unit_final, inverse_final = unit_norm(result)
    head_normed = (unit_final * weights.final_gain + weights.final_bias).astype(BF16)
    raw_embed = product(head_normed, weights.projection)
    scaling = lax.rsqrt(jnp.sum(raw_embed * raw_embed, -1, keepdims=True) + 1e-06)
    direction = raw_embed * scaling
    kept = (unit_two, inverse_two, normed_two, hidden, active, unit_final, inverse_final, head_normed)
    return direction.astype(BF16), direction, scaling, kept


def head_backward(upstream, direction, scaling, kept, weights):
    unit_two, inverse_two, normed_two, hidden, active, unit_final, inverse_final, head_normed = kept
    raw_low = (
        scaling * (upstream - direction * jnp.sum(upstream * direction, -1, keepdims=True))
    ).astype(BF16)
    head_grad = right_product(raw_low, weights.projection)
    result_grad = norm_inward(head_grad, unit_final, inverse_final, weights.final_gain)
    second_low = result_grad.astype(BF16)
    gate = jax.nn.sigmoid(1.702 * hidden)
    hidden_low = (
        right_product(second_low, weights.reduce) * (gate + 1.702 * hidden * gate * (1.0 - gate))
    ).astype(BF16)
    two_grad = right_product(hidden_low, weights.expand)
    middle_grad = result_grad + norm_inward(two_grad, unit_two, inverse_two, weights.second_gain)
    branch_low = middle_grad.astype(BF16)
    attended_grad = right_product(branch_low, weights.output).astype(BF16)
    sums = SimpleNamespace(
        final_gain=jnp.sum(head_grad * unit_final, 0),
        final_bias=jnp.sum(head_grad, 0),
        reduce_bias=jnp.sum(second_low.astype(F32), 0),
        expand_bias=jnp.sum(hidden_low.astype(F32), 0),
        second_gain=jnp.sum(two_grad * unit_two, 0),
        second_bias=jnp.sum(two_grad, 0),
        output_bias=jnp.sum(branch_low.astype(F32), 0),
    )
    factors = SimpleNamespace(
        projection=(head_normed, raw_low),
        reduce=(active, second_low),
        expand=(normed_two, hidden_low),
    )
    return middle_grad, branch_low, attended_grad, sums, factors


def local_backward(kept, mine, pick_rows, middle_grad_rows, attended_grad_rows, weights):
    width = weights.output.shape[0]
    count = pick_rows.shape[0]
    heads = width // HD
    wide_grad = spread_heads(attended_grad_rows)
    soft = kept.soft
    soft_grad = right_product(kept.values, wide_grad)
    score_low = (soft * (soft_grad - jnp.sum(soft_grad * soft, 0, keepdims=True))).astype(BF16)
    query_grad = (fold_heads(left_product(score_low, kept.keys), count) / 8.0).astype(BF16)
    key_factor = left_product(kept.normed, score_low).astype(BF16)
    attend = weights.attend
    key_side = right_product(spread_heads(kept.query_rows), attend[:, width : 2 * width]) / 8.0
    value_side = right_product(wide_grad, attend[:, 2 * width :])
    query_side = right_product(query_grad, attend[:, :width])
    normed_grad = product(score_low, key_side.astype(BF16)) + product(
        soft.astype(BF16), value_side.astype(BF16)
    )
    normed_grad = normed_grad.at[pick_rows].add(query_side)
    inward = norm_inward(normed_grad, kept.unit_one, kept.inverse_one, weights.norm_gain)
    input_grad = inward.at[pick_rows].add(middle_grad_rows)
    gain_grad = jnp.sum(normed_grad * kept.unit_one, 0)
    bias_grad = jnp.sum(normed_grad, 0)
    return input_grad, query_grad, key_factor, gain_grad, bias_grad


def my_columns(rows, size, index):
    return lax.dynamic_slice_in_dim(rows, index * size, size, rows.ndim - 1)


NAMES = (
    "norm_gain",
    "norm_bias",
    "attend",
    "attend_bias",
    "output",
    "output_bias",
    "second_gain",
    "second_bias",
    "expand",
    "expand_bias",
    "reduce",
    "reduce_bias",
    "final_gain",
    "final_bias",
    "projection",
)
VECTORS = tuple(name for name in NAMES if name[-4:] in ("bias", "gain"))


MATRICES = (NAMES[2], NAMES[4], NAMES[8], NAMES[10], NAMES[14])
PAIRED = (NAMES[2], NAMES[4], NAMES[8], NAMES[14])
VMEM_LIMIT = 65000 << 10


def gather(rows):
    return lax.all_gather(rows, "dp", axis=0, tiled=True)


def exchange(rows, devices):
    width, terms = rows.shape
    blocks = rows.reshape(devices, width // devices, terms)
    return lax.all_to_all(blocks, "dp", 0, 0)


def gather_weights(shards):
    devices = lax.axis_size("dp")
    whole = {}
    wide = PAIRED
    block = gather(jnp.concatenate([shards[name] for name in wide], 1))
    start = 0
    for name in wide:
        size = shards[name].shape[1]
        whole[name] = block[:, start : start + size]
        start += size
    whole[MATRICES[3]] = gather(shards[MATRICES[3]])
    flat = jnp.concatenate([shards[name] for name in VECTORS])
    flat = gather(flat[None].astype(F32))
    start = 0
    for name in VECTORS:
        size = shards[name].shape[0]
        whole[name] = flat[:, start : start + size].reshape(devices * size)
        start += size
    return SimpleNamespace(**whole)


def per_device(images, captions, caption_ends, *rest):
    image_shards = dict(zip(NAMES, rest[:15]))
    caption_shards = dict(zip(NAMES, rest[15:30]))
    logit_scale = rest[30]
    devices = lax.axis_size("dp")
    if (devices, images.shape, captions.shape) == (BOX, (8, 50, 768), (4, 77, 512)):
        return step_on_box(
            images, captions, caption_ends, image_shards, caption_shards, logit_scale
        )
    index = lax.axis_index("dp")
    image_weights = gather_weights(image_shards)
    caption_weights = gather_weights(caption_shards)
    image_count, patches, image_width = images.shape
    row_count, row_length, caption_width = captions.shape
    batch = devices * image_count

    image_tokens = jnp.arange(image_count * patches, dtype=jnp.int32)
    image_picks = jnp.arange(image_count, dtype=jnp.int32) * patches
    image_mine = image_tokens[:, None] // patches == jnp.arange(image_count)[None, :]
    image_kept = local_forward(images, None, image_mine, image_picks, image_weights)

    caption_tokens = jnp.arange(row_count * row_length, dtype=jnp.int32)[:, None]
    row_start = jnp.arange(row_count, dtype=jnp.int32)[:, None] * row_length
    caption_picks = (row_start + caption_ends - 1).reshape(row_count * 2)
    starts = row_start + jnp.concatenate([jnp.zeros((row_count, 1), jnp.int32), caption_ends[:, :1]], 1)
    caption_mine = (caption_tokens >= starts.reshape(1, -1)) & (caption_tokens <= caption_picks[None, :])
    allowed = caption_allowed(caption_ends, row_length)
    caption_kept = local_forward(captions, allowed, caption_mine, caption_picks, caption_weights)

    towers = (
        (image_kept, image_weights, image_mine, image_picks, image_count),
        (caption_kept, caption_weights, caption_mine, caption_picks, row_count * 2),
    )
    middle_all = gather(jnp.concatenate([image_kept.middle_rows, caption_kept.middle_rows], 1))
    low_rows = []
    for kept in (image_kept, caption_kept):
        low_rows += [kept.attended_rows, kept.normed_rows, kept.query_rows]
    low_all = gather(jnp.concatenate(low_rows, 1))
    widths = (image_width, caption_width)
    middles = (middle_all[:, :image_width], middle_all[:, image_width:])
    lows = []
    start = 0
    for width in widths:
        lows.append(tuple(low_all[:, start + j * width : start + (j + 1) * width] for j in range(3)))
        start += 3 * width

    image_vectors, image_direction, image_scaling, image_head = head_forward(middles[0], image_weights)
    caption_vectors, caption_direction, caption_scaling, caption_head = head_forward(
        middles[1], caption_weights
    )
    scale = jnp.exp(logit_scale[0])
    logits = scale * right_product(image_vectors, caption_vectors)
    places = jnp.arange(batch, dtype=jnp.int32)
    one_hot = (places[:, None] == places[None, :]).astype(F32)
    row_top = jnp.max(logits, 1, keepdims=True)
    row_lse = row_top + jnp.log(jnp.sum(jnp.exp(logits - row_top), 1, keepdims=True))
    col_top = jnp.max(logits, 0, keepdims=True)
    col_lse = col_top + jnp.log(jnp.sum(jnp.exp(logits - col_top), 0, keepdims=True))
    diagonal = jnp.sum(logits * one_hot)
    factor = 1.0 / (2.0 * batch)
    loss = (jnp.sum(row_lse) + jnp.sum(col_lse) - 2.0 * diagonal) * factor
    row_grad = (jnp.exp(logits - row_lse) - one_hot) * factor
    col_grad = (jnp.exp(logits - col_lse) - one_hot) * factor
    scale_grad = jnp.sum(row_grad * logits) + jnp.sum(col_grad * logits)
    row_low = (scale * row_grad).astype(BF16)
    col_low = (scale * col_grad).astype(BF16)
    image_vec_grad = product(row_low, caption_vectors) + product(col_low, caption_vectors)
    caption_vec_grad = left_product(col_low, image_vectors) + left_product(row_low, image_vectors)

    backs = (
        head_backward(image_vec_grad, image_direction, image_scaling, image_head, image_weights),
        head_backward(caption_vec_grad, caption_direction, caption_scaling, caption_head, caption_weights),
    )
    input_grads, query_grads, key_factors, norm_sums = [], [], [], []
    for (kept, weights, mine, picks, count), back in zip(towers, backs):
        mine_of = lambda rows: lax.dynamic_slice_in_dim(rows, index * count, count, 0)
        input_grad, query_grad, key_factor, gain_grad, bias_grad = local_backward(
            kept, mine, picks, mine_of(back[0]), mine_of(back[2]), weights
        )
        input_grads.append(input_grad)
        query_grads.append(query_grad)
        key_factors.append(key_factor)
        norm_sums.extend((gain_grad, bias_grad))

    query_all = gather(jnp.concatenate(query_grads, 1))
    query_all = (query_all[:, :image_width], query_all[:, image_width:])
    sums = jnp.concatenate([image_kept.squares, caption_kept.squares] + norm_sums)
    sums = lax.psum(sums, "dp")
    square_sums = sums[:6]
    norm_totals = []
    start = 6
    for width in (image_width, image_width, caption_width, caption_width):
        norm_totals.append(sums[start : start + width])
        start += width

    shards = []
    for tower in range(2):
        kept, weights, _, _, count = towers[tower]
        _, branch_low, attended_grad, head_sums, factors = backs[tower]
        width = widths[tower]
        size = width // devices
        heads = width // HD
        attended_all, normed_all, queries_all = lows[tower]
        columns = lambda rows: my_columns(rows, rows.shape[-1] // devices, index)
        query_block = left_product(columns(normed_all), query_all[tower])
        blocks = [query_block]
        for factor_rows, side in ((key_factors[tower], queries_all), (kept.value_factor, attended_grad)):
            met = exchange(factor_rows, devices).reshape(devices, size, heads, count)
            side = side.reshape(devices, count, heads, HD)
            blocks.append(
                jnp.einsum("sfhi,sihd->fhd", met, side, preferred_element_type=F32).reshape(size, width)
            )
        blocks[1] = blocks[1] / 8.0
        bias_wide = jnp.concatenate(
            [
                jnp.sum(query_all[tower].astype(F32), 0),
                jnp.sum(attended_grad.astype(F32), 0),
            ]
        )
        shards.extend(
            (
                columns(norm_totals[2 * tower]),
                columns(norm_totals[2 * tower + 1]),
                jnp.concatenate(blocks, 1),
                columns(bias_wide),
                left_product(columns(attended_all), branch_low),
                columns(head_sums.output_bias),
                columns(head_sums.second_gain),
                columns(head_sums.second_bias),
                left_product(columns(factors.expand[0]), factors.expand[1]),
                columns(head_sums.expand_bias),
                left_product(columns(factors.reduce[0]), factors.reduce[1]),
                columns(head_sums.reduce_bias),
                columns(head_sums.final_gain),
                columns(head_sums.final_bias),
                left_product(columns(factors.projection[0]), factors.projection[1]),
            )
        )
    image_cells = float(batch * patches * image_width)
    caption_cells = float(devices * row_count * row_length * caption_width)
    cells = jnp.array([image_cells] * 3 + [caption_cells] * 3, F32)
    return (
        loss.reshape(1),
        jnp.sqrt(square_sums / cells),
        input_grads[0].reshape(images.shape).astype(BF16),
        input_grads[1].reshape(captions.shape).astype(BF16),
        *shards,
        scale_grad.reshape(1),
    )


MESH = pl.DeviceIdType.MESH
BOX = 32


class Tower:
    def __init__(self, is_image, sequences, length, width, hidden, picks):
        self.is_image, self.sequences, self.length = is_image, sequences, length
        self.width, self.hidden = width, hidden
        self.heads = width // HD
        self.picks = picks
        self.tokens = sequences * length
        self.rows = -(-self.tokens // 80) * 80
        self.terms = self.heads * picks
        self.batch = BOX * picks
        self.mine = width // BOX
        self.vector_rows = (0, 8, 9) if is_image else (16, 10, 11)
        if is_image:
            self.window = 112
            self.windows = [(96 * j, 100 * j, 100 * j + 100) for j in range(sequences // 2)]
        else:
            self.window = 96
            self.windows = [
                (length * j // 16 * 16, length * j, length * (j + 1)) for j in range(sequences)
            ]


def iota(shape, axis):
    return lax.broadcasted_iota(jnp.int32, shape, axis)


def dot(left, right, over=((1,), (0,)), precision=None):
    return lax.dot_general(
        left, right, (over, ((), ())), preferred_element_type=F32, precision=precision
    )


ROWS_BY_COLUMNS = ((1,), (1,))
COLUMNS_BY_COLUMNS = ((0,), (0,))
HIGHEST = lax.Precision.HIGHEST


UNROLL = 1
PACE = 2
LATE_EVERY = 2
LATE_FROM = 6


def loop(count, body):
    lax.fori_loop(0, count, lambda step, carry: (body(step), carry)[1], 0, unroll=min(count, UNROLL))


def rows_at(step, size):
    return pl.ds(pl.multiple_of(step * size, size), size)


def centred_unit(rows):
    width = rows.shape[-1]
    centred = rows - jnp.sum(rows, -1, keepdims=True) * (1.0 / width)
    inverse = lax.rsqrt(jnp.sum(centred * centred, -1, keepdims=True) * (1.0 / width) + 1e-05)
    return centred * inverse, inverse


def inward_of(upstream, unit_rows, inverse, gain):
    width = upstream.shape[-1]
    scaled = upstream * gain
    mean = jnp.sum(scaled, -1, keepdims=True) * (1.0 / width)
    slope = jnp.sum(scaled * unit_rows, -1, keepdims=True) * (1.0 / width)
    return inverse * (scaled - mean - unit_rows * slope)


def gate_of(hidden):
    return 0.5 * jnp.tanh(0.851 * hidden) + 0.5


def column_sum(rows):
    return jnp.sum(rows, 0, keepdims=True)


def spread_rows(rows, heads):
    lane_head = jnp.right_shift(iota(rows.shape, 1), 6)
    return jnp.concatenate([jnp.where(lane_head == h, rows, 0.0) for h in range(heads)], 0).astype(BF16)


def fold_rows(rows, heads, picks):
    lane_head = jnp.right_shift(iota((picks, rows.shape[1]), 1), 6)
    total = jnp.zeros((picks, rows.shape[1]), F32)
    for h in range(heads):
        total = total + jnp.where(lane_head == h, rows[h * picks : (h + 1) * picks], 0.0)
    return total


WIDTH_VECTORS = tuple(name for name in VECTORS if name not in (NAMES[3], NAMES[9]))


class Row:
    norm_gain, norm_bias, output_bias, second_gain, second_bias, reduce_bias, final_gain, final_bias = range(8)


class Places:
    def __init__(self):
        self.me = lax.axis_index("dp")
        self.core = lax.rem(self.me, 2)
        self.x = lax.rem(self.me // 2, 2)
        self.y = lax.rem(self.me // 4, 2)
        self.z = self.me // 8

    def device(self, ahead, across_y, across_x, other):
        z = lax.rem(self.z + ahead, 4)
        y = self.y + across_y - 2 * self.y * across_y
        x = self.x + across_x - 2 * self.x * across_x
        core = self.core + other - 2 * self.core * other
        return ((z * 2 + y) * 2 + x) * 2 + core


class Item:
    def __init__(self, target, size, odd, paired=False):
        self.target, self.size, self.odd, self.paired = target, size, odd, paired
        self.sent = 0


class Spread:
    def __init__(self, places, items, near_sem, core_sem, send_sem):
        self.places, self.items = places, items
        self.near_sem, self.core_sem, self.send_sem = near_sem, core_sem, send_sem
        self.x_next = places.device(0, 0, 1, 0)
        self.y_next = places.device(0, 1, 0, 0)
        self.sibling = places.device(0, 0, 0, 1)
        self.z_next = [None] + [places.device(step, 0, 0, 0) for step in (1, 2, 3)]

    def block(self, number, key):
        item = self.items[number]
        ahead, across_y, across_x = key
        owner = self.places.device((4 - ahead) % 4, across_y, across_x, 0)
        if item.paired:
            half = item.target.shape[1] // 2
            rows = pl.ds(pl.multiple_of((owner // 2) * (2 * item.size), 2 * item.size), 2 * item.size)
            return item.target.at[rows, pl.ds(pl.multiple_of(self.places.core * half, 128), half)]
        return item.target.at[pl.ds(pl.multiple_of(owner * item.size, item.size), item.size)]

    def send(self, number, key, device, sem):
        block = self.block(number, key)
        pltpu.make_async_remote_copy(
            src_ref=block,
            dst_ref=block,
            send_sem=self.send_sem.at[number],
            recv_sem=sem,
            device_id=(device,),
            device_id_type=MESH,
        ).start()
        self.items[number].sent += 1

    def near(self, number, key):
        ahead, across_y, across_x = key
        return self.near_sem.at[number, ahead * 4 + across_y * 2 + across_x]

    def forward(self, number, key):
        ahead, across_y, across_x = key
        item = self.items[number]
        if (across_y, across_x) == (0, 0):
            if ahead == 0:
                for step in (1, 2, 3):
                    self.send(number, key, self.z_next[step], self.near(number, (step, 0, 0)))
            self.send(number, key, self.x_next, self.near(number, (ahead, 0, 1)))
            self.send(number, key, self.y_next, self.near(number, (ahead, 1, 0)))
        elif (across_y, across_x) == (0, 1) and ahead % 2 == item.odd:
            self.send(number, key, self.y_next, self.near(number, (ahead, 1, 1)))
        elif (across_y, across_x) == (1, 0) and ahead % 2 != item.odd:
            self.send(number, key, self.x_next, self.near(number, (ahead, 1, 1)))
        if not (item.paired and key == (0, 0, 0)):
            self.send(number, key, self.sibling, self.core_sem.at[number])

    def whole(self, ref, number, sem):
        return pltpu.make_async_remote_copy(
            src_ref=ref,
            dst_ref=ref,
            send_sem=self.send_sem.at[number],
            recv_sem=sem,
            device_id=(self.sibling,),
            device_id_type=MESH,
        )

    def start(self, number):
        self.forward(number, (0, 0, 0))

    def keys(self, stage):
        return (
            [(step, 0, 0) for step in (1, 2, 3)],
            [(step, *side) for step in range(4) for side in ((0, 1), (1, 0))],
            [(step, 1, 1) for step in range(4)],
        )[stage]

    def pass_on(self, number, key):
        self.whole(self.block(number, key), number, self.near(number, key)).wait_recv()
        self.forward(number, key)

    def wait(self, number):
        item = self.items[number]
        if item.paired:
            ref = item.target.at[pl.ds(0, 30 * item.size), pl.ds(0, item.target.shape[1] // 2)]
        else:
            ref = item.target.at[pl.ds(0, 16 * item.size)]
        self.whole(ref, number, self.core_sem.at[number]).wait_recv()

    def finish(self, number):
        item = self.items[number]
        ref = item.target.at[pl.ds(0, item.sent * item.size)]
        self.whole(ref, number, self.core_sem.at[number]).wait_send()


def fraction_floor(numbers, divisor):
    return jnp.floor((numbers.astype(F32) + 0.5) * (1.0 / divisor))


def columns_at(step, size):
    if isinstance(step, int):
        return slice(step * size, step * size + size)
    return pl.ds(pl.multiple_of(step * size, size), size)


class Step:
    def __init__(self, towers, r, places):
        self.towers, self.r, self.places = towers, r, places
        self.me = places.me

    def vector(self, tower, row):
        return tower.refs.vectors[row : row + 1, :]

    def pause(self, count=None):
        pass

    def paced(self, count, body, group=3):
        for first in range(0, count, group):
            loop(min(group, count - first), lambda step, first=first: body(first + step))
            self.pause()


    def pack_vectors(self):
        r = self.r
        pack = r.vpack
        pack[...] = jnp.zeros_like(pack)
        for tower in self.towers:
            first, attend_row, expand_row = tower.vector_rows
            shards = tower.shards
            rows = [(first + k, getattr(shards, name)) for k, name in enumerate(WIDTH_VECTORS)]
            for row, source in rows + [(attend_row, shards.attend_bias), (expand_row, shards.expand_bias)]:
                pack[row : row + 1, 0 : source.shape[0]] = source[...].astype(F32)[None, :]
        r.vall[pl.ds(pl.multiple_of(self.me * 24, 8), 24)] = pack[...]

    def place_own(self, shard, whole):
        size = shard.shape[0]
        whole[pl.ds(pl.multiple_of(self.me * size, size), size)] = shard[...]

    def join_pair(self, shard, other, whole):
        size = shard.shape[0]
        rows = pl.ds(pl.multiple_of((self.me // 2) * (2 * size), 2 * size), 2 * size)
        first = self.places.core == 0

        def body(step):
            columns = columns_at(step, 256)
            own, met = shard[:, columns].astype(F32), other[:, columns].astype(F32)
            both = jnp.concatenate([jnp.where(first, own, met), jnp.where(first, met, own)], 0)
            whole[rows, columns] = both.astype(BF16)

        loop(shard.shape[1] // 256, body)

    def unpack_vectors(self, tower):
        r = self.r
        first, attend_row, expand_row = tower.vector_rows
        width, hidden = tower.width, tower.hidden
        for row, size, target in (
            (first, width // BOX, tower.refs.vectors),
            (attend_row, 2 * width // BOX, tower.refs.attend_vector),
            (expand_row, hidden // BOX, tower.refs.expand_vector),
        ):
            group = row // 8 * 8
            blocks = r.vall[...].reshape(BOX, 24, 128)[:, group : group + 8, :]
            blocks = blocks.reshape(BOX * 8, 128).astype(BF16)
            chunk = 256

            def body(step, row=row, size=size, blocks=blocks, target=target):
                lane = iota((1, chunk), 1) + step * chunk
                owner = fraction_floor(lane, size)
                within = lane.astype(F32) - owner * size
                spread = (iota((128, chunk), 0).astype(F32) == within).astype(F32).astype(BF16)
                met = dot(blocks, spread).reshape(BOX, 8, chunk)
                device = iota((BOX, 8, chunk), 0).astype(F32)
                total = jnp.sum(jnp.where(device == owner.reshape(1, 1, chunk), met, 0.0), 0)
                if target is tower.refs.vectors:
                    target[:, columns_at(step, chunk)] = total
                else:
                    target[0:1, columns_at(step, chunk)] = total[row % 8 : row % 8 + 1]

            loop(target.shape[1] // chunk, body)
            self.pause()
        bias = tower.refs.mixed_bias
        bias[0:1, 0:width] = tower.refs.attend_vector[0:1, 0:width]
        bias[0:1, width : 2 * width] = jnp.zeros((1, width), F32)
        bias[0:1, 2 * width :] = tower.refs.attend_vector[0:1, width:]

    def load_tokens(self, tower):
        source, rows = tower.refs.tokens, tower.refs.x
        if tower.rows > tower.tokens:
            low = tower.tokens // 8 * 8
            rows[low:, :] = jnp.zeros((tower.rows - low, tower.width), F32)
        for number in range(tower.sequences):
            start = number * tower.length
            rows[start : start + tower.length, :] = source[:, number, :].astype(F32)

    def norm_tokens(self, tower, source, target, gain, bias):
        gain, bias = self.vector(tower, gain), self.vector(tower, bias)

        def body(step):
            rows = rows_at(step, 80)
            unit, _ = centred_unit(source[rows, :])
            target[rows, :] = (unit * gain + bias).astype(BF16)

        loop(tower.rows // 80, body)
        self.pause()


    def mix(self, tower):
        normed, mixed = tower.refs.normed, tower.refs.mixed
        weight, bias = tower.weights.attend, tower.refs.mixed_bias

        def body(step):
            columns = columns_at(step, 256)
            mixed[:, columns] = (dot(normed[...], weight[:, columns]) + bias[0:1, columns]).astype(BF16)

        self.paced(3 * tower.width // 256, body)

    def masks(self, tower):
        bias = tower.refs.mask
        side = tower.window
        query, key = iota((side, side), 0), iota((side, side), 1)
        for number, (row, _, _) in enumerate(tower.windows):
            if tower.is_image:
                allowed = fraction_floor(query + row, tower.length) == fraction_floor(
                    key + row, tower.length
                )
            else:
                first, second = self.r.ends[0, number], self.r.ends[1, number]
                query_place, key_place = [
                    place + (row - number * tower.length) for place in (query, key)
                ]

                def piece(place):
                    return jnp.where(place >= first, 1, 0) + jnp.where(place >= second, 1, 0)

                allowed = (
                    (piece(query_place) == piece(key_place))
                    & (query_place >= key_place)
                    & (key_place < second)
                    & (key_place >= 0)
                    & (query_place < tower.length)
                ) | (query == key)
            bias[number] = jnp.where(allowed, 0.0, -1e30)

    def attend(self, tower):
        width, side = tower.width, tower.window
        mixed, total, bias = tower.refs.mixed, tower.refs.att, tower.refs.mask
        total[...] = jnp.zeros_like(total)

        def body(step, windows):
            lane = iota((1, 128), 1)
            left = jnp.where(lane < HD, 1.0, 0.0)
            sides = (left.astype(BF16), (1.0 - left).astype(BF16))
            for number in windows:
                row, first, last = tower.windows[number]
                rows = slice(row, row + side)
                query, key, value = [
                    mixed[rows, columns_at(step + part * (width // 128), 128)] for part in range(3)
                ]
                out = []
                for half in sides:
                    scores = dot(query * half, key, ROWS_BY_COLUMNS) * 0.125 + bias[number]
                    weights = jnp.exp(scores - jnp.max(scores, -1, keepdims=True))
                    weights = weights * (1.0 / jnp.sum(weights, -1, keepdims=True))
                    out.append(dot(weights.astype(BF16), value))
                both = jnp.where(lane < HD, out[0], out[1])
                place = iota((side, 1), 0) + row
                kept = jnp.where((place >= first) & (place < last), 1.0, 0.0)
                columns = columns_at(step, 128)
                total[rows, columns] = total[rows, columns] + both * kept

        for pair in range(0, width // 128, 2):
            for first in range(0, len(tower.windows), 2):
                loop(2, lambda step, pair=pair, first=first: body(pair + step, (first, first + 1)))
                self.pause(2 * PACE + 1)
        low = tower.refs.attlow

        def narrow(step):
            low[rows_at(step, 80), :] = total[rows_at(step, 80), :].astype(BF16)

        loop(tower.rows // 80, narrow)

    def add_square(self, slot, rows, tower):
        if tower.rows > tower.tokens:
            rows = jnp.where(iota((rows.shape[0], 1), 0) < tower.tokens, rows, 0.0)
        squares = column_sum(rows * rows)
        width = squares.shape[1]
        folded = sum(squares[:, k * 128 : (k + 1) * 128] for k in range(width // 128))
        self.r.squares[slot : slot + 1, :] = self.r.squares[slot : slot + 1, :] + folded

    def project(self, tower):
        stream, middle, low = tower.refs.x, tower.refs.middle, tower.refs.attlow
        weight = tower.weights.output
        slot = 0 if tower.is_image else 3
        bias_row = Row.output_bias

        def body(step):
            columns = columns_at(step, 256)
            bias = tower.refs.vectors[bias_row : bias_row + 1, columns]
            branch = dot(low[...], weight[:, columns]) + bias
            middle[:, columns] = stream[:, columns] + branch
            self.add_square(slot, branch, tower)

        loop(tower.width // 256, body)
        self.pause()

    def own_active(self, tower):
        rows = slice(0, tower.rows)
        normed, active = tower.refs.normed_two, self.r.active
        weight, bias = tower.weights.expand, tower.refs.expand_vector

        def body(step):
            columns = columns_at(step, 256)
            hidden = dot(normed[...], weight[:, columns]) + bias[0:1, columns]
            active[rows, columns] = (hidden * gate_of(hidden)).astype(BF16)

        self.paced(tower.hidden // 256, body, 2)

    def own_second(self, tower):
        rows = slice(0, tower.rows)
        active, middle, weight = self.r.active, tower.refs.middle, tower.weights.reduce
        slot = 1 if tower.is_image else 4
        bias_row = Row.reduce_bias

        def body(step):
            columns = columns_at(step, 256)
            bias = tower.refs.vectors[bias_row : bias_row + 1, columns]
            second = dot(active[rows, 0 : tower.hidden], weight[:, columns]) + bias
            self.add_square(slot, second, tower)
            self.add_square(slot + 1, second + middle[:, columns], tower)

        self.paced(tower.width // 256, body, 1)


    def pick_places(self, tower):
        if tower.is_image:
            return [(i * tower.length, i * tower.length) for i in range(tower.picks)]
        places = []
        for i in range(tower.picks):
            start, ends = (i // 2) * tower.length, self.r.ends
            first = start + (ends[0, i // 2] if i % 2 else 0)
            places.append((first, start + ends[i % 2, i // 2] - 1))
        return places

    def selection(self, tower):
        row = iota((tower.picks, 1), 0)
        token = jnp.zeros((tower.picks, 1), jnp.int32)
        for i, (_, pick) in enumerate(self.pick_places(tower)):
            token = jnp.where(row == i, pick, token)
        return jnp.where(iota((tower.picks, tower.rows), 1) == token, 1.0, 0.0)

    def placement(self, tower):
        lane = iota((1, tower.picks), 1)
        token = jnp.zeros((1, tower.picks), jnp.int32)
        for i, (_, pick) in enumerate(self.pick_places(tower)):
            token = jnp.where(lane == i, pick, token)
        return jnp.where(iota((tower.rows, tower.picks), 0) == token, 1.0, 0.0)

    def picked_forward(self, tower):
        width, heads, terms, picks = tower.width, tower.heads, tower.terms, tower.picks
        select = self.selection(tower)
        low_select = select.astype(BF16)
        mixed, normed = tower.refs.mixed, tower.refs.normed
        queries = dot(low_select, mixed[:, 0:width])
        middle_rows = dot(select, tower.refs.middle[...], precision=HIGHEST)
        normed_rows = dot(low_select, normed[...])
        attended_rows = dot(low_select, tower.refs.attlow[...])
        wide = spread_rows(queries, heads)
        tower.refs.qe[...] = wide
        scores = dot(mixed[:, width : 2 * width], wide, ROWS_BY_COLUMNS) * 0.125
        lane = jnp.bitwise_and(iota((1, terms), 1), picks - 1)
        first = jnp.zeros((1, terms), jnp.int32)
        last = jnp.zeros((1, terms), jnp.int32)
        for i, (begin, pick) in enumerate(self.pick_places(tower)):
            first = jnp.where(lane == i, begin, first)
            last = jnp.where(lane == i, pick, last)
        if tower.is_image:
            last = first + (tower.length - 1)
        place = iota((tower.rows, terms), 0)
        scores = jnp.where((place >= first) & (place <= last), scores, -1e30)
        soft = jnp.exp(scores - jnp.max(scores, 0, keepdims=True))
        soft = soft * (1.0 / column_sum(soft))
        tower.refs.soft[...] = soft
        factor = dot(soft.astype(BF16), normed[...], COLUMNS_BY_COLUMNS)
        pad = jnp.zeros((128 - terms - 2 * picks, width), F32)
        rows = jnp.concatenate([factor, normed_rows, attended_rows, pad], 0)
        self.store_factor(tower, tower.refs.t_met, rows)
        return middle_rows, queries

    def store_factor(self, tower, met, rows):
        blocks = rows.T.reshape(BOX, tower.mine, 128).astype(BF16)
        tower.refs.factor_out[...] = blocks
        met[self.me] = tower.refs.factor_out[self.me]


    def head_middle(self, tower, rows):
        start = 0 if tower.is_image else self.towers[0].width
        return self.r.middles[rows, start : start + tower.width]

    def head_hidden(self, tower):
        normed = tower.refs.h_normed
        gain, bias = self.vector(tower, Row.second_gain), self.vector(tower, Row.second_bias)

        def norm(step):
            rows = rows_at(step, 64)
            unit, _ = centred_unit(self.head_middle(tower, rows))
            normed[rows, :] = (unit * gain + bias).astype(BF16)

        loop(tower.batch // 64, norm)
        weight, expand_bias = tower.weights.expand, tower.refs.expand_vector
        hidden_ref, active = tower.refs.h_hidden, tower.refs.h_active

        def body(step):
            columns = columns_at(step, 256)
            hidden = dot(normed[...], weight[:, columns]) + expand_bias[0:1, columns]
            hidden_ref[:, columns] = hidden
            active[:, columns] = (hidden * gate_of(hidden)).astype(BF16)

        self.paced(tower.hidden // 256, body, 3)

    def head_vectors(self, tower):
        result, active = tower.refs.h_unit, tower.refs.h_active
        weight = tower.weights.reduce
        bias_row = Row.reduce_bias
        start = 0 if tower.is_image else self.towers[0].width

        def body(step):
            columns = columns_at(step, 256)
            bias = tower.refs.vectors[bias_row : bias_row + 1, columns]
            middle = self.r.middles[:, pl.ds(pl.multiple_of(start + step * 256, 256), 256)]
            result[:, columns] = middle + (dot(active[...], weight[:, columns]) + bias)

        self.paced(tower.width // 256, body, 1)
        gain, bias = self.vector(tower, Row.final_gain), self.vector(tower, Row.final_bias)
        inverse_ref, normed = tower.refs.h_inverse, tower.refs.h_final

        def norm(step):
            rows = rows_at(step, 64)
            unit, inverse = centred_unit(result[rows, :])
            result[rows, :] = unit
            inverse_ref[rows, :] = inverse
            normed[rows, :] = (unit * gain + bias).astype(BF16)

        loop(tower.batch // 64, norm)
        self.pause()

        def embed(step):
            rows = rows_at(step, 64)
            raw = dot(normed[rows, :], tower.weights.projection[...])
            scaling = lax.rsqrt(jnp.sum(raw * raw, -1, keepdims=True) + 1e-06)
            direction = raw * scaling
            tower.refs.h_scaling[rows, :] = scaling
            tower.refs.h_direction[rows, :] = direction
            tower.refs.h_vectors[rows, :] = direction.astype(BF16)

        loop(tower.batch // 64, embed)

    def contrast(self):
        image, caption = self.towers
        batch = image.batch
        vectors, others = image.refs.h_vectors[...], caption.refs.h_vectors[...]
        scale = jnp.exp(jnp.full((1, 1), self.r.logit_scale[0], F32))
        logits = scale * dot(vectors, others, ROWS_BY_COLUMNS)
        same = jnp.where(iota((batch, batch), 0) == iota((batch, batch), 1), 1.0, 0.0)
        row_top = jnp.max(logits, 1, keepdims=True)
        row_lse = row_top + jnp.log(jnp.sum(jnp.exp(logits - row_top), 1, keepdims=True))
        column_top = jnp.max(logits, 0, keepdims=True)
        column_lse = column_top + jnp.log(column_sum(jnp.exp(logits - column_top)))

        def whole_sum(rows):
            return jnp.sum(column_sum(rows), 1, keepdims=True)

        factor = 1.0 / (2.0 * batch)
        loss = (
            whole_sum(row_lse) + whole_sum(column_lse) - 2.0 * whole_sum(logits * same)
        ) * factor
        row_grad = (jnp.exp(logits - row_lse) - same) * factor
        column_grad = (jnp.exp(logits - column_lse) - same) * factor
        scale_grad = whole_sum(row_grad * logits) + whole_sum(column_grad * logits)
        self.r.out_loss[...] = loss[0, :]
        self.r.out_scale[...] = scale_grad[0, :]
        row_low, column_low = self.r.row_low, self.r.column_low
        row_low[...] = (scale * row_grad).astype(BF16)
        column_low[...] = (scale * column_grad).astype(BF16)

        def image_side(step):
            rows = rows_at(step, 64)
            others = caption.refs.h_vectors[...]
            self.raw_grad(image, rows, dot(row_low[rows, :], others) + dot(column_low[rows, :], others))

        def caption_side(step):
            rows = rows_at(step, 128)
            others = image.refs.h_vectors[...]
            upstream = dot(column_low[:, rows], others, COLUMNS_BY_COLUMNS)
            upstream = upstream + dot(row_low[:, rows], others, COLUMNS_BY_COLUMNS)
            self.raw_grad(caption, rows, upstream)

        loop(batch // 64, image_side)
        loop(batch // 128, caption_side)

    def raw_grad(self, tower, rows, upstream):
        direction = tower.refs.h_direction[rows, :]
        along = jnp.sum(upstream * direction, -1, keepdims=True)
        raw = tower.refs.h_scaling[rows, :] * (upstream - direction * along)
        tower.refs.h_raw[rows, :] = raw.astype(BF16)

    def add_sum(self, tower, slot, row):
        sums = tower.refs.sums
        sums[slot : slot + 1, :] = sums[slot : slot + 1, :] + row

    def against(self, tower, source, weight, target):
        def body(step):
            target[:, columns_at(step, 256)] = dot(
                source[...], weight[rows_at(step, 256), :], ROWS_BY_COLUMNS
            )

        loop(tower.width // 256, body)

    def head_backward(self, tower):
        grad, result_grad = tower.refs.h_grad, tower.refs.h_middle_grad
        unit_ref, inverse_ref = tower.refs.h_unit, tower.refs.h_inverse
        second_low = tower.refs.h_second_low
        tower.refs.sums[...] = jnp.zeros_like(tower.refs.sums)
        self.against(tower, tower.refs.h_raw, tower.weights.projection, grad)
        gain = self.vector(tower, Row.final_gain)

        def final_norm(step):
            rows = rows_at(step, 64)
            upstream, unit = grad[rows, :], unit_ref[rows, :]
            inward = inward_of(upstream, unit, inverse_ref[rows, :], gain)
            low = inward.astype(BF16)
            result_grad[rows, :] = inward
            second_low[rows, :] = low
            self.add_sum(tower, Row.final_gain, column_sum(upstream * unit))
            self.add_sum(tower, Row.final_bias, column_sum(upstream))
            self.add_sum(tower, Row.reduce_bias, column_sum(low.astype(F32)))

        loop(tower.batch // 64, final_norm)
        weight, hidden_ref = tower.weights.reduce, tower.refs.h_hidden
        hidden_low, expand_sums = tower.refs.h_hidden_low, tower.refs.expand_sums

        def body(step):
            columns = columns_at(step, 256)
            active_grad = dot(second_low[...], weight[rows_at(step, 256), :], ROWS_BY_COLUMNS)
            hidden = hidden_ref[:, columns]
            gate = gate_of(hidden)
            low = (active_grad * (gate + 1.702 * hidden * gate * (1.0 - gate))).astype(BF16)
            hidden_low[:, columns] = low
            expand_sums[0:1, columns] = column_sum(low.astype(F32))

        loop(tower.hidden // 256, body)
        self.against(tower, hidden_low, tower.weights.expand, grad)
        second_gain, branch_low = self.vector(tower, Row.second_gain), tower.refs.h_branch_low

        def second_norm(step):
            rows = rows_at(step, 64)
            upstream = grad[rows, :]
            unit, inverse = centred_unit(self.head_middle(tower, rows))
            inward = result_grad[rows, :] + inward_of(upstream, unit, inverse, second_gain)
            low = inward.astype(BF16)
            result_grad[rows, :] = inward
            branch_low[rows, :] = low
            self.add_sum(tower, Row.second_gain, column_sum(upstream * unit))
            self.add_sum(tower, Row.second_bias, column_sum(upstream))
            self.add_sum(tower, Row.output_bias, column_sum(low.astype(F32)))

        loop(tower.batch // 64, second_norm)
        self.against(tower, branch_low, tower.weights.output, grad)

        def narrow(step):
            rows = rows_at(step, 64)
            low = grad[rows, :].astype(BF16).astype(F32)
            grad[rows, :] = low
            tower.refs.value_sums[0:1, :] = tower.refs.value_sums[0:1, :] + column_sum(low)

        tower.refs.value_sums[...] = jnp.zeros_like(tower.refs.value_sums)
        loop(tower.batch // 64, narrow)


    def local_backward(self, tower):
        width, heads, picks, terms = tower.width, tower.heads, tower.picks, tower.terms
        mine = pl.ds(pl.multiple_of(self.me * picks, picks), picks)
        wide_grad = spread_rows(tower.refs.h_grad[mine, :], heads)
        mixed, normed = tower.refs.mixed, tower.refs.normed
        soft = tower.refs.soft[...]
        soft_grad = dot(mixed[:, 2 * width :], wide_grad, ROWS_BY_COLUMNS)
        score_low = (soft * (soft_grad - column_sum(soft_grad * soft))).astype(BF16)
        query_grad = fold_rows(
            dot(score_low, mixed[:, width : 2 * width], COLUMNS_BY_COLUMNS), heads, picks
        )
        query_low = (query_grad * 0.125).astype(BF16)
        attend = tower.weights.attend
        scores_ref, soft_low, wide_ref = self.r.score_low, self.r.soft_low, self.r.wide_grad
        scores_ref[0 : tower.rows, 0:terms] = score_low
        soft_low[0 : tower.rows, 0:terms] = soft.astype(BF16)
        wide_ref[0:terms, 0:width] = wide_grad
        placement = self.r.placement
        placement[0 : tower.rows, :] = self.placement(tower)
        queries = tower.refs.qe

        def sides(step):
            rows = rows_at(step, 256)
            key_side = dot(queries[...], attend[rows, width : 2 * width], ROWS_BY_COLUMNS) * 0.125
            value_side = dot(wide_ref[0:terms, 0:width], attend[rows, 2 * width :], ROWS_BY_COLUMNS)
            query_side = dot(query_low, attend[rows, 0:width], ROWS_BY_COLUMNS)
            tower.refs.att[:, rows] = (
                dot(scores_ref[0 : tower.rows, 0:terms], key_side.astype(BF16))
                + dot(soft_low[0 : tower.rows, 0:terms], value_side.astype(BF16))
                + dot(placement[0 : tower.rows, :], query_side, precision=HIGHEST)
            )

        loop(width // 256, sides)
        key_factor = dot(score_low, normed[...], COLUMNS_BY_COLUMNS)
        gain = self.vector(tower, Row.norm_gain)
        source, grad = tower.refs.tokens, tower.refs.att
        sums = tower.refs.norm_sums
        sums[...] = jnp.zeros_like(sums)
        for number in range(tower.sequences):
            rows = slice(number * tower.length, (number + 1) * tower.length)
            upstream = grad[rows, :]
            unit, inverse = centred_unit(source[:, number, :].astype(F32))
            grad[rows, :] = inward_of(upstream, unit, inverse, gain)
            sums[0:1, :] = sums[0:1, :] + column_sum(upstream * unit)
            sums[1:2, :] = sums[1:2, :] + column_sum(upstream)
        pad = jnp.zeros((128 - terms - 8, width), F32)
        self.store_factor(tower, tower.refs.s_met, jnp.concatenate([key_factor, sums[...], pad], 0))
        return query_low.astype(F32)

    def input_gradient(self, tower):
        mine = pl.ds(pl.multiple_of(self.me * tower.picks, tower.picks), tower.picks)
        grad, out = tower.refs.att, tower.refs.out_tokens
        placement = self.r.placement
        placement[0 : tower.rows, :] = self.placement(tower)

        def add(step):
            columns = columns_at(step, 256)
            middle_grad = tower.refs.h_middle_grad[mine, columns]
            placed = dot(placement[0 : tower.rows, :], middle_grad, precision=HIGHEST)
            grad[:, columns] = grad[:, columns] + placed

        loop(tower.width // 256, add)
        for number in range(tower.sequences):
            start = number * tower.length
            out[:, number, :] = grad[start : start + tower.length, :].astype(BF16)


    def my_columns(self, total, size):
        return jnp.where(iota((size, total), 1) == iota((size, total), 0) + self.me * size, 1.0, 0.0)

    def turned_columns(self, source, size):
        pick = self.my_columns(source.shape[1], size).astype(BF16)
        return dot(pick, source[...], ROWS_BY_COLUMNS).astype(BF16)

    def gradient_blocks(self, left, right, out):
        step_size = 256

        def body(step):
            columns = columns_at(step, step_size)
            out[:, columns] = dot(left, right[:, columns])

        loop(right.shape[1] // step_size, body)

    def turn_head(self, tower):
        refs, size = tower.refs, tower.mine
        refs.turned_normed[...] = self.turned_columns(refs.h_normed, size)
        refs.turned_active[...] = self.turned_columns(refs.h_active, tower.hidden // BOX)
        refs.turned_final[...] = self.turned_columns(refs.h_final, size)

    def head_gradients(self, tower):
        size = tower.mine
        self.gradient_blocks(
            tower.refs.turned_final[...],
            tower.refs.h_raw,
            tower.outs.projection,
        )
        self.gradient_blocks(
            tower.refs.turned_active[...],
            tower.refs.h_second_low,
            tower.outs.reduce,
        )
        self.gradient_blocks(
            tower.refs.turned_normed[...],
            tower.refs.h_hidden_low,
            tower.outs.expand,
        )
        pick = self.my_columns(tower.width, size)
        sums = dot(tower.refs.sums[...], pick, ROWS_BY_COLUMNS, HIGHEST)
        for k, name in enumerate(WIDTH_VECTORS[2:], 2):
            getattr(tower.outs, name)[...] = sums[k, :]
        pick = self.my_columns(tower.hidden, tower.hidden // BOX)
        tower.outs.expand_bias[...] = dot(
            tower.refs.expand_sums[...], pick, ROWS_BY_COLUMNS, HIGHEST
        )[0, :]

    def regroup(self, tower, met):
        grouped, size = self.r.grouped, tower.mine
        lane = jnp.right_shift(iota((size, 128), 1), 3)

        def body(tile):
            blocks = [met[tile * 16 + k].astype(F32) for k in range(16)]
            for span in (1, 2, 4, 8):
                low = jnp.bitwise_and(lane, span) == 0
                for k in range(16):
                    if k & span:
                        continue
                    first, second = blocks[k], blocks[k + span]
                    blocks[k] = jnp.where(low, first, pltpu.roll(second, 8 * span, 1))
                    blocks[k + span] = jnp.where(low, pltpu.roll(first, 128 - 8 * span, 1), second)
            for group, block in enumerate(blocks):
                start = (tile * 16 + group) * size
                grouped[pl.ds(pl.multiple_of(start, 8), size), :] = block

        loop(BOX // 16, body)

    def group_terms(self, tower, group, count=1):
        size, tiles = tower.mine, []
        for tile in range(BOX // 16):
            start = (tile * 16 + group) * size
            tiles.append(self.r.grouped[start : start + count * size, :])
        return jnp.concatenate(tiles, 1).astype(BF16)

    def output_gradient(self, tower):
        self.gradient_blocks(
            self.group_terms(tower, tower.heads + 1), tower.refs.h_branch_low, tower.outs.output
        )

    def factor_gradient(self, tower, side, part):
        size, width = tower.mine, tower.width
        left = self.group_terms(tower, 0, tower.heads)

        def body(step):
            columns = columns_at(step, 128)
            met = dot(left, side[:, columns].astype(BF16))
            lane = jnp.right_shift(iota((size, 128), 1), 6)
            total = jnp.zeros((size, 128), F32)
            for head in range(tower.heads):
                mine = lane + 2 * step == head
                total = total + jnp.where(mine, met[head * size : (head + 1) * size], 0.0)
            out = pl.ds(pl.multiple_of(part * width + step * 128, 128), 128)
            tower.outs.attend[:, out] = total

        loop(width // 128, body)

    def rows_of_pair(self, tower, ref, device):
        block = ref[pl.ds(pl.multiple_of(device * 16, 16), 16), :].astype(F32)
        rows = jnp.concatenate([block[0:8], block[8:16]], 1)
        start = 0 if tower.is_image else self.towers[0].width
        return rows[:, start : start + tower.width]

    def unpack_rows(self, tower, source, target, scale):
        for device in range(0, BOX, 2):
            pair = [self.rows_of_pair(tower, source, device + k) for k in range(2)]
            target[device * 8 : device * 8 + 16, :] = (jnp.concatenate(pair, 0) * scale).astype(BF16)

    def query_gradient(self, tower):
        r, size, width = self.r, tower.mine, tower.width
        rows = tower.refs.h_query_low
        self.unpack_rows(tower, r.query_grads, rows, 1.0)
        tower.outs.attend[:, 0:width] = dot(tower.refs.normed_terms[...], rows[...])
        bias = tower.refs.bias_sums
        bias[0:1, 0:width] = column_sum(rows[...].astype(F32))
        bias[0:1, width:] = tower.refs.value_sums[0:1, :]
        pick = self.my_columns(2 * width, 2 * size)
        tower.outs.attend_bias[...] = dot(bias[...], pick, ROWS_BY_COLUMNS, HIGHEST)[0, :]
        total = jnp.zeros((size, 128), F32)
        met = tower.refs.s_met
        for device in range(BOX):
            total = total + met[device].astype(F32)
        lane = iota((8, 128), 1)
        row = iota((8, 128), 0)
        pick = jnp.where(lane == row + tower.terms, 1.0, 0.0)
        sums = dot(pick, total, ROWS_BY_COLUMNS, HIGHEST)
        tower.outs.norm_gain[...] = sums[0, :]
        tower.outs.norm_bias[...] = sums[1, :]


class Route:
    (
        vectors,
        caption_attend,
        caption_output,
        image_attend,
        image_output,
        image_expand,
        image_projection,
        middles,
        queries,
        image_reduce,
        caption_projection,
        caption_expand,
        caption_reduce,
        query_grads,
    ) = range(14)


def swap_out(me, count, source_of, target, send_sem, recv_sem):
    def body(step):
        device = lax.rem(me + 1 + step, count)
        pltpu.make_async_remote_copy(
            src_ref=source_of(device),
            dst_ref=target.at[me],
            send_sem=send_sem,
            recv_sem=recv_sem,
            device_id=(device,),
            device_id_type=MESH,
        ).start()

    loop(count - 1, body)


def swap_descriptor(me, count, target, send_sem, recv_sem):
    most = target.at[pl.ds(0, count - 1)]
    return pltpu.make_async_remote_copy(
        src_ref=most,
        dst_ref=most,
        send_sem=send_sem,
        recv_sem=recv_sem,
        device_id=(lax.rem(me + 1, count),),
        device_id_type=MESH,
    )


def step_kernel(image, caption, r):
    for tower in (image, caption):
        refs, batch = tower.refs, tower.batch
        refs.middle = refs.x
        refs.normed_two = refs.mixed.at[:, 0 : tower.width]
        refs.h_branch_low = refs.attlow.at[0:batch]
        refs.h_second_low = refs.mixed.at[0:batch, 0 : tower.width]
        refs.h_query_low = refs.h_normed
        refs.h_queries = refs.attlow.at[0:batch]
        refs.h_direction = refs.h_grad.at[:, 0 : tower.weights.projection.shape[1]]
        refs.h_unit = refs.att.at[0:batch]
    r.grouped = r.vall
    places = Places()
    me = places.me
    step = Step((image, caption), r, places)
    routes = (
        (None, r.vall, 24, 1),
        (caption.shards.attend, caption.weights.attend, 0, 0),
        (caption.shards.output, caption.weights.output, 0, 1),
        (image.shards.attend, image.weights.attend, r.sib_attend, 0),
        (image.shards.output, image.weights.output, r.sib_output, 1),
        (image.shards.expand, image.weights.expand, r.sib_expand, 0),
        (image.shards.projection, image.weights.projection, r.sib_projection, 1),
        (None, r.middles, 8, 0),
        (None, r.queries, 16, 1),
        (image.shards.reduce, image.weights.reduce, 0, 0),
        (caption.shards.projection, caption.weights.projection, 0, 1),
        (caption.shards.expand, caption.weights.expand, 0, 0),
        (caption.shards.reduce, caption.weights.reduce, 0, 1),
        (None, r.query_grads, 16, 0),
    )
    items, pairs = [], {}
    for number, (shard, whole, other, odd) in enumerate(routes):
        if shard is None:
            items.append(Item(whole, other, odd))
            continue
        paired = not isinstance(other, int)
        if paired:
            pairs[number] = other
        items.append(Item(whole, shard.shape[0], odd, paired))
    spread = Spread(places, items, r.near_sem, r.core_sem, r.send_sem)

    barrier = pltpu.get_barrier_semaphore()
    loop(
        BOX - 1,
        lambda k: pl.semaphore_signal(
            barrier, inc=1, device_id=(lax.rem(me + 1 + k, BOX),), device_id_type=MESH
        ),
    )
    step.pack_vectors()
    pl.semaphore_wait(barrier, BOX - 1)

    pair_copies = {}
    for k, (number, other) in enumerate(pairs.items()):
        pair_copies[number] = pltpu.make_async_remote_copy(
            src_ref=routes[number][0],
            dst_ref=other,
            send_sem=r.pair_sem.at[0, k],
            recv_sem=r.pair_sem.at[1, k],
            device_id=(spread.sibling,),
            device_id_type=MESH,
        )
        pair_copies[number].start()
    for number, (shard, whole, other, _) in enumerate(routes):
        if number in pairs:
            pair_copies[number].wait()
            step.join_pair(shard, other, whole)
        elif shard is not None:
            step.place_own(shard, whole)
        if number == Route.vectors or shard is not None:
            spread.start(number)

    queue = []
    for turn in range(Route.query_grads + 2):
        for stage in range(3):
            if 0 <= turn - stage < Route.query_grads:
                queue += [(turn - stage, key) for key in spread.keys(stage)]

    held = [Route.middles, Route.queries]

    def serve(count=None):
        count = PACE if count is None else count
        for _ in range(count):
            ready = [entry for entry in queue if entry[0] not in held]
            if ready:
                queue.remove(ready[0])
                spread.pass_on(*ready[0])

    def need(number):
        while any(entry[0] == number for entry in queue):
            serve(1)
        spread.wait(number)

    step.pause = serve
    serve(3)
    for work in (
        lambda: step.load_tokens(caption),
        lambda: step.load_tokens(image),
        lambda: step.masks(image),
        lambda: step.masks(caption),
    ):
        work()
        serve(3)
    r.squares[...] = jnp.zeros_like(r.squares)
    need(Route.vectors)
    for tower in (caption, image):
        step.unpack_vectors(tower)
        step.norm_tokens(tower, tower.refs.x, tower.refs.normed, Row.norm_gain, Row.norm_bias)
    need(Route.caption_attend)
    step.mix(caption)
    step.attend(caption)
    need(Route.caption_output)
    step.project(caption)
    need(Route.image_attend)
    step.mix(image)
    step.attend(image)
    need(Route.image_output)
    step.project(image)
    picked = []
    for tower in (image, caption):
        picked.append(step.picked_forward(tower))
        serve(3)
    mine = pl.ds(pl.multiple_of(me * 8, 8), 8)
    r.middles[mine, :] = jnp.concatenate([rows for rows, _ in picked], 1)
    queries = jnp.concatenate([rows for _, rows in picked], 1)
    half = queries.shape[1] // 2
    wide_mine = pl.ds(pl.multiple_of(me * 16, 16), 16)
    r.queries[wide_mine, :] = jnp.concatenate([queries[:, :half], queries[:, half:]], 0).astype(BF16)
    spread.start(Route.middles)
    rest = [entry for entry in queue if entry[0] not in held]
    late = [(Route.middles, key) for stage in range(3) for key in spread.keys(stage)]
    queue.clear()
    for place, entry in enumerate(rest):
        queue.append(entry)
        if place % LATE_EVERY == 0 and place >= LATE_FROM and late:
            queue.append(late.pop(0))
    queue += late
    held.clear()
    for tower in (image, caption):
        step.norm_tokens(
            tower, tower.refs.middle, tower.refs.normed_two, Row.second_gain, Row.second_bias
        )
    need(Route.image_expand)
    step.own_active(image)
    need(Route.middles)
    step.head_hidden(image)
    need(Route.image_reduce)
    need(Route.image_projection)
    step.head_vectors(image)
    step.turn_head(image)
    serve()
    step.own_second(image)
    need(Route.caption_expand)
    step.head_hidden(caption)
    step.own_active(caption)
    need(Route.caption_reduce)
    need(Route.caption_projection)
    spread.start(Route.queries)
    swap_sem = r.swap_sem
    for k, tower in enumerate((image, caption)):
        out, met = tower.refs.factor_out, tower.refs.t_met
        swap_out(me, BOX, lambda d, out=out: out.at[d], met, swap_sem.at[0, k], swap_sem.at[1, k])
    step.head_vectors(caption)
    queue += [(Route.queries, key) for stage in range(3) for key in spread.keys(stage)]
    step.pause = lambda count=2: None
    step.contrast()
    serve(3)
    step.head_backward(image)
    serve(8)
    step.head_backward(caption)
    serve(4)
    for k, tower in enumerate((image, caption)):
        swap_descriptor(me, BOX, tower.refs.t_met, swap_sem.at[0, k], swap_sem.at[1, k]).wait()
    queue += [(Route.query_grads, key) for stage in range(3) for key in spread.keys(stage)]
    grads = jnp.concatenate([step.local_backward(tower) for tower in (image, caption)], 1)
    r.query_grads[wide_mine, :] = jnp.concatenate([grads[:, :half], grads[:, half:]], 0).astype(BF16)
    spread.start(Route.query_grads)
    for k, tower in enumerate((image, caption), 2):
        out, met = tower.refs.factor_out, tower.refs.s_met
        swap_out(me, BOX, lambda d, out=out: out.at[d], met, swap_sem.at[0, k], swap_sem.at[1, k])
    step.own_second(caption)
    serve(3)
    squares = r.squares
    r.squares_met[me] = squares[...]
    swap_out(me, BOX, lambda d: squares, r.squares_met, swap_sem.at[0, 4], swap_sem.at[1, 4])
    step.turn_head(caption)
    step.head_gradients(caption)
    serve(8)
    step.head_gradients(image)
    serve(4)
    spread.wait(Route.queries)
    spread.finish(Route.vectors)
    for tower in (image, caption):
        refs = tower.refs
        step.input_gradient(tower)
        step.regroup(tower, refs.t_met)
        step.output_gradient(tower)
        refs.normed_terms[...] = step.group_terms(tower, tower.heads)
        step.factor_gradient(tower, refs.h_grad, 2)
        step.unpack_rows(tower, r.queries, refs.h_queries, 0.125)
    for k, tower in enumerate((image, caption), 2):
        swap_descriptor(me, BOX, tower.refs.s_met, swap_sem.at[0, k], swap_sem.at[1, k]).wait()
    for tower in (image, caption):
        step.regroup(tower, tower.refs.s_met)
        step.factor_gradient(tower, tower.refs.h_queries, 1)
    spread.wait(Route.query_grads)
    for tower in (image, caption):
        step.query_gradient(tower)
    swap_descriptor(me, BOX, r.squares_met, swap_sem.at[0, 4], swap_sem.at[1, 4]).wait()
    totals = jnp.sum(r.squares_met[...], 0)
    slot = iota((8, 128), 0)
    cells = jnp.where(
        slot < 3,
        1.0 / (BOX * image.tokens * image.width),
        1.0 / (BOX * caption.tokens * caption.width),
    )
    means = jnp.sqrt(jnp.sum(totals, 1, keepdims=True) * cells)
    diagonal = jnp.where(slot == iota((8, 128), 1), means, 0.0)
    r.out_rms[...] = column_sum(diagonal)[0, :6]
    for number in range(1, len(items)):
        spread.finish(number)


def tower_scratch(tower, embed):
    width, hidden, rows, batch = tower.width, tower.hidden, tower.rows, tower.batch
    return dict(
        vectors=((8, width), F32),
        attend_vector=((8, 2 * width), F32),
        expand_vector=((8, hidden), F32),
        mixed_bias=((8, 3 * width), F32),
        sums=((8, width), F32),
        value_sums=((8, width), F32),
        norm_sums=((8, width), F32),
        bias_sums=((8, 2 * width), F32),
        expand_sums=((8, hidden), F32),
        x=((rows, width), F32),
        normed=((rows, width), BF16),
        mixed=((rows, 3 * width), BF16),
        att=((rows, width), F32),
        attlow=((rows, width), BF16),
        mask=((len(tower.windows), tower.window, tower.window), F32),
        soft=((rows, tower.terms), F32),
        qe=((tower.terms, width), BF16),
        factor_out=((BOX, tower.mine, 128), BF16),
        t_met=((BOX, tower.mine, 128), BF16),
        s_met=((BOX, tower.mine, 128), BF16),
        normed_terms=((tower.mine, batch), BF16),
        turned_final=((tower.mine, batch), BF16),
        turned_normed=((tower.mine, batch), BF16),
        turned_active=((hidden // BOX, batch), BF16),
        h_normed=((batch, width), BF16),
        h_hidden=((batch, hidden), F32),
        h_active=((batch, hidden), BF16),
        h_hidden_low=((batch, hidden), BF16),
        h_inverse=((batch, 1), F32),
        h_final=((batch, width), BF16),
        h_scaling=((batch, 1), F32),
        h_vectors=((batch, embed), BF16),
        h_raw=((batch, embed), BF16),
        h_grad=((batch, width), F32),
        h_middle_grad=((batch, width), F32),
    )


def step_on_box(images, captions, caption_ends, image_shards, caption_shards, logit_scale):
    image_in, caption_in = SimpleNamespace(**image_shards), SimpleNamespace(**caption_shards)
    image = Tower(True, *images.shape, image_in.expand.shape[1], images.shape[0])
    caption = Tower(False, *captions.shape, caption_in.expand.shape[1], 2 * captions.shape[0])
    both = image.width + caption.width
    count = Route.query_grads + 1
    shared = dict(
        vpack=((24, 128), F32),
        vall=((BOX * 24, 128), F32),
        middles=((BOX * 8, both), F32),
        queries=((BOX * 16, both // 2), BF16),
        query_grads=((BOX * 16, both // 2), BF16),
        squares=((8, 128), F32),
        squares_met=((BOX, 8, 128), F32),
        active=((image.rows, image.hidden), BF16),
        row_low=((image.batch, image.batch), BF16),
        column_low=((image.batch, image.batch), BF16),
        score_low=((image.rows, image.terms), BF16),
        soft_low=((image.rows, image.terms), BF16),
        wide_grad=((image.terms, image.width), BF16),
        placement=((image.rows, image.picks), F32),
        sib_attend=(image_in.attend.shape, BF16),
        sib_output=(image_in.output.shape, BF16),
        sib_projection=(image_in.projection.shape, BF16),
        sib_expand=(image_in.expand.shape, BF16),
    )
    semaphores = dict(near_sem=(count, 16), core_sem=(count,), send_sem=(count,), pair_sem=(2, 4), swap_sem=(2, 5))
    towers, shards = (image, caption), (image_shards, caption_shards)
    local = [tower_scratch(tower, image_in.projection.shape[1]) for tower in towers]

    def kernel(*refs):
        refs = iter(refs)

        def take(names):
            return SimpleNamespace(**{name: next(refs) for name in names})

        tokens = [next(refs), next(refs)]
        for tower in towers:
            tower.shards = take(NAMES)
        ends, logit_ref, out_loss, out_rms = [next(refs) for _ in range(4)]
        out_tokens = [next(refs), next(refs)]
        for tower in towers:
            tower.outs = take(NAMES)
        out_scale = next(refs)
        r = take(shared)
        for k, tower in enumerate(towers):
            tower.weights = take(MATRICES)
            tower.refs = take(local[k])
            tower.refs.tokens, tower.refs.out_tokens = tokens[k], out_tokens[k]
        for name in semaphores:
            setattr(r, name, next(refs))
        r.ends, r.logit_scale = ends, logit_ref
        r.out_loss, r.out_rms, r.out_scale = out_loss, out_rms, out_scale
        step_kernel(image, caption, r)

    scratch = [pltpu.VMEM(*spec) for spec in shared.values()]
    for own, specs in zip(shards, local):
        scratch += [pltpu.VMEM((BOX * own[name].shape[0], own[name].shape[1]), BF16) for name in MATRICES]
        scratch += [pltpu.VMEM(*spec) for spec in specs.values()]
    scratch += [pltpu.SemaphoreType.DMA(shape) for shape in semaphores.values()]
    weights = [own[name] for own in shards for name in NAMES]
    tokens = [jnp.swapaxes(images, 0, 1), jnp.swapaxes(captions, 0, 1)]
    outputs = [((1,), F32), ((6,), F32)] + [(array.shape, BF16) for array in tokens]
    outputs += [(array.shape, F32) for array in weights] + [((1,), F32)]
    vmem, smem = pl.BlockSpec(memory_space=pltpu.VMEM), pl.BlockSpec(memory_space=pltpu.SMEM)
    shapes = [jax.ShapeDtypeStruct(*spec) for spec in outputs]
    results = pl.pallas_call(
        kernel,
        out_shape=shapes,
        in_specs=[vmem] * (2 + len(weights)) + [smem] * 2,
        out_specs=[vmem] * len(outputs),
        scratch_shapes=scratch,
        compiler_params=pltpu.CompilerParams(
            collective_id=0, has_side_effects=True, vmem_limit_bytes=VMEM_LIMIT
        ),
        name="contrastive_step",
    )(*tokens, *weights, caption_ends.T, logit_scale)

    def hand_over(*refs):
        sems = refs[-1]
        pairs = zip(refs[: len(shapes)], refs[len(shapes) : -1])
        copies = [pltpu.make_async_copy(*pair, sems.at[k]) for k, pair in enumerate(pairs)]
        for copy in copies:
            copy.start()
        for copy in copies:
            copy.wait()

    anywhere = pl.BlockSpec(memory_space=pl.ANY)
    results = pl.pallas_call(
        hand_over,
        out_shape=shapes,
        in_specs=[anywhere] * len(shapes),
        out_specs=[vmem] * len(shapes),
        scratch_shapes=[pltpu.SemaphoreType.DMA((len(shapes),))],
        compiler_params=pltpu.CompilerParams(vmem_limit_bytes=VMEM_LIMIT),
        name="hand_over",
    )(*results)
    tokens = [jnp.swapaxes(rows, 0, 1) for rows in results[2:4]]
    return (*results[:2], *tokens, *results[4:])


def solution(mesh):
    rows, matrix, cube = P("dp"), P("dp", None), P("dp", None, None)
    weights = tuple(rows if name in VECTORS else matrix for name in NAMES)
    return jax.shard_map(
        per_device,
        mesh=mesh,
        in_specs=(cube, cube, matrix) + weights + weights + (P(),),
        out_specs=(P(), P(), cube, cube) + weights + weights + (P(),),
        check_vma=False,
    )
```

```python
from types import SimpleNamespace

import jax
import jax.numpy as jnp
from jax import lax
from jax.experimental import pallas as pl
from jax.experimental.pallas import tpu as pltpu
from jax.sharding import PartitionSpec as P

HD = 64
F32 = jnp.float32
BF16 = jnp.bfloat16


def product(left, right):
    return jnp.dot(left, right, preferred_element_type=F32)


def left_product(left, right):
    return lax.dot_general(left, right, (((0,), (0,)), ((), ())), preferred_element_type=F32)


def right_product(left, right):
    return lax.dot_general(left, right, (((1,), (1,)), ((), ())), preferred_element_type=F32)


def unit_norm(rows):
    centred = rows - jnp.mean(rows, -1, keepdims=True)
    inverse = lax.rsqrt(jnp.mean(centred * centred, -1, keepdims=True) + 1e-05)
    return centred * inverse, inverse


def norm_inward(upstream, unit_rows, inverse, gain):
    scaled = upstream * gain
    return inverse * (
        scaled
        - jnp.mean(scaled, -1, keepdims=True)
        - unit_rows * jnp.mean(scaled * unit_rows, -1, keepdims=True)
    )


def caption_allowed(end_rows, length):
    places = jnp.arange(length, dtype=jnp.int32)
    pieces = (places[None, :] >= end_rows[:, 0:1]).astype(jnp.int32) + (
        places[None, :] >= end_rows[:, 1:2]
    ).astype(jnp.int32)
    living = places[None, :] < end_rows[:, 1:2]
    same_piece = pieces[:, :, None] == pieces[:, None, :]
    causal = places[:, None] >= places[None, :]
    diagonal = places[:, None] == places[None, :]
    return same_piece & causal[None] & living[:, None, :] | diagonal[None]


def spread_heads(rows):
    count, width = rows.shape
    heads = width // HD
    head = jnp.arange(heads)[:, None, None]
    lane_head = jnp.arange(width)[None, None, :] // HD
    return jnp.where(head == lane_head, rows[None], jnp.zeros((), rows.dtype)).reshape(
        heads * count, width
    )


def fold_heads(rows, count):
    total, width = rows.shape
    heads = width // HD
    head = jnp.arange(heads)[:, None, None]
    lane_head = jnp.arange(width)[None, None, :] // HD
    return jnp.sum(jnp.where(head == lane_head, rows.reshape(heads, count, width), 0.0), 0)


def local_forward(inputs, allowed, mine, pick_rows, weights):
    sequences, length, width = inputs.shape
    heads = width // HD
    stream = inputs.reshape(sequences * length, width).astype(F32)
    unit_one, inverse_one = unit_norm(stream)
    normed = (unit_one * weights.norm_gain + weights.norm_bias).astype(BF16)
    bias = weights.attend_bias
    bias_full = jnp.concatenate([bias[:width], jnp.zeros((width,), F32), bias[width:]])
    mixed = (product(normed, weights.attend) + bias_full).astype(BF16)
    queries, keys, values = mixed[:, :width], mixed[:, width : 2 * width], mixed[:, 2 * width :]
    split = lambda rows: rows.reshape(sequences, length, heads, HD)
    scores = jnp.einsum("sqhd,skhd->shqk", split(queries), split(keys), preferred_element_type=F32)
    scores = scores / 8.0
    if allowed is not None:
        scores = jnp.where(allowed[:, None], scores, -1e30)
    softened = jax.nn.softmax(scores, axis=-1).astype(BF16)
    attended = jnp.einsum("shqk,skhd->sqhd", softened, split(values), preferred_element_type=F32)
    attended = attended.astype(BF16).reshape(sequences * length, width)
    branch = product(attended, weights.output) + weights.output_bias
    middle = stream + branch
    unit_two, _ = unit_norm(middle)
    normed_two = (unit_two * weights.second_gain + weights.second_bias).astype(BF16)
    hidden = product(normed_two, weights.expand) + weights.expand_bias
    active = (hidden * jax.nn.sigmoid(1.702 * hidden)).astype(BF16)
    second = product(active, weights.reduce) + weights.reduce_bias
    result = middle + second
    squares = jnp.stack([jnp.sum(branch * branch), jnp.sum(second * second), jnp.sum(result * result)])
    picked_queries = queries[pick_rows]
    picked_scores = right_product(keys, spread_heads(picked_queries)) / 8.0
    seen = jnp.tile(mine, (1, heads))
    picked_scores = jnp.where(seen, picked_scores, -1e30)
    soft = jax.nn.softmax(picked_scores, axis=0)
    return SimpleNamespace(
        squares=squares,
        unit_one=unit_one,
        inverse_one=inverse_one,
        normed=normed,
        keys=keys,
        values=values,
        soft=soft,
        value_factor=left_product(normed, soft.astype(BF16)).astype(BF16),
        middle_rows=middle[pick_rows],
        attended_rows=attended[pick_rows],
        normed_rows=normed[pick_rows],
        query_rows=picked_queries,
    )


def head_forward(middle, weights):
    unit_two, inverse_two = unit_norm(middle)
    normed_two = (unit_two * weights.second_gain + weights.second_bias).astype(BF16)
    hidden = product(normed_two, weights.expand) + weights.expand_bias
    active = (hidden * jax.nn.sigmoid(1.702 * hidden)).astype(BF16)
    result = middle + (product(active, weights.reduce) + weights.reduce_bias)
    unit_final, inverse_final = unit_norm(result)
    head_normed = (unit_final * weights.final_gain + weights.final_bias).astype(BF16)
    raw_embed = product(head_normed, weights.projection)
    scaling = lax.rsqrt(jnp.sum(raw_embed * raw_embed, -1, keepdims=True) + 1e-06)
    direction = raw_embed * scaling
    kept = (unit_two, inverse_two, normed_two, hidden, active, unit_final, inverse_final, head_normed)
    return direction.astype(BF16), direction, scaling, kept


def head_backward(upstream, direction, scaling, kept, weights):
    unit_two, inverse_two, normed_two, hidden, active, unit_final, inverse_final, head_normed = kept
    raw_low = (
        scaling * (upstream - direction * jnp.sum(upstream * direction, -1, keepdims=True))
    ).astype(BF16)
    head_grad = right_product(raw_low, weights.projection)
    result_grad = norm_inward(head_grad, unit_final, inverse_final, weights.final_gain)
    second_low = result_grad.astype(BF16)
    gate = jax.nn.sigmoid(1.702 * hidden)
    hidden_low = (
        right_product(second_low, weights.reduce) * (gate + 1.702 * hidden * gate * (1.0 - gate))
    ).astype(BF16)
    two_grad = right_product(hidden_low, weights.expand)
    middle_grad = result_grad + norm_inward(two_grad, unit_two, inverse_two, weights.second_gain)
    branch_low = middle_grad.astype(BF16)
    attended_grad = right_product(branch_low, weights.output).astype(BF16)
    sums = SimpleNamespace(
        final_gain=jnp.sum(head_grad * unit_final, 0),
        final_bias=jnp.sum(head_grad, 0),
        reduce_bias=jnp.sum(second_low.astype(F32), 0),
        expand_bias=jnp.sum(hidden_low.astype(F32), 0),
        second_gain=jnp.sum(two_grad * unit_two, 0),
        second_bias=jnp.sum(two_grad, 0),
        output_bias=jnp.sum(branch_low.astype(F32), 0),
    )
    factors = SimpleNamespace(
        projection=(head_normed, raw_low),
        reduce=(active, second_low),
        expand=(normed_two, hidden_low),
    )
    return middle_grad, branch_low, attended_grad, sums, factors


def local_backward(kept, mine, pick_rows, middle_grad_rows, attended_grad_rows, weights):
    width = weights.output.shape[0]
    count = pick_rows.shape[0]
    heads = width // HD
    wide_grad = spread_heads(attended_grad_rows)
    soft = kept.soft
    soft_grad = right_product(kept.values, wide_grad)
    score_low = (soft * (soft_grad - jnp.sum(soft_grad * soft, 0, keepdims=True))).astype(BF16)
    query_grad = (fold_heads(left_product(score_low, kept.keys), count) / 8.0).astype(BF16)
    key_factor = left_product(kept.normed, score_low).astype(BF16)
    attend = weights.attend
    key_side = right_product(spread_heads(kept.query_rows), attend[:, width : 2 * width]) / 8.0
    value_side = right_product(wide_grad, attend[:, 2 * width :])
    query_side = right_product(query_grad, attend[:, :width])
    normed_grad = product(score_low, key_side.astype(BF16)) + product(
        soft.astype(BF16), value_side.astype(BF16)
    )
    normed_grad = normed_grad.at[pick_rows].add(query_side)
    inward = norm_inward(normed_grad, kept.unit_one, kept.inverse_one, weights.norm_gain)
    input_grad = inward.at[pick_rows].add(middle_grad_rows)
    gain_grad = jnp.sum(normed_grad * kept.unit_one, 0)
    bias_grad = jnp.sum(normed_grad, 0)
    return input_grad, query_grad, key_factor, gain_grad, bias_grad


def my_columns(rows, size, index):
    return lax.dynamic_slice_in_dim(rows, index * size, size, rows.ndim - 1)


NAMES = (
    "norm_gain",
    "norm_bias",
    "attend",
    "attend_bias",
    "output",
    "output_bias",
    "second_gain",
    "second_bias",
    "expand",
    "expand_bias",
    "reduce",
    "reduce_bias",
    "final_gain",
    "final_bias",
    "projection",
)
VECTORS = tuple(name for name in NAMES if name[-4:] in ("bias", "gain"))


MATRICES = (NAMES[2], NAMES[4], NAMES[8], NAMES[10], NAMES[14])
PAIRED = (NAMES[2], NAMES[4], NAMES[8], NAMES[14])
VMEM_LIMIT = 65000 << 10


def gather(rows):
    return lax.all_gather(rows, "dp", axis=0, tiled=True)


def exchange(rows, devices):
    width, terms = rows.shape
    blocks = rows.reshape(devices, width // devices, terms)
    return lax.all_to_all(blocks, "dp", 0, 0)


def gather_weights(shards):
    devices = lax.axis_size("dp")
    whole = {}
    wide = PAIRED
    block = gather(jnp.concatenate([shards[name] for name in wide], 1))
    start = 0
    for name in wide:
        size = shards[name].shape[1]
        whole[name] = block[:, start : start + size]
        start += size
    whole[MATRICES[3]] = gather(shards[MATRICES[3]])
    flat = jnp.concatenate([shards[name] for name in VECTORS])
    flat = gather(flat[None].astype(F32))
    start = 0
    for name in VECTORS:
        size = shards[name].shape[0]
        whole[name] = flat[:, start : start + size].reshape(devices * size)
        start += size
    return SimpleNamespace(**whole)


def per_device(images, captions, caption_ends, *rest):
    image_shards = dict(zip(NAMES, rest[:15]))
    caption_shards = dict(zip(NAMES, rest[15:30]))
    logit_scale = rest[30]
    devices = lax.axis_size("dp")
    if (devices, images.shape, captions.shape) == (BOX, (8, 50, 768), (4, 77, 512)):
        return step_on_box(
            images, captions, caption_ends, image_shards, caption_shards, logit_scale
        )
    index = lax.axis_index("dp")
    image_weights = gather_weights(image_shards)
    caption_weights = gather_weights(caption_shards)
    image_count, patches, image_width = images.shape
    row_count, row_length, caption_width = captions.shape
    batch = devices * image_count

    image_tokens = jnp.arange(image_count * patches, dtype=jnp.int32)
    image_picks = jnp.arange(image_count, dtype=jnp.int32) * patches
    image_mine = image_tokens[:, None] // patches == jnp.arange(image_count)[None, :]
    image_kept = local_forward(images, None, image_mine, image_picks, image_weights)

    caption_tokens = jnp.arange(row_count * row_length, dtype=jnp.int32)[:, None]
    row_start = jnp.arange(row_count, dtype=jnp.int32)[:, None] * row_length
    caption_picks = (row_start + caption_ends - 1).reshape(row_count * 2)
    starts = row_start + jnp.concatenate([jnp.zeros((row_count, 1), jnp.int32), caption_ends[:, :1]], 1)
    caption_mine = (caption_tokens >= starts.reshape(1, -1)) & (caption_tokens <= caption_picks[None, :])
    allowed = caption_allowed(caption_ends, row_length)
    caption_kept = local_forward(captions, allowed, caption_mine, caption_picks, caption_weights)

    towers = (
        (image_kept, image_weights, image_mine, image_picks, image_count),
        (caption_kept, caption_weights, caption_mine, caption_picks, row_count * 2),
    )
    middle_all = gather(jnp.concatenate([image_kept.middle_rows, caption_kept.middle_rows], 1))
    low_rows = []
    for kept in (image_kept, caption_kept):
        low_rows += [kept.attended_rows, kept.normed_rows, kept.query_rows]
    low_all = gather(jnp.concatenate(low_rows, 1))
    widths = (image_width, caption_width)
    middles = (middle_all[:, :image_width], middle_all[:, image_width:])
    lows = []
    start = 0
    for width in widths:
        lows.append(tuple(low_all[:, start + j * width : start + (j + 1) * width] for j in range(3)))
        start += 3 * width

    image_vectors, image_direction, image_scaling, image_head = head_forward(middles[0], image_weights)
    caption_vectors, caption_direction, caption_scaling, caption_head = head_forward(
        middles[1], caption_weights
    )
    scale = jnp.exp(logit_scale[0])
    logits = scale * right_product(image_vectors, caption_vectors)
    places = jnp.arange(batch, dtype=jnp.int32)
    one_hot = (places[:, None] == places[None, :]).astype(F32)
    row_top = jnp.max(logits, 1, keepdims=True)
    row_lse = row_top + jnp.log(jnp.sum(jnp.exp(logits - row_top), 1, keepdims=True))
    col_top = jnp.max(logits, 0, keepdims=True)
    col_lse = col_top + jnp.log(jnp.sum(jnp.exp(logits - col_top), 0, keepdims=True))
    diagonal = jnp.sum(logits * one_hot)
    factor = 1.0 / (2.0 * batch)
    loss = (jnp.sum(row_lse) + jnp.sum(col_lse) - 2.0 * diagonal) * factor
    row_grad = (jnp.exp(logits - row_lse) - one_hot) * factor
    col_grad = (jnp.exp(logits - col_lse) - one_hot) * factor
    scale_grad = jnp.sum(row_grad * logits) + jnp.sum(col_grad * logits)
    row_low = (scale * row_grad).astype(BF16)
    col_low = (scale * col_grad).astype(BF16)
    image_vec_grad = product(row_low, caption_vectors) + product(col_low, caption_vectors)
    caption_vec_grad = left_product(col_low, image_vectors) + left_product(row_low, image_vectors)

    backs = (
        head_backward(image_vec_grad, image_direction, image_scaling, image_head, image_weights),
        head_backward(caption_vec_grad, caption_direction, caption_scaling, caption_head, caption_weights),
    )
    input_grads, query_grads, key_factors, norm_sums = [], [], [], []
    for (kept, weights, mine, picks, count), back in zip(towers, backs):
        mine_of = lambda rows: lax.dynamic_slice_in_dim(rows, index * count, count, 0)
        input_grad, query_grad, key_factor, gain_grad, bias_grad = local_backward(
            kept, mine, picks, mine_of(back[0]), mine_of(back[2]), weights
        )
        input_grads.append(input_grad)
        query_grads.append(query_grad)
        key_factors.append(key_factor)
        norm_sums.extend((gain_grad, bias_grad))

    query_all = gather(jnp.concatenate(query_grads, 1))
    query_all = (query_all[:, :image_width], query_all[:, image_width:])
    sums = jnp.concatenate([image_kept.squares, caption_kept.squares] + norm_sums)
    sums = lax.psum(sums, "dp")
    square_sums = sums[:6]
    norm_totals = []
    start = 6
    for width in (image_width, image_width, caption_width, caption_width):
        norm_totals.append(sums[start : start + width])
        start += width

    shards = []
    for tower in range(2):
        kept, weights, _, _, count = towers[tower]
        _, branch_low, attended_grad, head_sums, factors = backs[tower]
        width = widths[tower]
        size = width // devices
        heads = width // HD
        attended_all, normed_all, queries_all = lows[tower]
        columns = lambda rows: my_columns(rows, rows.shape[-1] // devices, index)
        query_block = left_product(columns(normed_all), query_all[tower])
        blocks = [query_block]
        for factor_rows, side in ((key_factors[tower], queries_all), (kept.value_factor, attended_grad)):
            met = exchange(factor_rows, devices).reshape(devices, size, heads, count)
            side = side.reshape(devices, count, heads, HD)
            blocks.append(
                jnp.einsum("sfhi,sihd->fhd", met, side, preferred_element_type=F32).reshape(size, width)
            )
        blocks[1] = blocks[1] / 8.0
        bias_wide = jnp.concatenate(
            [
                jnp.sum(query_all[tower].astype(F32), 0),
                jnp.sum(attended_grad.astype(F32), 0),
            ]
        )
        shards.extend(
            (
                columns(norm_totals[2 * tower]),
                columns(norm_totals[2 * tower + 1]),
                jnp.concatenate(blocks, 1),
                columns(bias_wide),
                left_product(columns(attended_all), branch_low),
                columns(head_sums.output_bias),
                columns(head_sums.second_gain),
                columns(head_sums.second_bias),
                left_product(columns(factors.expand[0]), factors.expand[1]),
                columns(head_sums.expand_bias),
                left_product(columns(factors.reduce[0]), factors.reduce[1]),
                columns(head_sums.reduce_bias),
                columns(head_sums.final_gain),
                columns(head_sums.final_bias),
                left_product(columns(factors.projection[0]), factors.projection[1]),
            )
        )
    image_cells = float(batch * patches * image_width)
    caption_cells = float(devices * row_count * row_length * caption_width)
    cells = jnp.array([image_cells] * 3 + [caption_cells] * 3, F32)
    return (
        loss.reshape(1),
        jnp.sqrt(square_sums / cells),
        input_grads[0].reshape(images.shape).astype(BF16),
        input_grads[1].reshape(captions.shape).astype(BF16),
        *shards,
        scale_grad.reshape(1),
    )


MESH = pl.DeviceIdType.MESH
BOX = 32


class Tower:
    def __init__(self, is_image, sequences, length, width, hidden, picks):
        self.is_image, self.sequences, self.length = is_image, sequences, length
        self.width, self.hidden = width, hidden
        self.heads = width // HD
        self.picks = picks
        self.tokens = sequences * length
        self.rows = -(-self.tokens // 80) * 80
        self.terms = self.heads * picks
        self.batch = BOX * picks
        self.mine = width // BOX
        self.vector_rows = (0, 8, 9) if is_image else (16, 10, 11)
        if is_image:
            self.window = 112
            self.windows = [(96 * j, 100 * j, 100 * j + 100) for j in range(sequences // 2)]
        else:
            self.window = 96
            self.windows = [
                (length * j // 16 * 16, length * j, length * (j + 1)) for j in range(sequences)
            ]


def iota(shape, axis):
    return lax.broadcasted_iota(jnp.int32, shape, axis)


def dot(left, right, over=((1,), (0,)), precision=None):
    return lax.dot_general(
        left, right, (over, ((), ())), preferred_element_type=F32, precision=precision
    )


ROWS_BY_COLUMNS = ((1,), (1,))
COLUMNS_BY_COLUMNS = ((0,), (0,))
HIGHEST = lax.Precision.HIGHEST


UNROLL = 1
PACE = 2
LATE_EVERY = 2
LATE_FROM = 6


def loop(count, body):
    lax.fori_loop(0, count, lambda step, carry: (body(step), carry)[1], 0, unroll=min(count, UNROLL))


def rows_at(step, size):
    return pl.ds(pl.multiple_of(step * size, size), size)


def centred_unit(rows):
    width = rows.shape[-1]
    centred = rows - jnp.sum(rows, -1, keepdims=True) * (1.0 / width)
    inverse = lax.rsqrt(jnp.sum(centred * centred, -1, keepdims=True) * (1.0 / width) + 1e-05)
    return centred * inverse, inverse


def inward_of(upstream, unit_rows, inverse, gain):
    width = upstream.shape[-1]
    scaled = upstream * gain
    mean = jnp.sum(scaled, -1, keepdims=True) * (1.0 / width)
    slope = jnp.sum(scaled * unit_rows, -1, keepdims=True) * (1.0 / width)
    return inverse * (scaled - mean - unit_rows * slope)


def gate_of(hidden):
    return 0.5 * jnp.tanh(0.851 * hidden) + 0.5


def column_sum(rows):
    return jnp.sum(rows, 0, keepdims=True)


def spread_rows(rows, heads):
    lane_head = jnp.right_shift(iota(rows.shape, 1), 6)
    return jnp.concatenate([jnp.where(lane_head == h, rows, 0.0) for h in range(heads)], 0).astype(BF16)


def fold_rows(rows, heads, picks):
    lane_head = jnp.right_shift(iota((picks, rows.shape[1]), 1), 6)
    total = jnp.zeros((picks, rows.shape[1]), F32)
    for h in range(heads):
        total = total + jnp.where(lane_head == h, rows[h * picks : (h + 1) * picks], 0.0)
    return total


WIDTH_VECTORS = tuple(name for name in VECTORS if name not in (NAMES[3], NAMES[9]))


class Row:
    norm_gain, norm_bias, output_bias, second_gain, second_bias, reduce_bias, final_gain, final_bias = range(8)


class Places:
    def __init__(self):
        self.me = lax.axis_index("dp")
        self.core = lax.rem(self.me, 2)
        self.x = lax.rem(self.me // 2, 2)
        self.y = lax.rem(self.me // 4, 2)
        self.z = self.me // 8

    def device(self, ahead, across_y, across_x, other):
        z = lax.rem(self.z + ahead, 4)
        y = self.y + across_y - 2 * self.y * across_y
        x = self.x + across_x - 2 * self.x * across_x
        core = self.core + other - 2 * self.core * other
        return ((z * 2 + y) * 2 + x) * 2 + core


class Item:
    def __init__(self, target, size, odd, paired=False):
        self.target, self.size, self.odd, self.paired = target, size, odd, paired
        self.sent = 0


class Spread:
    def __init__(self, places, items, near_sem, core_sem, send_sem):
        self.places, self.items = places, items
        self.near_sem, self.core_sem, self.send_sem = near_sem, core_sem, send_sem
        self.x_next = places.device(0, 0, 1, 0)
        self.y_next = places.device(0, 1, 0, 0)
        self.sibling = places.device(0, 0, 0, 1)
        self.z_next = [None] + [places.device(step, 0, 0, 0) for step in (1, 2, 3)]

    def block(self, number, key):
        item = self.items[number]
        ahead, across_y, across_x = key
        owner = self.places.device((4 - ahead) % 4, across_y, across_x, 0)
        if item.paired:
            half = item.target.shape[1] // 2
            rows = pl.ds(pl.multiple_of((owner // 2) * (2 * item.size), 2 * item.size), 2 * item.size)
            return item.target.at[rows, pl.ds(pl.multiple_of(self.places.core * half, 128), half)]
        return item.target.at[pl.ds(pl.multiple_of(owner * item.size, item.size), item.size)]

    def send(self, number, key, device, sem):
        block = self.block(number, key)
        pltpu.make_async_remote_copy(
            src_ref=block,
            dst_ref=block,
            send_sem=self.send_sem.at[number],
            recv_sem=sem,
            device_id=(device,),
            device_id_type=MESH,
        ).start()
        self.items[number].sent += 1

    def near(self, number, key):
        ahead, across_y, across_x = key
        return self.near_sem.at[number, ahead * 4 + across_y * 2 + across_x]

    def forward(self, number, key):
        ahead, across_y, across_x = key
        item = self.items[number]
        if (across_y, across_x) == (0, 0):
            if ahead == 0:
                for step in (1, 2, 3):
                    self.send(number, key, self.z_next[step], self.near(number, (step, 0, 0)))
            self.send(number, key, self.x_next, self.near(number, (ahead, 0, 1)))
            self.send(number, key, self.y_next, self.near(number, (ahead, 1, 0)))
        elif (across_y, across_x) == (0, 1) and ahead % 2 == item.odd:
            self.send(number, key, self.y_next, self.near(number, (ahead, 1, 1)))
        elif (across_y, across_x) == (1, 0) and ahead % 2 != item.odd:
            self.send(number, key, self.x_next, self.near(number, (ahead, 1, 1)))
        if not (item.paired and key == (0, 0, 0)):
            self.send(number, key, self.sibling, self.core_sem.at[number])

    def whole(self, ref, number, sem):
        return pltpu.make_async_remote_copy(
            src_ref=ref,
            dst_ref=ref,
            send_sem=self.send_sem.at[number],
            recv_sem=sem,
            device_id=(self.sibling,),
            device_id_type=MESH,
        )

    def start(self, number):
        self.forward(number, (0, 0, 0))

    def keys(self, stage):
        return (
            [(step, 0, 0) for step in (1, 2, 3)],
            [(step, *side) for step in range(4) for side in ((0, 1), (1, 0))],
            [(step, 1, 1) for step in range(4)],
        )[stage]

    def pass_on(self, number, key):
        self.whole(self.block(number, key), number, self.near(number, key)).wait_recv()
        self.forward(number, key)

    def wait(self, number):
        item = self.items[number]
        if item.paired:
            ref = item.target.at[pl.ds(0, 30 * item.size), pl.ds(0, item.target.shape[1] // 2)]
        else:
            ref = item.target.at[pl.ds(0, 16 * item.size)]
        self.whole(ref, number, self.core_sem.at[number]).wait_recv()

    def finish(self, number):
        item = self.items[number]
        ref = item.target.at[pl.ds(0, item.sent * item.size)]
        self.whole(ref, number, self.core_sem.at[number]).wait_send()


def fraction_floor(numbers, divisor):
    return jnp.floor((numbers.astype(F32) + 0.5) * (1.0 / divisor))


def columns_at(step, size):
    if isinstance(step, int):
        return slice(step * size, step * size + size)
    return pl.ds(pl.multiple_of(step * size, size), size)


class Step:
    def __init__(self, towers, r, places):
        self.towers, self.r, self.places = towers, r, places
        self.me = places.me

    def vector(self, tower, row):
        return tower.refs.vectors[row : row + 1, :]

    def pause(self, count=None):
        pass

    def paced(self, count, body, group=3):
        for first in range(0, count, group):
            loop(min(group, count - first), lambda step, first=first: body(first + step))
            self.pause()


    def pack_vectors(self):
        r = self.r
        pack = r.vpack
        pack[...] = jnp.zeros_like(pack)
        for tower in self.towers:
            first, attend_row, expand_row = tower.vector_rows
            shards = tower.shards
            rows = [(first + k, getattr(shards, name)) for k, name in enumerate(WIDTH_VECTORS)]
            for row, source in rows + [(attend_row, shards.attend_bias), (expand_row, shards.expand_bias)]:
                pack[row : row + 1, 0 : source.shape[0]] = source[...].astype(F32)[None, :]
        r.vall[pl.ds(pl.multiple_of(self.me * 24, 8), 24)] = pack[...]

    def place_own(self, shard, whole):
        size = shard.shape[0]
        whole[pl.ds(pl.multiple_of(self.me * size, size), size)] = shard[...]

    def join_pair(self, shard, other, whole):
        size = shard.shape[0]
        rows = pl.ds(pl.multiple_of((self.me // 2) * (2 * size), 2 * size), 2 * size)
        first = self.places.core == 0

        def body(step):
            columns = columns_at(step, 256)
            own, met = shard[:, columns].astype(F32), other[:, columns].astype(F32)
            both = jnp.concatenate([jnp.where(first, own, met), jnp.where(first, met, own)], 0)
            whole[rows, columns] = both.astype(BF16)

        loop(shard.shape[1] // 256, body)

    def unpack_vectors(self, tower):
        r = self.r
        first, attend_row, expand_row = tower.vector_rows
        width, hidden = tower.width, tower.hidden
        for row, size, target in (
            (first, width // BOX, tower.refs.vectors),
            (attend_row, 2 * width // BOX, tower.refs.attend_vector),
            (expand_row, hidden // BOX, tower.refs.expand_vector),
        ):
            group = row // 8 * 8
            blocks = r.vall[...].reshape(BOX, 24, 128)[:, group : group + 8, :]
            blocks = blocks.reshape(BOX * 8, 128).astype(BF16)
            chunk = 256

            def body(step, row=row, size=size, blocks=blocks, target=target):
                lane = iota((1, chunk), 1) + step * chunk
                owner = fraction_floor(lane, size)
                within = lane.astype(F32) - owner * size
                spread = (iota((128, chunk), 0).astype(F32) == within).astype(F32).astype(BF16)
                met = dot(blocks, spread).reshape(BOX, 8, chunk)
                device = iota((BOX, 8, chunk), 0).astype(F32)
                total = jnp.sum(jnp.where(device == owner.reshape(1, 1, chunk), met, 0.0), 0)
                if target is tower.refs.vectors:
                    target[:, columns_at(step, chunk)] = total
                else:
                    target[0:1, columns_at(step, chunk)] = total[row % 8 : row % 8 + 1]

            loop(target.shape[1] // chunk, body)
            self.pause()
        bias = tower.refs.mixed_bias
        bias[0:1, 0:width] = tower.refs.attend_vector[0:1, 0:width]
        bias[0:1, width : 2 * width] = jnp.zeros((1, width), F32)
        bias[0:1, 2 * width :] = tower.refs.attend_vector[0:1, width:]

    def load_tokens(self, tower):
        source, rows = tower.refs.tokens, tower.refs.x
        if tower.rows > tower.tokens:
            low = tower.tokens // 8 * 8
            rows[low:, :] = jnp.zeros((tower.rows - low, tower.width), F32)
        for number in range(tower.sequences):
            start = number * tower.length
            rows[start : start + tower.length, :] = source[:, number, :].astype(F32)

    def norm_tokens(self, tower, source, target, gain, bias):
        gain, bias = self.vector(tower, gain), self.vector(tower, bias)

        def body(step):
            rows = rows_at(step, 80)
            unit, _ = centred_unit(source[rows, :])
            target[rows, :] = (unit * gain + bias).astype(BF16)

        loop(tower.rows // 80, body)
        self.pause()


    def mix(self, tower):
        normed, mixed = tower.refs.normed, tower.refs.mixed
        weight, bias = tower.weights.attend, tower.refs.mixed_bias

        def body(step):
            columns = columns_at(step, 256)
            mixed[:, columns] = (dot(normed[...], weight[:, columns]) + bias[0:1, columns]).astype(BF16)

        self.paced(3 * tower.width // 256, body)

    def masks(self, tower):
        bias = tower.refs.mask
        side = tower.window
        query, key = iota((side, side), 1), iota((side, side), 0)
        for number, (row, _, _) in enumerate(tower.windows):
            if tower.is_image:
                allowed = fraction_floor(query + row, tower.length) == fraction_floor(
                    key + row, tower.length
                )
            else:
                first, second = self.r.ends[0, number], self.r.ends[1, number]
                query_place, key_place = [
                    place + (row - number * tower.length) for place in (query, key)
                ]

                def piece(place):
                    return jnp.where(place >= first, 1, 0) + jnp.where(place >= second, 1, 0)

                allowed = (
                    (piece(query_place) == piece(key_place))
                    & (query_place >= key_place)
                    & (key_place < second)
                    & (key_place >= 0)
                    & (query_place < tower.length)
                ) | (query == key)
            bias[number] = jnp.where(allowed, 0.0, -1e30)

    def attend(self, tower):
        width, side = tower.width, tower.window
        mixed, total, bias = tower.refs.mixed, tower.refs.att, tower.refs.mask
        total[...] = jnp.zeros_like(total)

        def body(step, windows):
            lane = iota((1, 128), 1)
            left = jnp.where(lane < HD, 1.0, 0.0)
            sides = (left.astype(BF16), (1.0 - left).astype(BF16))
            for number in windows:
                row, first, last = tower.windows[number]
                rows = slice(row, row + side)
                query, key, value = [
                    mixed[rows, columns_at(step + part * (width // 128), 128)] for part in range(3)
                ]
                out = []
                for half in sides:
                    scores = dot(key * half, query, ROWS_BY_COLUMNS) * 0.125 + bias[number]
                    weights = jnp.exp(scores - jnp.max(scores, 0, keepdims=True))
                    weights = weights * (1.0 / column_sum(weights))
                    out.append(dot(weights.astype(BF16), value, COLUMNS_BY_COLUMNS))
                both = jnp.where(lane < HD, out[0], out[1])
                place = iota((side, 1), 0) + row
                kept = jnp.where((place >= first) & (place < last), 1.0, 0.0)
                columns = columns_at(step, 128)
                total[rows, columns] = total[rows, columns] + both * kept

        for pair in range(0, width // 128, 2):
            for first in range(0, len(tower.windows), 2):
                loop(2, lambda step, pair=pair, first=first: body(pair + step, (first, first + 1)))
                self.pause(2 * PACE + 1)
        low = tower.refs.attlow

        def narrow(step):
            low[rows_at(step, 80), :] = total[rows_at(step, 80), :].astype(BF16)

        loop(tower.rows // 80, narrow)

    def add_square(self, slot, rows, tower):
        if tower.rows > tower.tokens:
            rows = jnp.where(iota((rows.shape[0], 1), 0) < tower.tokens, rows, 0.0)
        squares = column_sum(rows * rows)
        width = squares.shape[1]
        folded = sum(squares[:, k * 128 : (k + 1) * 128] for k in range(width // 128))
        self.r.squares[slot : slot + 1, :] = self.r.squares[slot : slot + 1, :] + folded

    def project(self, tower):
        stream, middle, low = tower.refs.x, tower.refs.middle, tower.refs.attlow
        weight = tower.weights.output
        slot = 0 if tower.is_image else 3
        bias_row = Row.output_bias

        def body(step):
            columns = columns_at(step, 256)
            bias = tower.refs.vectors[bias_row : bias_row + 1, columns]
            branch = dot(low[...], weight[:, columns]) + bias
            middle[:, columns] = stream[:, columns] + branch
            self.add_square(slot, branch, tower)

        loop(tower.width // 256, body)
        self.pause()

    def own_active(self, tower):
        rows = slice(0, tower.rows)
        normed, active = tower.refs.normed_two, self.r.active
        weight, bias = tower.weights.expand, tower.refs.expand_vector

        def body(step):
            columns = columns_at(step, 256)
            hidden = dot(normed[...], weight[:, columns]) + bias[0:1, columns]
            active[rows, columns] = (hidden * gate_of(hidden)).astype(BF16)

        self.paced(tower.hidden // 256, body, 2)

    def own_second(self, tower):
        rows = slice(0, tower.rows)
        active, middle, weight = self.r.active, tower.refs.middle, tower.weights.reduce
        slot = 1 if tower.is_image else 4
        bias_row = Row.reduce_bias

        def body(step):
            columns = columns_at(step, 256)
            bias = tower.refs.vectors[bias_row : bias_row + 1, columns]
            second = dot(active[rows, 0 : tower.hidden], weight[:, columns]) + bias
            self.add_square(slot, second, tower)
            self.add_square(slot + 1, second + middle[:, columns], tower)

        self.paced(tower.width // 256, body, 1)


    def pick_places(self, tower):
        if tower.is_image:
            return [(i * tower.length, i * tower.length) for i in range(tower.picks)]
        places = []
        for i in range(tower.picks):
            start, ends = (i // 2) * tower.length, self.r.ends
            first = start + (ends[0, i // 2] if i % 2 else 0)
            places.append((first, start + ends[i % 2, i // 2] - 1))
        return places

    def selection(self, tower):
        row = iota((tower.picks, 1), 0)
        token = jnp.zeros((tower.picks, 1), jnp.int32)
        for i, (_, pick) in enumerate(self.pick_places(tower)):
            token = jnp.where(row == i, pick, token)
        return jnp.where(iota((tower.picks, tower.rows), 1) == token, 1.0, 0.0)

    def placement(self, tower):
        lane = iota((1, tower.picks), 1)
        token = jnp.zeros((1, tower.picks), jnp.int32)
        for i, (_, pick) in enumerate(self.pick_places(tower)):
            token = jnp.where(lane == i, pick, token)
        return jnp.where(iota((tower.rows, tower.picks), 0) == token, 1.0, 0.0)

    def picked_forward(self, tower):
        width, heads, terms, picks = tower.width, tower.heads, tower.terms, tower.picks
        select = self.selection(tower)
        low_select = select.astype(BF16)
        mixed, normed = tower.refs.mixed, tower.refs.normed
        queries = dot(low_select, mixed[:, 0:width])
        middle_rows = dot(select, tower.refs.middle[...], precision=HIGHEST)
        normed_rows = dot(low_select, normed[...])
        attended_rows = dot(low_select, tower.refs.attlow[...])
        wide = spread_rows(queries, heads)
        tower.refs.qe[...] = wide
        scores = dot(mixed[:, width : 2 * width], wide, ROWS_BY_COLUMNS) * 0.125
        lane = jnp.bitwise_and(iota((1, terms), 1), picks - 1)
        first = jnp.zeros((1, terms), jnp.int32)
        last = jnp.zeros((1, terms), jnp.int32)
        for i, (begin, pick) in enumerate(self.pick_places(tower)):
            first = jnp.where(lane == i, begin, first)
            last = jnp.where(lane == i, pick, last)
        if tower.is_image:
            last = first + (tower.length - 1)
        place = iota((tower.rows, terms), 0)
        scores = jnp.where((place >= first) & (place <= last), scores, -1e30)
        soft = jnp.exp(scores - jnp.max(scores, 0, keepdims=True))
        soft = soft * (1.0 / column_sum(soft))
        tower.refs.soft[...] = soft
        factor = dot(soft.astype(BF16), normed[...], COLUMNS_BY_COLUMNS)
        pad = jnp.zeros((128 - terms - 2 * picks, width), F32)
        rows = jnp.concatenate([factor, normed_rows, attended_rows, pad], 0)
        self.store_factor(tower, tower.refs.t_met, rows)
        return middle_rows, queries

    def store_factor(self, tower, met, rows):
        blocks = rows.T.reshape(BOX, tower.mine, 128).astype(BF16)
        tower.refs.factor_out[...] = blocks
        met[self.me] = tower.refs.factor_out[self.me]


    def head_middle(self, tower, rows):
        start = 0 if tower.is_image else self.towers[0].width
        return self.r.middles[rows, start : start + tower.width]

    def head_hidden(self, tower):
        normed = tower.refs.h_normed
        gain, bias = self.vector(tower, Row.second_gain), self.vector(tower, Row.second_bias)

        def norm(step):
            rows = rows_at(step, 64)
            unit, _ = centred_unit(self.head_middle(tower, rows))
            normed[rows, :] = (unit * gain + bias).astype(BF16)

        loop(tower.batch // 64, norm)
        weight, expand_bias = tower.weights.expand, tower.refs.expand_vector
        hidden_ref, active = tower.refs.h_hidden, tower.refs.h_active

        def body(step):
            columns = columns_at(step, 256)
            hidden = dot(normed[...], weight[:, columns]) + expand_bias[0:1, columns]
            hidden_ref[:, columns] = hidden
            active[:, columns] = (hidden * gate_of(hidden)).astype(BF16)

        self.paced(tower.hidden // 256, body, 3)

    def head_vectors(self, tower):
        result, active = tower.refs.h_unit, tower.refs.h_active
        weight = tower.weights.reduce
        bias_row = Row.reduce_bias
        start = 0 if tower.is_image else self.towers[0].width

        def body(step):
            columns = columns_at(step, 256)
            bias = tower.refs.vectors[bias_row : bias_row + 1, columns]
            middle = self.r.middles[:, pl.ds(pl.multiple_of(start + step * 256, 256), 256)]
            result[:, columns] = middle + (dot(active[...], weight[:, columns]) + bias)

        self.paced(tower.width // 256, body, 1)
        gain, bias = self.vector(tower, Row.final_gain), self.vector(tower, Row.final_bias)
        inverse_ref, normed = tower.refs.h_inverse, tower.refs.h_final

        def norm(step):
            rows = rows_at(step, 64)
            unit, inverse = centred_unit(result[rows, :])
            result[rows, :] = unit
            inverse_ref[rows, :] = inverse
            normed[rows, :] = (unit * gain + bias).astype(BF16)

        loop(tower.batch // 64, norm)
        self.pause()

        def embed(step):
            rows = rows_at(step, 64)
            raw = dot(normed[rows, :], tower.weights.projection[...])
            scaling = lax.rsqrt(jnp.sum(raw * raw, -1, keepdims=True) + 1e-06)
            direction = raw * scaling
            tower.refs.h_scaling[rows, :] = scaling
            tower.refs.h_direction[rows, :] = direction
            tower.refs.h_vectors[rows, :] = direction.astype(BF16)

        loop(tower.batch // 64, embed)

    def contrast(self):
        image, caption = self.towers
        batch = image.batch
        vectors, others = image.refs.h_vectors[...], caption.refs.h_vectors[...]
        scale = jnp.exp(jnp.full((1, 1), self.r.logit_scale[0], F32))
        logits = scale * dot(vectors, others, ROWS_BY_COLUMNS)
        same = jnp.where(iota((batch, batch), 0) == iota((batch, batch), 1), 1.0, 0.0)
        row_top = jnp.max(logits, 1, keepdims=True)
        row_lse = row_top + jnp.log(jnp.sum(jnp.exp(logits - row_top), 1, keepdims=True))
        column_top = jnp.max(logits, 0, keepdims=True)
        column_lse = column_top + jnp.log(column_sum(jnp.exp(logits - column_top)))

        def whole_sum(rows):
            return jnp.sum(column_sum(rows), 1, keepdims=True)

        factor = 1.0 / (2.0 * batch)
        loss = (
            whole_sum(row_lse) + whole_sum(column_lse) - 2.0 * whole_sum(logits * same)
        ) * factor
        row_grad = (jnp.exp(logits - row_lse) - same) * factor
        column_grad = (jnp.exp(logits - column_lse) - same) * factor
        scale_grad = whole_sum(row_grad * logits) + whole_sum(column_grad * logits)
        self.r.out_loss[...] = loss[0, :]
        self.r.out_scale[...] = scale_grad[0, :]
        row_low, column_low = self.r.row_low, self.r.column_low
        row_low[...] = (scale * row_grad).astype(BF16)
        column_low[...] = (scale * column_grad).astype(BF16)

        def image_side(step):
            rows = rows_at(step, 64)
            others = caption.refs.h_vectors[...]
            self.raw_grad(image, rows, dot(row_low[rows, :], others) + dot(column_low[rows, :], others))

        def caption_side(step):
            rows = rows_at(step, 128)
            others = image.refs.h_vectors[...]
            upstream = dot(column_low[:, rows], others, COLUMNS_BY_COLUMNS)
            upstream = upstream + dot(row_low[:, rows], others, COLUMNS_BY_COLUMNS)
            self.raw_grad(caption, rows, upstream)

        loop(batch // 64, image_side)
        loop(batch // 128, caption_side)

    def raw_grad(self, tower, rows, upstream):
        direction = tower.refs.h_direction[rows, :]
        along = jnp.sum(upstream * direction, -1, keepdims=True)
        raw = tower.refs.h_scaling[rows, :] * (upstream - direction * along)
        tower.refs.h_raw[rows, :] = raw.astype(BF16)

    def add_sum(self, tower, slot, row):
        sums = tower.refs.sums
        sums[slot : slot + 1, :] = sums[slot : slot + 1, :] + row

    def against(self, tower, source, weight, target):
        def body(step):
            target[:, columns_at(step, 256)] = dot(
                source[...], weight[rows_at(step, 256), :], ROWS_BY_COLUMNS
            )

        loop(tower.width // 256, body)

    def head_backward(self, tower):
        grad, result_grad = tower.refs.h_grad, tower.refs.h_middle_grad
        unit_ref, inverse_ref = tower.refs.h_unit, tower.refs.h_inverse
        second_low = tower.refs.h_second_low
        tower.refs.sums[...] = jnp.zeros_like(tower.refs.sums)
        self.against(tower, tower.refs.h_raw, tower.weights.projection, grad)
        gain = self.vector(tower, Row.final_gain)

        def final_norm(step):
            rows = rows_at(step, 64)
            upstream, unit = grad[rows, :], unit_ref[rows, :]
            inward = inward_of(upstream, unit, inverse_ref[rows, :], gain)
            low = inward.astype(BF16)
            result_grad[rows, :] = inward
            second_low[rows, :] = low
            self.add_sum(tower, Row.final_gain, column_sum(upstream * unit))
            self.add_sum(tower, Row.final_bias, column_sum(upstream))
            self.add_sum(tower, Row.reduce_bias, column_sum(low.astype(F32)))

        loop(tower.batch // 64, final_norm)
        weight, hidden_ref = tower.weights.reduce, tower.refs.h_hidden
        hidden_low, expand_sums = tower.refs.h_hidden_low, tower.refs.expand_sums

        def body(step):
            columns = columns_at(step, 256)
            active_grad = dot(second_low[...], weight[rows_at(step, 256), :], ROWS_BY_COLUMNS)
            hidden = hidden_ref[:, columns]
            gate = gate_of(hidden)
            low = (active_grad * (gate + 1.702 * hidden * gate * (1.0 - gate))).astype(BF16)
            hidden_low[:, columns] = low
            expand_sums[0:1, columns] = column_sum(low.astype(F32))

        loop(tower.hidden // 256, body)
        self.against(tower, hidden_low, tower.weights.expand, grad)
        second_gain, branch_low = self.vector(tower, Row.second_gain), tower.refs.h_branch_low

        def second_norm(step):
            rows = rows_at(step, 64)
            upstream = grad[rows, :]
            unit, inverse = centred_unit(self.head_middle(tower, rows))
            inward = result_grad[rows, :] + inward_of(upstream, unit, inverse, second_gain)
            low = inward.astype(BF16)
            result_grad[rows, :] = inward
            branch_low[rows, :] = low
            self.add_sum(tower, Row.second_gain, column_sum(upstream * unit))
            self.add_sum(tower, Row.second_bias, column_sum(upstream))
            self.add_sum(tower, Row.output_bias, column_sum(low.astype(F32)))

        loop(tower.batch // 64, second_norm)
        self.against(tower, branch_low, tower.weights.output, grad)

        def narrow(step):
            rows = rows_at(step, 64)
            low = grad[rows, :].astype(BF16).astype(F32)
            grad[rows, :] = low
            tower.refs.value_sums[0:1, :] = tower.refs.value_sums[0:1, :] + column_sum(low)

        tower.refs.value_sums[...] = jnp.zeros_like(tower.refs.value_sums)
        loop(tower.batch // 64, narrow)


    def local_backward(self, tower):
        width, heads, picks, terms = tower.width, tower.heads, tower.picks, tower.terms
        mine = pl.ds(pl.multiple_of(self.me * picks, picks), picks)
        wide_grad = spread_rows(tower.refs.h_grad[mine, :], heads)
        mixed, normed = tower.refs.mixed, tower.refs.normed
        soft = tower.refs.soft[...]
        soft_grad = dot(mixed[:, 2 * width :], wide_grad, ROWS_BY_COLUMNS)
        score_low = (soft * (soft_grad - column_sum(soft_grad * soft))).astype(BF16)
        query_grad = fold_rows(
            dot(score_low, mixed[:, width : 2 * width], COLUMNS_BY_COLUMNS), heads, picks
        )
        query_low = (query_grad * 0.125).astype(BF16)
        attend = tower.weights.attend
        scores_ref, soft_low, wide_ref = self.r.score_low, self.r.soft_low, self.r.wide_grad
        scores_ref[0 : tower.rows, 0:terms] = score_low
        soft_low[0 : tower.rows, 0:terms] = soft.astype(BF16)
        wide_ref[0:terms, 0:width] = wide_grad
        placement = self.r.placement
        placement[0 : tower.rows, :] = self.placement(tower)
        queries = tower.refs.qe

        def sides(step):
            rows = rows_at(step, 256)
            key_side = dot(queries[...], attend[rows, width : 2 * width], ROWS_BY_COLUMNS) * 0.125
            value_side = dot(wide_ref[0:terms, 0:width], attend[rows, 2 * width :], ROWS_BY_COLUMNS)
            query_side = dot(query_low, attend[rows, 0:width], ROWS_BY_COLUMNS)
            tower.refs.att[:, rows] = (
                dot(scores_ref[0 : tower.rows, 0:terms], key_side.astype(BF16))
                + dot(soft_low[0 : tower.rows, 0:terms], value_side.astype(BF16))
                + dot(placement[0 : tower.rows, :], query_side, precision=HIGHEST)
            )

        loop(width // 256, sides)
        key_factor = dot(score_low, normed[...], COLUMNS_BY_COLUMNS)
        gain = self.vector(tower, Row.norm_gain)
        source, grad = tower.refs.tokens, tower.refs.att
        sums = tower.refs.norm_sums
        sums[...] = jnp.zeros_like(sums)
        for number in range(tower.sequences):
            rows = slice(number * tower.length, (number + 1) * tower.length)
            upstream = grad[rows, :]
            unit, inverse = centred_unit(source[:, number, :].astype(F32))
            grad[rows, :] = inward_of(upstream, unit, inverse, gain)
            sums[0:1, :] = sums[0:1, :] + column_sum(upstream * unit)
            sums[1:2, :] = sums[1:2, :] + column_sum(upstream)
        pad = jnp.zeros((128 - terms - 8, width), F32)
        self.store_factor(tower, tower.refs.s_met, jnp.concatenate([key_factor, sums[...], pad], 0))
        return query_low.astype(F32)

    def input_gradient(self, tower):
        mine = pl.ds(pl.multiple_of(self.me * tower.picks, tower.picks), tower.picks)
        grad, out = tower.refs.att, tower.refs.out_tokens
        placement = self.r.placement
        placement[0 : tower.rows, :] = self.placement(tower)

        def add(step):
            columns = columns_at(step, 256)
            middle_grad = tower.refs.h_middle_grad[mine, columns]
            placed = dot(placement[0 : tower.rows, :], middle_grad, precision=HIGHEST)
            grad[:, columns] = grad[:, columns] + placed

        loop(tower.width // 256, add)
        for number in range(tower.sequences):
            start = number * tower.length
            out[:, number, :] = grad[start : start + tower.length, :].astype(BF16)


    def my_columns(self, total, size):
        return jnp.where(iota((size, total), 1) == iota((size, total), 0) + self.me * size, 1.0, 0.0)

    def turned_columns(self, source, size):
        pick = self.my_columns(source.shape[1], size).astype(BF16)
        return dot(pick, source[...], ROWS_BY_COLUMNS).astype(BF16)

    def gradient_blocks(self, left, right, out):
        step_size = 256

        def body(step):
            columns = columns_at(step, step_size)
            out[:, columns] = dot(left, right[:, columns])

        loop(right.shape[1] // step_size, body)

    def turn_head(self, tower):
        refs, size = tower.refs, tower.mine
        refs.turned_normed[...] = self.turned_columns(refs.h_normed, size)
        refs.turned_active[...] = self.turned_columns(refs.h_active, tower.hidden // BOX)
        refs.turned_final[...] = self.turned_columns(refs.h_final, size)

    def head_gradients(self, tower):
        size = tower.mine
        self.gradient_blocks(
            tower.refs.turned_final[...],
            tower.refs.h_raw,
            tower.outs.projection,
        )
        self.gradient_blocks(
            tower.refs.turned_active[...],
            tower.refs.h_second_low,
            tower.outs.reduce,
        )
        self.gradient_blocks(
            tower.refs.turned_normed[...],
            tower.refs.h_hidden_low,
            tower.outs.expand,
        )
        pick = self.my_columns(tower.width, size)
        sums = dot(tower.refs.sums[...], pick, ROWS_BY_COLUMNS, HIGHEST)
        for k, name in enumerate(WIDTH_VECTORS[2:], 2):
            getattr(tower.outs, name)[...] = sums[k, :]
        pick = self.my_columns(tower.hidden, tower.hidden // BOX)
        tower.outs.expand_bias[...] = dot(
            tower.refs.expand_sums[...], pick, ROWS_BY_COLUMNS, HIGHEST
        )[0, :]

    def regroup(self, tower, met):
        grouped, size = self.r.grouped, tower.mine
        lane = jnp.right_shift(iota((size, 128), 1), 3)

        def body(tile):
            blocks = [met[tile * 16 + k].astype(F32) for k in range(16)]
            for span in (1, 2, 4, 8):
                low = jnp.bitwise_and(lane, span) == 0
                for k in range(16):
                    if k & span:
                        continue
                    first, second = blocks[k], blocks[k + span]
                    blocks[k] = jnp.where(low, first, pltpu.roll(second, 8 * span, 1))
                    blocks[k + span] = jnp.where(low, pltpu.roll(first, 128 - 8 * span, 1), second)
            for group, block in enumerate(blocks):
                start = (tile * 16 + group) * size
                grouped[pl.ds(pl.multiple_of(start, 8), size), :] = block

        loop(BOX // 16, body)

    def group_terms(self, tower, group, count=1):
        size, tiles = tower.mine, []
        for tile in range(BOX // 16):
            start = (tile * 16 + group) * size
            tiles.append(self.r.grouped[start : start + count * size, :])
        return jnp.concatenate(tiles, 1).astype(BF16)

    def output_gradient(self, tower):
        self.gradient_blocks(
            self.group_terms(tower, tower.heads + 1), tower.refs.h_branch_low, tower.outs.output
        )

    def factor_gradient(self, tower, side, part):
        size, width = tower.mine, tower.width
        left = self.group_terms(tower, 0, tower.heads)

        def body(step):
            columns = columns_at(step, 128)
            met = dot(left, side[:, columns].astype(BF16))
            lane = jnp.right_shift(iota((size, 128), 1), 6)
            total = jnp.zeros((size, 128), F32)
            for head in range(tower.heads):
                mine = lane + 2 * step == head
                total = total + jnp.where(mine, met[head * size : (head + 1) * size], 0.0)
            out = pl.ds(pl.multiple_of(part * width + step * 128, 128), 128)
            tower.outs.attend[:, out] = total

        loop(width // 128, body)

    def rows_of_pair(self, tower, ref, device):
        block = ref[pl.ds(pl.multiple_of(device * 16, 16), 16), :].astype(F32)
        rows = jnp.concatenate([block[0:8], block[8:16]], 1)
        start = 0 if tower.is_image else self.towers[0].width
        return rows[:, start : start + tower.width]

    def unpack_rows(self, tower, source, target, scale):
        for device in range(0, BOX, 2):
            pair = [self.rows_of_pair(tower, source, device + k) for k in range(2)]
            target[device * 8 : device * 8 + 16, :] = (jnp.concatenate(pair, 0) * scale).astype(BF16)

    def query_gradient(self, tower):
        r, size, width = self.r, tower.mine, tower.width
        rows = tower.refs.h_query_low
        self.unpack_rows(tower, r.query_grads, rows, 1.0)
        tower.outs.attend[:, 0:width] = dot(tower.refs.normed_terms[...], rows[...])
        bias = tower.refs.bias_sums
        bias[0:1, 0:width] = column_sum(rows[...].astype(F32))
        bias[0:1, width:] = tower.refs.value_sums[0:1, :]
        pick = self.my_columns(2 * width, 2 * size)
        tower.outs.attend_bias[...] = dot(bias[...], pick, ROWS_BY_COLUMNS, HIGHEST)[0, :]
        total = jnp.zeros((size, 128), F32)
        met = tower.refs.s_met
        for device in range(BOX):
            total = total + met[device].astype(F32)
        lane = iota((8, 128), 1)
        row = iota((8, 128), 0)
        pick = jnp.where(lane == row + tower.terms, 1.0, 0.0)
        sums = dot(pick, total, ROWS_BY_COLUMNS, HIGHEST)
        tower.outs.norm_gain[...] = sums[0, :]
        tower.outs.norm_bias[...] = sums[1, :]


class Route:
    (
        vectors,
        caption_attend,
        caption_output,
        image_attend,
        image_output,
        image_expand,
        image_projection,
        middles,
        queries,
        image_reduce,
        caption_projection,
        caption_expand,
        caption_reduce,
        query_grads,
    ) = range(14)


def swap_out(me, count, source_of, target, send_sem, recv_sem):
    def body(step):
        device = lax.rem(me + 1 + step, count)
        pltpu.make_async_remote_copy(
            src_ref=source_of(device),
            dst_ref=target.at[me],
            send_sem=send_sem,
            recv_sem=recv_sem,
            device_id=(device,),
            device_id_type=MESH,
        ).start()

    loop(count - 1, body)


def swap_descriptor(me, count, target, send_sem, recv_sem):
    most = target.at[pl.ds(0, count - 1)]
    return pltpu.make_async_remote_copy(
        src_ref=most,
        dst_ref=most,
        send_sem=send_sem,
        recv_sem=recv_sem,
        device_id=(lax.rem(me + 1, count),),
        device_id_type=MESH,
    )


def step_kernel(image, caption, r):
    for tower in (image, caption):
        refs, batch = tower.refs, tower.batch
        refs.middle = refs.x
        refs.normed_two = refs.mixed.at[:, 0 : tower.width]
        refs.h_branch_low = refs.attlow.at[0:batch]
        refs.h_second_low = refs.mixed.at[0:batch, 0 : tower.width]
        refs.h_query_low = refs.h_normed
        refs.h_queries = refs.attlow.at[0:batch]
        refs.h_direction = refs.h_grad.at[:, 0 : tower.weights.projection.shape[1]]
        refs.h_unit = refs.att.at[0:batch]
    r.grouped = r.vall
    places = Places()
    me = places.me
    step = Step((image, caption), r, places)
    routes = (
        (None, r.vall, 24, 1),
        (caption.shards.attend, caption.weights.attend, 0, 0),
        (caption.shards.output, caption.weights.output, 0, 1),
        (image.shards.attend, image.weights.attend, r.sib_attend, 0),
        (image.shards.output, image.weights.output, r.sib_output, 1),
        (image.shards.expand, image.weights.expand, r.sib_expand, 0),
        (image.shards.projection, image.weights.projection, r.sib_projection, 1),
        (None, r.middles, 8, 0),
        (None, r.queries, 16, 1),
        (image.shards.reduce, image.weights.reduce, 0, 0),
        (caption.shards.projection, caption.weights.projection, 0, 1),
        (caption.shards.expand, caption.weights.expand, 0, 0),
        (caption.shards.reduce, caption.weights.reduce, 0, 1),
        (None, r.query_grads, 16, 0),
    )
    items, pairs = [], {}
    for number, (shard, whole, other, odd) in enumerate(routes):
        if shard is None:
            items.append(Item(whole, other, odd))
            continue
        paired = not isinstance(other, int)
        if paired:
            pairs[number] = other
        items.append(Item(whole, shard.shape[0], odd, paired))
    spread = Spread(places, items, r.near_sem, r.core_sem, r.send_sem)

    barrier = pltpu.get_barrier_semaphore()
    loop(
        BOX - 1,
        lambda k: pl.semaphore_signal(
            barrier, inc=1, device_id=(lax.rem(me + 1 + k, BOX),), device_id_type=MESH
        ),
    )
    step.pack_vectors()
    pl.semaphore_wait(barrier, BOX - 1)

    pair_copies = {}
    for k, (number, other) in enumerate(pairs.items()):
        pair_copies[number] = pltpu.make_async_remote_copy(
            src_ref=routes[number][0],
            dst_ref=other,
            send_sem=r.pair_sem.at[0, k],
            recv_sem=r.pair_sem.at[1, k],
            device_id=(spread.sibling,),
            device_id_type=MESH,
        )
        pair_copies[number].start()
    for number, (shard, whole, other, _) in enumerate(routes):
        if number in pairs:
            pair_copies[number].wait()
            step.join_pair(shard, other, whole)
        elif shard is not None:
            step.place_own(shard, whole)
        if number == Route.vectors or shard is not None:
            spread.start(number)

    queue = []
    for turn in range(Route.query_grads + 2):
        for stage in range(3):
            if 0 <= turn - stage < Route.query_grads:
                queue += [(turn - stage, key) for key in spread.keys(stage)]

    held = [Route.middles, Route.queries]

    def serve(count=None):
        count = PACE if count is None else count
        for _ in range(count):
            ready = [entry for entry in queue if entry[0] not in held]
            if ready:
                queue.remove(ready[0])
                spread.pass_on(*ready[0])

    def need(number):
        while any(entry[0] == number for entry in queue):
            serve(1)
        spread.wait(number)

    step.pause = serve
    serve(3)
    for work in (
        lambda: step.load_tokens(caption),
        lambda: step.load_tokens(image),
        lambda: step.masks(image),
        lambda: step.masks(caption),
    ):
        work()
        serve(3)
    r.squares[...] = jnp.zeros_like(r.squares)
    need(Route.vectors)
    for tower in (caption, image):
        step.unpack_vectors(tower)
        step.norm_tokens(tower, tower.refs.x, tower.refs.normed, Row.norm_gain, Row.norm_bias)
    need(Route.caption_attend)
    step.mix(caption)
    step.attend(caption)
    need(Route.caption_output)
    step.project(caption)
    need(Route.image_attend)
    step.mix(image)
    step.attend(image)
    need(Route.image_output)
    step.project(image)
    picked = []
    for tower in (image, caption):
        picked.append(step.picked_forward(tower))
        serve(3)
    mine = pl.ds(pl.multiple_of(me * 8, 8), 8)
    r.middles[mine, :] = jnp.concatenate([rows for rows, _ in picked], 1)
    queries = jnp.concatenate([rows for _, rows in picked], 1)
    half = queries.shape[1] // 2
    wide_mine = pl.ds(pl.multiple_of(me * 16, 16), 16)
    r.queries[wide_mine, :] = jnp.concatenate([queries[:, :half], queries[:, half:]], 0).astype(BF16)
    spread.start(Route.middles)
    rest = [entry for entry in queue if entry[0] not in held]
    late = [(Route.middles, key) for stage in range(3) for key in spread.keys(stage)]
    queue.clear()
    for place, entry in enumerate(rest):
        queue.append(entry)
        if place % LATE_EVERY == 0 and place >= LATE_FROM and late:
            queue.append(late.pop(0))
    queue += late
    held.clear()
    for tower in (image, caption):
        step.norm_tokens(
            tower, tower.refs.middle, tower.refs.normed_two, Row.second_gain, Row.second_bias
        )
    need(Route.image_expand)
    step.own_active(image)
    need(Route.middles)
    step.head_hidden(image)
    need(Route.image_reduce)
    need(Route.image_projection)
    step.head_vectors(image)
    step.turn_head(image)
    serve()
    step.own_second(image)
    need(Route.caption_expand)
    step.head_hidden(caption)
    step.own_active(caption)
    need(Route.caption_reduce)
    need(Route.caption_projection)
    spread.start(Route.queries)
    swap_sem = r.swap_sem
    for k, tower in enumerate((image, caption)):
        out, met = tower.refs.factor_out, tower.refs.t_met
        swap_out(me, BOX, lambda d, out=out: out.at[d], met, swap_sem.at[0, k], swap_sem.at[1, k])
    step.head_vectors(caption)
    queue += [(Route.queries, key) for stage in range(3) for key in spread.keys(stage)]
    step.pause = lambda count=2: None
    step.contrast()
    serve(3)
    step.head_backward(image)
    serve(8)
    step.head_backward(caption)
    serve(4)
    for k, tower in enumerate((image, caption)):
        swap_descriptor(me, BOX, tower.refs.t_met, swap_sem.at[0, k], swap_sem.at[1, k]).wait()
    queue += [(Route.query_grads, key) for stage in range(3) for key in spread.keys(stage)]
    grads = jnp.concatenate([step.local_backward(tower) for tower in (image, caption)], 1)
    r.query_grads[wide_mine, :] = jnp.concatenate([grads[:, :half], grads[:, half:]], 0).astype(BF16)
    spread.start(Route.query_grads)
    for k, tower in enumerate((image, caption), 2):
        out, met = tower.refs.factor_out, tower.refs.s_met
        swap_out(me, BOX, lambda d, out=out: out.at[d], met, swap_sem.at[0, k], swap_sem.at[1, k])
    step.own_second(caption)
    serve(3)
    squares = r.squares
    r.squares_met[me] = squares[...]
    swap_out(me, BOX, lambda d: squares, r.squares_met, swap_sem.at[0, 4], swap_sem.at[1, 4])
    step.turn_head(caption)
    step.head_gradients(caption)
    serve(8)
    step.head_gradients(image)
    serve(4)
    spread.wait(Route.queries)
    spread.finish(Route.vectors)
    for tower in (image, caption):
        refs = tower.refs
        step.input_gradient(tower)
        step.regroup(tower, refs.t_met)
        step.output_gradient(tower)
        refs.normed_terms[...] = step.group_terms(tower, tower.heads)
        step.factor_gradient(tower, refs.h_grad, 2)
        step.unpack_rows(tower, r.queries, refs.h_queries, 0.125)
    for k, tower in enumerate((image, caption), 2):
        swap_descriptor(me, BOX, tower.refs.s_met, swap_sem.at[0, k], swap_sem.at[1, k]).wait()
    for tower in (image, caption):
        step.regroup(tower, tower.refs.s_met)
        step.factor_gradient(tower, tower.refs.h_queries, 1)
    spread.wait(Route.query_grads)
    for tower in (image, caption):
        step.query_gradient(tower)
    swap_descriptor(me, BOX, r.squares_met, swap_sem.at[0, 4], swap_sem.at[1, 4]).wait()
    totals = jnp.sum(r.squares_met[...], 0)
    slot = iota((8, 128), 0)
    cells = jnp.where(
        slot < 3,
        1.0 / (BOX * image.tokens * image.width),
        1.0 / (BOX * caption.tokens * caption.width),
    )
    means = jnp.sqrt(jnp.sum(totals, 1, keepdims=True) * cells)
    diagonal = jnp.where(slot == iota((8, 128), 1), means, 0.0)
    r.out_rms[...] = column_sum(diagonal)[0, :6]
    for number in range(1, len(items)):
        spread.finish(number)


def tower_scratch(tower, embed):
    width, hidden, rows, batch = tower.width, tower.hidden, tower.rows, tower.batch
    return dict(
        vectors=((8, width), F32),
        attend_vector=((8, 2 * width), F32),
        expand_vector=((8, hidden), F32),
        mixed_bias=((8, 3 * width), F32),
        sums=((8, width), F32),
        value_sums=((8, width), F32),
        norm_sums=((8, width), F32),
        bias_sums=((8, 2 * width), F32),
        expand_sums=((8, hidden), F32),
        x=((rows, width), F32),
        normed=((rows, width), BF16),
        mixed=((rows, 3 * width), BF16),
        att=((rows, width), F32),
        attlow=((rows, width), BF16),
        mask=((len(tower.windows), tower.window, tower.window), F32),
        soft=((rows, tower.terms), F32),
        qe=((tower.terms, width), BF16),
        factor_out=((BOX, tower.mine, 128), BF16),
        t_met=((BOX, tower.mine, 128), BF16),
        s_met=((BOX, tower.mine, 128), BF16),
        normed_terms=((tower.mine, batch), BF16),
        turned_final=((tower.mine, batch), BF16),
        turned_normed=((tower.mine, batch), BF16),
        turned_active=((hidden // BOX, batch), BF16),
        h_normed=((batch, width), BF16),
        h_hidden=((batch, hidden), F32),
        h_active=((batch, hidden), BF16),
        h_hidden_low=((batch, hidden), BF16),
        h_inverse=((batch, 1), F32),
        h_final=((batch, width), BF16),
        h_scaling=((batch, 1), F32),
        h_vectors=((batch, embed), BF16),
        h_raw=((batch, embed), BF16),
        h_grad=((batch, width), F32),
        h_middle_grad=((batch, width), F32),
    )


def step_on_box(images, captions, caption_ends, image_shards, caption_shards, logit_scale):
    image_in, caption_in = SimpleNamespace(**image_shards), SimpleNamespace(**caption_shards)
    image = Tower(True, *images.shape, image_in.expand.shape[1], images.shape[0])
    caption = Tower(False, *captions.shape, caption_in.expand.shape[1], 2 * captions.shape[0])
    both = image.width + caption.width
    count = Route.query_grads + 1
    shared = dict(
        vpack=((24, 128), F32),
        vall=((BOX * 24, 128), F32),
        middles=((BOX * 8, both), F32),
        queries=((BOX * 16, both // 2), BF16),
        query_grads=((BOX * 16, both // 2), BF16),
        squares=((8, 128), F32),
        squares_met=((BOX, 8, 128), F32),
        active=((image.rows, image.hidden), BF16),
        row_low=((image.batch, image.batch), BF16),
        column_low=((image.batch, image.batch), BF16),
        score_low=((image.rows, image.terms), BF16),
        soft_low=((image.rows, image.terms), BF16),
        wide_grad=((image.terms, image.width), BF16),
        placement=((image.rows, image.picks), F32),
        sib_attend=(image_in.attend.shape, BF16),
        sib_output=(image_in.output.shape, BF16),
        sib_projection=(image_in.projection.shape, BF16),
        sib_expand=(image_in.expand.shape, BF16),
    )
    semaphores = dict(near_sem=(count, 16), core_sem=(count,), send_sem=(count,), pair_sem=(2, 4), swap_sem=(2, 5))
    towers, shards = (image, caption), (image_shards, caption_shards)
    local = [tower_scratch(tower, image_in.projection.shape[1]) for tower in towers]

    def kernel(*refs):
        refs = iter(refs)

        def take(names):
            return SimpleNamespace(**{name: next(refs) for name in names})

        tokens = [next(refs), next(refs)]
        for tower in towers:
            tower.shards = take(NAMES)
        ends, logit_ref, out_loss, out_rms = [next(refs) for _ in range(4)]
        out_tokens = [next(refs), next(refs)]
        for tower in towers:
            tower.outs = take(NAMES)
        out_scale = next(refs)
        r = take(shared)
        for k, tower in enumerate(towers):
            tower.weights = take(MATRICES)
            tower.refs = take(local[k])
            tower.refs.tokens, tower.refs.out_tokens = tokens[k], out_tokens[k]
        for name in semaphores:
            setattr(r, name, next(refs))
        r.ends, r.logit_scale = ends, logit_ref
        r.out_loss, r.out_rms, r.out_scale = out_loss, out_rms, out_scale
        step_kernel(image, caption, r)

    scratch = [pltpu.VMEM(*spec) for spec in shared.values()]
    for own, specs in zip(shards, local):
        scratch += [pltpu.VMEM((BOX * own[name].shape[0], own[name].shape[1]), BF16) for name in MATRICES]
        scratch += [pltpu.VMEM(*spec) for spec in specs.values()]
    scratch += [pltpu.SemaphoreType.DMA(shape) for shape in semaphores.values()]
    weights = [own[name] for own in shards for name in NAMES]
    tokens = [jnp.swapaxes(images, 0, 1), jnp.swapaxes(captions, 0, 1)]
    outputs = [((1,), F32), ((6,), F32)] + [(array.shape, BF16) for array in tokens]
    outputs += [(array.shape, F32) for array in weights] + [((1,), F32)]
    vmem, smem = pl.BlockSpec(memory_space=pltpu.VMEM), pl.BlockSpec(memory_space=pltpu.SMEM)
    shapes = [jax.ShapeDtypeStruct(*spec) for spec in outputs]
    results = pl.pallas_call(
        kernel,
        out_shape=shapes,
        in_specs=[vmem] * (2 + len(weights)) + [smem] * 2,
        out_specs=[vmem] * len(outputs),
        scratch_shapes=scratch,
        compiler_params=pltpu.CompilerParams(
            collective_id=0, has_side_effects=True, vmem_limit_bytes=VMEM_LIMIT
        ),
        name="contrastive_step",
    )(*tokens, *weights, caption_ends.T, logit_scale)

    def hand_over(*refs):
        sems = refs[-1]
        pairs = zip(refs[: len(shapes)], refs[len(shapes) : -1])
        copies = [pltpu.make_async_copy(*pair, sems.at[k]) for k, pair in enumerate(pairs)]
        for copy in copies:
            copy.start()
        for copy in copies:
            copy.wait()

    anywhere = pl.BlockSpec(memory_space=pl.ANY)
    results = pl.pallas_call(
        hand_over,
        out_shape=shapes,
        in_specs=[anywhere] * len(shapes),
        out_specs=[vmem] * len(shapes),
        scratch_shapes=[pltpu.SemaphoreType.DMA((len(shapes),))],
        compiler_params=pltpu.CompilerParams(vmem_limit_bytes=VMEM_LIMIT),
        name="hand_over",
    )(*results)
    tokens = [jnp.swapaxes(rows, 0, 1) for rows in results[2:4]]
    return (*results[:2], *tokens, *results[4:])


def solution(mesh):
    rows, matrix, cube = P("dp"), P("dp", None), P("dp", None, None)
    weights = tuple(rows if name in VECTORS else matrix for name in NAMES)
    return jax.shard_map(
        per_device,
        mesh=mesh,
        in_specs=(cube, cube, matrix) + weights + weights + (P(),),
        out_specs=(P(), P(), cube, cube) + weights + weights + (P(),),
        check_vma=False,
    )
```
